32 devices in a mesh: group: 4 (over x, core), dp: 8 (over z, y).
Axes of the slice: x: 2, y: 2, z: 4, core: 2. Of those that a mesh axis runs over, the one named last changes fastest.
Arguments:
- images: float32 [64, 576, 768], P(('group', 'dp')), may hold values from -6 to 6
- cotangent: float32 [64, 576, 768], P(('group', 'dp')), may hold values from -6 to 6
- resolution: int32 [64], P(('group', 'dp')), may hold values from 0 to 2, as said below
- assignment: int32 [64], P(('group', 'dp')), may hold values from 0 to 3, as said below
- counts: int32 [4], replicated, may hold values from 1000 to 63999
- ln1_gain: float32 [768], P('dp'), may hold values from 0.25 to 1.75
- ln1_shift: float32 [768], P('dp'), may hold values from -3 to 3
- qkv_weight: float32 [768, 2304], P('dp'), may hold values from -0.21875 to 0.21875
- qkv_bias: float32 [2304], P('dp'), may hold values from -3 to 3
- rope_freqs: float32 [768], P('dp'), may hold values from -3 to 3
- out_weight: float32 [768, 768], P('dp'), may hold values from -1.75 to 1.75
- out_bias: float32 [768], P('dp'), may hold values from -3 to 3
- ln2_gain: float32 [768], P('dp'), may hold values from 0.25 to 1.75
- ln2_shift: float32 [768], P('dp'), may hold values from -3 to 3
- up_weight: float32 [768, 3072], P('dp'), may hold values from -0.21875 to 0.21875
- up_bias: float32 [3072], P('dp'), may hold values from -3 to 3
- down_weight: float32 [3072, 768], P('dp'), may hold values from -0.109375 to 0.109375
- down_bias: float32 [768], P('dp'), may hold values from -3 to 3
Outputs:
- activations: float32 [64, 576, 768], P(('group', 'dp'))
- input_grad: float32 [64, 576, 768], P(('group', 'dp'))
- grad_ln1_gain: float32 [768], P('dp')
- grad_ln1_shift: float32 [768], P('dp')
- grad_qkv_weight: float32 [768, 2304], P('dp')
- grad_qkv_bias: float32 [2304], P('dp')
- grad_rope_freqs: float32 [768], P('dp')
- grad_out_weight: float32 [768, 768], P('dp')
- grad_out_bias: float32 [768], P('dp')
- grad_ln2_gain: float32 [768], P('dp')
- grad_ln2_shift: float32 [768], P('dp')
- grad_up_weight: float32 [768, 3072], P('dp')
- grad_up_bias: float32 [3072], P('dp')
- grad_down_weight: float32 [3072, 768], P('dp')
- grad_down_bias: float32 [768], P('dp')
The draws below stay inside these ranges and needn't reach their ends.
Inputs may be any that keep to these rules, and one draw needn't show every extreme that they name: resolution index 0, 1, 2 means 14, 20, 24 patches a side; the first image of each index of group has resolution equal to its group number mod 3, and the group's other images often do. `assignment`: all images on one index of group carry the same group number, and the 4 indices carry different ones.
All inputs are finite; a program needn't handle non-finite values.
Results may differ from the reference program's by a relative error of at most 0.015.
The reference program's roundings to bfloat16 on the way count: a program that leaves them out, or rounds other values in their place, can miss the bound.
Values may be sent and summed in bfloat16 or wider, within the bound.
A program may use at most 256 MiB of HBM per device.

```python
import math
import jax
import jax.numpy as jnp
from jax import lax

D = 768
FF = 3072
HEADS = 12
HD = 64
SIDE_S = 14
SIDE_M = 20
SIDE_L = 24
SLOT = 576
IMAGES = 64
GROUPS = 4
GROUP_ROWS = 9216


def shared_groups(key):
    order_key = jax.random.fold_in(key, 11)
    order = jax.random.permutation(order_key, GROUPS).astype(jnp.int32)
    per_block = IMAGES // GROUPS
    return jnp.repeat(order, per_block, total_repeat_length=IMAGES).astype(jnp.int32)


def draw_assignment(key, part):
    return shared_groups(key)


def draw_resolution(key, part):
    groups = shared_groups(key)
    base = groups % 3
    per_block = IMAGES // GROUPS
    picker = jax.random.randint(jax.random.fold_in(key, 23), (IMAGES,), 0, 10)
    other = jax.random.randint(jax.random.fold_in(key, 29), (IMAGES,), 0, 3)
    first = jnp.arange(IMAGES, dtype=jnp.int32) % per_block == 0
    keep_base = jnp.logical_or(first, picker < 7)
    return jnp.where(keep_base, base, other).astype(jnp.int32)


def plant(drawn, stream_key, low, largest):
    index_at = [jax.random.randint(jax.random.fold_in(stream_key, axis), (), 0, length) for axis, length in enumerate(drawn.shape)]
    widest = drawn.shape.index(max(drawn.shape))
    next_to = index_at[:widest] + [(index_at[widest] + 1) % drawn.shape[widest]] + index_at[widest + 1:]
    return drawn.at[tuple(index_at)].set(low).at[tuple(next_to)].set(largest)


def block_scale(own_key, dims, cuts, least, high):
    def one(dim, blocks):
        steps = jax.random.uniform(jax.random.fold_in(jax.random.fold_in(own_key, 6), dim), (blocks,), jnp.float32, least / len(cuts), high / len(cuts))
        return jnp.repeat(jnp.exp(steps), dims[dim] // blocks).reshape((-1,) + (1,) * (len(dims) - dim - 1))

    factor_of = one(*cuts[0])
    for cut in cuts[1:]:
        factor_of = factor_of * one(*cut)
    return factor_of


def gaussian(stream_key, shape, width, bound, pieces=(), kind=jnp.bfloat16):
    entries = width * jax.random.normal(stream_key, shape, jnp.float32)
    if pieces:
        entries = entries * block_scale(stream_key, shape, pieces, -0.22, 0.18)
    return jnp.clip(entries, -bound, bound).astype(kind)


def setup_inputs(seed: int = 0) -> dict:
    key_list = jax.random.split(jax.random.key(seed), 19)
    images = gaussian(key_list[0], (IMAGES, SLOT, D), 1.0, 6.0, ((0, 32),), jnp.float32)
    cotangent = gaussian(key_list[1], (IMAGES, SLOT, D), 1.0, 6.0, ((0, 32),), jnp.float32)
    resolution = draw_resolution(jax.random.fold_in(key_list[18], 71), 0)
    assignment = draw_assignment(jax.random.fold_in(key_list[18], 71), 0)
    counts = plant(jax.random.randint(key_list[4], (GROUPS,), 1000, 64000), jax.random.fold_in(key_list[4], 1), 1000, 63999).astype(jnp.int32)
    ln1_gain = jnp.clip(1.0 + 0.15 * jax.random.normal(key_list[5], (D,), jnp.float32), 0.25, 1.75)
    ln1_shift = gaussian(key_list[6], (D,), 0.5, 3.0, ((0, 8),), jnp.float32)
    qkv_weight = gaussian(key_list[7], (D, 3 * D), D ** -0.5, 0.21875, ((0, 8),), jnp.float32)
    qkv_bias = gaussian(key_list[8], (3 * D,), 0.5, 3.0, ((0, 8),), jnp.float32)
    rope_freqs = gaussian(key_list[9], (D,), 0.5, 3.0, ((0, 8),), jnp.float32)
    out_weight = gaussian(key_list[10], (D, D), (D // 64) ** -0.5, 1.75, ((0, 8),), jnp.float32)
    out_bias = gaussian(key_list[11], (D,), 0.5, 3.0, ((0, 8),), jnp.float32)
    ln2_gain = jnp.clip(1.0 + 0.15 * jax.random.normal(key_list[12], (D,), jnp.float32), 0.25, 1.75)
    ln2_shift = gaussian(key_list[13], (D,), 0.5, 3.0, ((0, 8),), jnp.float32)
    up_weight = gaussian(key_list[14], (D, FF), D ** -0.5, 0.21875, ((0, 8),), jnp.float32)
    up_bias = gaussian(key_list[15], (FF,), 0.5, 3.0, ((0, 8),), jnp.float32)
    down_weight = gaussian(key_list[16], (FF, D), FF ** -0.5, 0.109375, ((0, 8),), jnp.float32)
    down_bias = gaussian(key_list[17], (D,), 0.5, 3.0, ((0, 8),), jnp.float32)
    return {"images": images, "cotangent": cotangent, "resolution": resolution, "assignment": assignment, "counts": counts, "ln1_gain": ln1_gain, "ln1_shift": ln1_shift, "qkv_weight": qkv_weight, "qkv_bias": qkv_bias, "rope_freqs": rope_freqs, "out_weight": out_weight, "out_bias": out_bias, "ln2_gain": ln2_gain, "ln2_shift": ln2_shift, "up_weight": up_weight, "up_bias": up_bias, "down_weight": down_weight, "down_bias": down_bias}


@jax.custom_vjp
def low(v):
    return lax.optimization_barrier(v.astype(jnp.bfloat16)).astype(jnp.float32)

@jax.custom_vjp
def low_back(v):
    return v

def low_keep(v):
    return (low(v), None)

def low_pass(kept, grad):
    return (grad,)

def back_keep(v):
    return (v, None)

def back_low(kept, grad):
    return (low(grad),)
low.defvjp(low_keep, low_pass)
low_back.defvjp(back_keep, back_low)
LN_EPS = 1e-06
MASK_FILL = -1e+30
HIGHEST = lax.Precision.HIGHEST

def layer_norm(values, gain, shift):
    average = lax.optimization_barrier(jnp.mean(values, axis=-1, keepdims=True))
    centred = values - average
    variance = lax.optimization_barrier(jnp.mean(centred * centred, axis=-1, keepdims=True))
    return centred * lax.rsqrt(variance + LN_EPS) * gain + shift

def patch_grid(res_index):
    side_len = jnp.where(res_index == 0, SIDE_S, jnp.where(res_index == 1, SIDE_M, SIDE_L)).astype(jnp.int32)
    positions = jnp.arange(SLOT, dtype=jnp.int32)
    column = (positions % side_len).astype(jnp.float32)
    row_pos = (positions // side_len).astype(jnp.float32)
    return (column, row_pos, positions < side_len * side_len)

def rotate(values, cosine, sine):
    half_dim = values.shape[-1] // 2
    lower_half = values[..., :half_dim]
    upper_half = values[..., half_dim:]
    return jnp.concatenate([lower_half * cosine - upper_half * sine, lower_half * sine + upper_half * cosine], axis=-1)

def gelu_exact(values):
    return jax.nn.gelu(values, approximate=False)

def layer(image, params, res_index):
    copies = [low(tensor) for tensor in params]
    gain_one, shift_one, weight_qkv, bias_qkv, freq_flat, weight_out, bias_out, gain_two, shift_two, weight_up, bias_up, weight_down, bias_down = copies
    column, row_pos, valid = patch_grid(res_index)
    normed_one = low(layer_norm(image, gain_one, shift_one))
    projected = low_back(jnp.dot(normed_one, weight_qkv, precision=HIGHEST) + bias_qkv)
    query_raw = projected[:, :D].reshape(SLOT, HEADS, HD)
    key_raw = projected[:, D:2 * D].reshape(SLOT, HEADS, HD)
    value_raw = projected[:, 2 * D:].reshape(SLOT, HEADS, HD)
    freq_table = freq_flat.reshape(2, HEADS, HD // 2)
    angle = column[:, None, None] * freq_table[0] + row_pos[:, None, None] * freq_table[1]
    cosine = jnp.cos(angle)
    sine = jnp.sin(angle)
    query_rows = low(rotate(query_raw, cosine, sine))
    key_rows = low(rotate(key_raw, cosine, sine))
    value_rows = low(value_raw)
    scores = jnp.einsum('shd,thd->hst', query_rows, key_rows, precision=HIGHEST) * (1.0 / math.sqrt(HD))
    scores = low_back(scores)
    masked = jnp.where(valid[None, None, :], scores, MASK_FILL)
    probs_low = low(jax.nn.softmax(masked, axis=-1))
    context = jnp.einsum('hst,thd->shd', probs_low, value_rows, precision=HIGHEST).reshape(SLOT, D)
    context = low(low_back(context))
    attended = low_back(jnp.dot(context, weight_out, precision=HIGHEST) + bias_out)
    middle = image + attended
    normed_two = low(layer_norm(middle, gain_two, shift_two))
    hidden_pre = low_back(jnp.dot(normed_two, weight_up, precision=HIGHEST) + bias_up)
    hidden = low(gelu_exact(hidden_pre))
    branch = low_back(jnp.dot(hidden, weight_down, precision=HIGHEST) + bias_down)
    return jnp.where(valid[:, None], middle + branch, 0.0)

def reference(images, cotangent, resolution, assignment, counts, ln1_gain, ln1_shift, qkv_weight, qkv_bias, rope_freqs, out_weight, out_bias, ln2_gain, ln2_shift, up_weight, up_bias, down_weight, down_bias):
    params = (ln1_gain, ln1_shift, qkv_weight, qkv_bias, rope_freqs, out_weight, out_bias, ln2_gain, ln2_shift, up_weight, up_bias, down_weight, down_bias)
    counts_float = counts.astype(jnp.float32)
    picked = jnp.take(counts_float, assignment)
    image_weight = GROUPS * picked / jnp.sum(counts_float) / math.sqrt(GROUP_ROWS)

    def one_image(running, inputs_one):
        image, grad_out, res_index, weight_img = inputs_one
        result, pull_back = jax.vjp(lambda values, weights: layer(values, weights, res_index), image, params)
        image_grad, weight_grads = pull_back(grad_out)
        running = tuple((summed + weight_img * piece_grad for summed, piece_grad in zip(running, weight_grads)))
        return (running, (result, image_grad))
    zeros_init = tuple((jnp.zeros(tensor.shape, jnp.float32) for tensor in params))
    grads, (outputs, input_grads) = lax.scan(one_image, zeros_init, (images, cotangent, resolution, image_weight))
    return (outputs, input_grads, grads[0], grads[1], grads[2], grads[3], grads[4], grads[5], grads[6], grads[7], grads[8], grads[9], grads[10], grads[11], grads[12])
```

```python
import functools
import math

import jax
import jax.numpy as jnp
from jax import lax
from jax.experimental import pallas as pl
from jax.experimental.pallas import tpu as pltpu
from jax.sharding import PartitionSpec as P

HEADS = 12
HD = 64
SIDE_S = 14
SIDE_M = 20
SIDE_L = 24
SLOT = 576
D = 768
FF = 3072
LN_EPS = 1e-06
MASK_FILL = -1e30
BF = jnp.bfloat16
F32 = jnp.float32
NT = (((1,), (1,)), ((), ()))
NN = (((1,), (0,)), ((), ()))
TN = (((0,), (0,)), ((), ()))
R_G1, R_S1, R_QB, R_FR, R_OB, R_G2, R_S2, R_UB, R_DB, R_ALL = 0, 1, 2, 5, 6, 7, 8, 9, 13, 16
LOG2E = math.log2(math.e)


def dot(a, b, dims, precision=None):
    return lax.dot_general(a, b, dims, preferred_element_type=F32, precision=precision)


def vm(n):
    return [pl.BlockSpec(memory_space=pltpu.VMEM)] * n


def norm_stats(x):
    mean = jnp.mean(x, axis=-1, keepdims=True)
    cen = x - mean
    var = jnp.mean(cen * cen, axis=-1, keepdims=True)
    inv = lax.rsqrt(var + LN_EPS)
    return cen * inv, inv


def sincos(x):
    n = jnp.floor(x * (2.0 / math.pi) + 0.5)
    r = x - n * 1.5703125
    r = r - n * 4.837512969970703125e-4
    r = r - n * 7.54978995489188216e-8
    q = n.astype(jnp.int32)
    r2 = r * r
    s = r + r * r2 * (-1.6666654611e-1 + r2 * (8.3321608736e-3 + r2 * -1.9515295891e-4))
    c = 1.0 - 0.5 * r2 + r2 * r2 * (
        4.166664568298827e-2 + r2 * (-1.388731625493765e-3 + r2 * 2.443315711809948e-5)
    )
    odd = (q & 1) == 1
    ss = jnp.where(odd, c, s)
    cc = jnp.where(odd, s, c)
    ss = jnp.where((q & 2) == 2, -ss, ss)
    cc = jnp.where(((q + 1) & 2) == 2, -cc, cc)
    return ss, cc


def gelu_pair(x):
    z = jnp.abs(x) * math.sqrt(0.5)
    t = 1.0 / (1.0 + 0.5 * z)
    poly = 0.17087277
    for c in (
        -0.82215223,
        1.48851587,
        -1.13520398,
        0.27886807,
        -0.18628806,
        0.09678418,
        0.37409196,
        1.00002368,
        -1.26551223,
    ):
        poly = poly * t + c
    zz = z * z
    half = 0.5 * t * jnp.exp2((poly - zz) * LOG2E)
    cdf = jnp.where(x < 0, half, 1.0 - half)
    dens = math.sqrt(0.5 / math.pi) * jnp.exp2(zz * -LOG2E)
    return x * cdf, cdf + x * dens


def swap_halves(x):
    width = x.shape[-1]
    lane = lax.broadcasted_iota(jnp.int32, (1, width), 1)
    ahead = pltpu.roll(x, width - HD // 2, 1)
    behind = pltpu.roll(x, HD // 2, 1)
    return jnp.where(lane % HD < HD // 2, ahead, behind)


def half_sign(width):
    lane = lax.broadcasted_iota(jnp.int32, (1, width), 1)
    return jnp.where(lane % HD < HD // 2, 1.0, -1.0).astype(F32)


def patch_columns(side_ref, image):
    side = side_ref[image].astype(F32)
    slot = lax.broadcasted_iota(jnp.int32, (SLOT, 128), 0).astype(F32)
    row = jnp.floor((slot + 0.5) / side)
    col = slot - row * side
    valid = slot < side * side
    return col, row, valid


def spread(which):
    src = lax.broadcasted_iota(jnp.int32, (D, D), 0)
    lane = lax.broadcasted_iota(jnp.int32, (D, D), 1)
    want = which * (D // 2) + (lane // HD) * (HD // 2) + lane % (HD // 2)
    return (src == want).astype(BF)


def qkv_kernel(images, side_ref, x_ref, small_ref, w_ref, qkv_ref, norm_ref, cos_ref, sin_ref):
    gain = small_ref[R_G1 : R_G1 + 1]
    shift = small_ref[R_S1 : R_S1 + 1]
    freq = jnp.broadcast_to(small_ref[R_FR : R_FR + 1], (8, D)).astype(BF)
    fcol = dot(freq, spread(0), NN)[0:1]
    frow = dot(freq, spread(1), NN)[0:1]
    for i in range(images):
        rows = pl.ds(i * SLOT, SLOT)
        unit, _ = norm_stats(x_ref[rows])
        norm_ref[rows] = (unit * gain + shift).astype(BF)
        col, row, _ = patch_columns(side_ref, i)
        for j in range(D // 128):
            lanes = pl.ds(j * 128, 128)
            sn, cs = sincos(col * fcol[:, j * 128 : (j + 1) * 128] + row * frow[:, j * 128 : (j + 1) * 128])
            cos_ref[rows, lanes] = cs
            sin_ref[rows, lanes] = sn * -half_sign(128)

    def block(step, _):
        i, j = step // 9, step % 9
        rows = pl.ds(pl.multiple_of(i * SLOT, SLOT), SLOT)
        lanes = pl.ds(pl.multiple_of(j * 256, 256), 256)
        inner = pl.ds(pl.multiple_of((j % 3) * 256, 256), 256)
        raw = dot(norm_ref[rows], w_ref[:, lanes], NN) + small_ref[pl.ds(R_QB + j // 3, 1), inner]

        @pl.when(j < 6)
        def _():
            turned = raw * cos_ref[rows, inner] + swap_halves(raw) * sin_ref[rows, inner]
            qkv_ref[rows, lanes] = turned.astype(BF)

        @pl.when(j >= 6)
        def _():
            qkv_ref[rows, lanes] = raw.astype(BF)

        return 0

    lax.fori_loop(0, images * 9, block, 0)


def mask_column(side_ref, image):
    side = side_ref[image]
    slot = lax.broadcasted_iota(jnp.int32, (SLOT, 1), 0)
    return jnp.where(slot < side * side, 0.0, MASK_FILL).astype(F32)


def attend_step(step, side_ref, qkv_ref, ctx_ref, lse_ref):
    i, j = step // (HEADS // 2), step % (HEADS // 2)
    rows = pl.ds(pl.multiple_of(i * SLOT, SLOT), SLOT)
    c = pl.multiple_of(j * 128, 128)
    q = qkv_ref[rows, pl.ds(c, 128)]
    k = qkv_ref[rows, pl.ds(c + D, 128)]
    v = qkv_ref[rows, pl.ds(c + 2 * D, 128)]
    lane = lax.broadcasted_iota(jnp.int32, (1, 128), 1)
    mask = mask_column(side_ref, i)
    outs, logs = [], []
    for h in range(2):
        qm = jnp.where(lane // HD == h, q, jnp.zeros_like(q))
        s = dot(k, qm, NT) * (LOG2E / math.sqrt(HD)) + mask
        top = jnp.max(s, axis=0, keepdims=True)
        e = jnp.exp2(s - top)
        total = jnp.sum(e, axis=0, keepdims=True)
        p = (e * (1.0 / total)).astype(BF)
        outs.append(dot(p, v, TN))
        logs.append(top + jnp.log2(total))
    ctx_ref[rows, pl.ds(c, 128)] = jnp.where(lane < HD, outs[0], outs[1]).astype(BF)
    lse_ref[step] = jnp.concatenate(logs + [jnp.zeros((6, SLOT), F32)], axis=0)


def attend_kernel(images, side_ref, qkv_ref, ctx_ref, lse_ref):
    def body(step, _):
        attend_step(step, side_ref, qkv_ref, ctx_ref, lse_ref)
        return 0

    lax.fori_loop(0, images * HEADS // 2, body, 0)


def mlp_kernel(
    tiles,
    tm,
    wsteps,
    side_ref,
    scale_ref,
    x_ref,
    cot_ref,
    ctx_ref,
    small_ref,
    wo_ref,
    wu_ref,
    wd_ref,
    act_ref,
    gm_ref,
    gctx_ref,
    gd_ref,
    gu_ref,
    go_ref,
    gs_ref,
    hid_ref,
    gp_ref,
    n2_ref,
    bl_ref,
    al_ref,
    ctxall_ref,
):
    step = pl.program_id(0)

    @pl.when(step == 0)
    def _():
        gs_ref[...] = jnp.zeros_like(gs_ref)

    @pl.when(step < tiles)
    def _():
        per_image = SLOT // tm
        side = side_ref[step // per_image]
        slot = lax.broadcasted_iota(jnp.int32, (tm, 1), 0) + (step % per_image) * tm
        valid = slot < side * side
        rows = pl.ds(pl.multiple_of(step * tm, tm), tm)
        ctx = ctx_ref[...]
        ctxall_ref[rows] = ctx
        middle = x_ref[...] + (dot(ctx, wo_ref[...], NN) + small_ref[R_OB : R_OB + 1])
        unit, inv = norm_stats(middle)
        gain = small_ref[R_G2 : R_G2 + 1]
        n2_ref[rows] = (unit * gain + small_ref[R_S2 : R_S2 + 1]).astype(BF)
        gbranch = jnp.where(valid, cot_ref[...], 0.0)
        low = gbranch.astype(BF)
        bl_ref[rows] = low

        def block(j, _):
            lanes = pl.ds(pl.multiple_of(j * 256, 256), 256)
            inner = pl.ds(pl.multiple_of((j % 3) * 256, 256), 256)
            pre = dot(n2_ref[rows], wu_ref[:, lanes], NN) + small_ref[pl.ds(R_UB + j // 3, 1), inner]
            back = dot(bl_ref[rows], wd_ref[lanes], NT)
            value, slope = gelu_pair(pre)
            hid_ref[rows, lanes] = value.astype(BF)
            gpre = (back * slope).astype(BF)
            gp_ref[rows, lanes] = gpre
            gs_ref[pl.ds(R_UB + j // 3, 1), inner] += jnp.sum(gpre.astype(F32), axis=0, keepdims=True)
            return 0

        lax.fori_loop(0, FF // 256, block, 0)
        branch = dot(hid_ref[rows], wd_ref[...], NN) + small_ref[R_DB : R_DB + 1]
        act_ref[...] = jnp.where(valid, middle + branch, 0.0)
        gn = dot(gp_ref[rows], wu_ref[...], NT)
        gs_ref[R_G2 : R_G2 + 1] += jnp.sum(gn * unit, axis=0, keepdims=True)
        gs_ref[R_S2 : R_S2 + 1] += jnp.sum(gn, axis=0, keepdims=True)
        a = gn * gain
        ma = jnp.mean(a, axis=-1, keepdims=True)
        mu = jnp.mean(a * unit, axis=-1, keepdims=True)
        gm = gbranch + inv * (a - ma - unit * mu)
        gm_ref[...] = gm
        al = gm.astype(BF)
        al_ref[rows] = al
        gs_ref[R_OB : R_OB + 1] += jnp.sum(al.astype(F32), axis=0, keepdims=True)
        gs_ref[R_DB : R_DB + 1] += jnp.sum(low.astype(F32), axis=0, keepdims=True)
        gctx_ref[...] = dot(al, wo_ref[...], NT).astype(BF)

    @pl.when(step >= tiles)
    def _():
        scale = scale_ref[0]
        width = FF // wsteps
        lanes = pl.ds(pl.multiple_of((step - tiles) * width, width), width)
        gd_ref[...] = (dot(hid_ref[:, lanes], bl_ref[...], TN) * scale).astype(BF)
        gu_ref[...] = (dot(n2_ref[...], gp_ref[:, lanes], TN) * scale).astype(BF)

        @pl.when(step == tiles)
        def _():
            go_ref[...] = (dot(ctxall_ref[...], al_ref[...], TN) * scale).astype(BF)
            gs_ref[...] = gs_ref[...] * scale


def attend_back_step(step, side_ref, qkv_ref, gctx_ref, lse_ref, cos_ref, sin_ref, gproj_ref, gs_ref, gf_ref):
    i, j = step // (HEADS // 2), step % (HEADS // 2)
    rows = pl.ds(pl.multiple_of(i * SLOT, SLOT), SLOT)
    c = pl.multiple_of(j * 128, 128)
    q = qkv_ref[rows, pl.ds(c, 128)]
    k = qkv_ref[rows, pl.ds(c + D, 128)]
    v = qkv_ref[rows, pl.ds(c + 2 * D, 128)]
    go = gctx_ref[rows, pl.ds(c, 128)]
    lane = lax.broadcasted_iota(jnp.int32, (1, 128), 1)
    mask = mask_column(side_ref, i)
    lse = lse_ref[step]
    dq, dk, dv = [], [], []
    for h in range(2):
        mine = lane // HD == h
        qm = jnp.where(mine, q, jnp.zeros_like(q))
        gom = jnp.where(mine, go, jnp.zeros_like(go))
        s = dot(k, qm, NT) * (LOG2E / math.sqrt(HD)) + mask
        p = jnp.exp2(s - lse[h : h + 1])
        dp = dot(v, gom, NT)
        dv.append(dot(p.astype(BF), go, NN))
        t = p * dp
        ds = (t - p * jnp.sum(t, axis=0, keepdims=True)).astype(BF)
        dk.append(dot(ds, q, NN))
        dq.append(dot(ds, k, TN))
    first = lane < HD
    cs = cos_ref[rows, pl.ds(c, 128)]
    sn = sin_ref[rows, pl.ds(c, 128)]
    angle = None
    for n, (pair, rot) in enumerate(((dq, q), (dk, k))):
        e = jnp.where(first, pair[0], pair[1]) * (1.0 / math.sqrt(HD))
        other = swap_halves(e)
        back = (e * cs - other * sn).astype(BF)
        gproj_ref[rows, pl.ds(c + n * D, 128)] = back
        gs_ref[pl.ds(R_QB + n, 1), pl.ds(c, 128)] += jnp.sum(back.astype(F32), axis=0, keepdims=True)
        term = rot.astype(F32) * other
        angle = term if angle is None else angle + term
    gv = jnp.where(first, dv[0], dv[1]).astype(BF)
    gproj_ref[rows, pl.ds(c + 2 * D, 128)] = gv
    gs_ref[R_QB + 2 : R_QB + 3, pl.ds(c, 128)] += jnp.sum(gv.astype(F32), axis=0, keepdims=True)
    angle = angle * half_sign(128)
    col, row, _ = patch_columns(side_ref, i)
    gf_ref[0:1, pl.ds(c, 128)] += jnp.sum(angle * col, axis=0, keepdims=True)
    gf_ref[1:2, pl.ds(c, 128)] += jnp.sum(angle * row, axis=0, keepdims=True)


def freq_row(gf_ref):
    hi = lax.Precision.HIGHEST
    both = gf_ref[...]
    return (
        dot(both[0:8], spread(0).astype(F32), NT, hi)[0:1] + dot(both[0:8], spread(1).astype(F32), NT, hi)[1:2]
    )


def attend_back_kernel(
    images, side_ref, qkv_ref, gctx_ref, lse_ref, cos_ref, sin_ref, gproj_ref, gs_ref, gf_ref
):
    gs_ref[...] = jnp.zeros_like(gs_ref)
    gf_ref[...] = jnp.zeros_like(gf_ref)

    def body(step, _):
        attend_back_step(step, side_ref, qkv_ref, gctx_ref, lse_ref, cos_ref, sin_ref, gproj_ref, gs_ref, gf_ref)
        return 0

    lax.fori_loop(0, images * HEADS // 2, body, 0)
    gs_ref[R_FR : R_FR + 1] = freq_row(gf_ref)


def qkv_back_kernel(
    images, scale_ref, x_ref, norm_ref, gproj_ref, gm_ref, small_ref, w_ref, gs_in, gw_ref, gin_ref, gs_ref
):
    scale = scale_ref[0]

    def wblock(j, _):
        lanes = pl.ds(pl.multiple_of(j * 256, 256), 256)
        gw_ref[:, lanes] = (dot(norm_ref[...], gproj_ref[:, lanes], TN) * scale).astype(BF)
        return 0

    lax.fori_loop(0, 9, wblock, 0)
    gain = small_ref[R_G1 : R_G1 + 1]
    gs_ref[...] = gs_in[...]
    for i in range(images):
        rows = pl.ds(i * SLOT, SLOT)
        unit, inv = norm_stats(x_ref[rows])
        gn = dot(gproj_ref[rows], w_ref[...], NT)
        gs_ref[R_G1 : R_G1 + 1] += jnp.sum(gn * unit, axis=0, keepdims=True)
        gs_ref[R_S1 : R_S1 + 1] += jnp.sum(gn, axis=0, keepdims=True)
        a = gn * gain
        ma = jnp.mean(a, axis=-1, keepdims=True)
        mu = jnp.mean(a * unit, axis=-1, keepdims=True)
        gin_ref[rows] = gm_ref[rows] + inv * (a - ma - unit * mu)
    gs_ref[...] = gs_ref[...] * scale


def params(mb=56):
    return pltpu.CompilerParams(vmem_limit_bytes=mb << 20)


def place_rows(p, dp, vec):
    n = vec.shape[0]
    whole = jnp.tile(vec, dp)
    owner = jnp.arange(n * dp, dtype=jnp.int32) // n
    return jnp.where(owner == p, whole, 0.0).reshape(-1, D)


def on_device(
    images,
    cotangent,
    resolution,
    assignment,
    counts,
    ln1_gain,
    ln1_shift,
    qkv_weight,
    qkv_bias,
    rope_freqs,
    out_weight,
    out_bias,
    ln2_gain,
    ln2_shift,
    up_weight,
    up_bias,
    down_weight,
    down_bias,
):
    p = lax.axis_index("dp")
    dp = lax.axis_size("dp")
    n = images.shape[0]
    rows = n * SLOT
    x = images.reshape(rows, D)
    cot = cotangent.reshape(rows, D)
    side = jnp.where(resolution == 0, SIDE_S, jnp.where(resolution == 1, SIDE_M, SIDE_L)).astype(jnp.int32)
    group_total = counts.shape[0]
    cf = counts.astype(F32)
    picked = jnp.sum(jnp.where(assignment[0] == jnp.arange(group_total, dtype=jnp.int32), cf, 0.0))
    scale = group_total * picked / jnp.sum(cf) / math.sqrt(dp * n * SLOT)
    scale = scale.reshape(1)
    packed = jnp.concatenate(
        [
            place_rows(p, dp, v.astype(BF).astype(F32))
            for v in (ln1_gain, ln1_shift, qkv_bias, rope_freqs, out_bias, ln2_gain, ln2_shift, up_bias, down_bias)
        ]
        + [jnp.zeros((2, D), F32)],
        axis=0,
    )
    small = lax.psum(packed, "dp")
    wqkv = lax.all_gather(qkv_weight.astype(BF), "dp", axis=0, tiled=True)
    wo = lax.all_gather(out_weight.astype(BF), "dp", axis=0, tiled=True)
    wu = lax.all_gather(up_weight.astype(BF), "dp", axis=0, tiled=True)
    wd = lax.all_gather(down_weight.astype(BF), "dp", axis=0, tiled=True)

    sds = jax.ShapeDtypeStruct
    smem = pl.BlockSpec(memory_space=pltpu.SMEM)
    qkv, norm1, cos, sin = pl.pallas_call(
        functools.partial(qkv_kernel, n),
        out_shape=[sds((rows, 3 * D), BF), sds((rows, D), BF), sds((rows, D), F32), sds((rows, D), F32)],
        in_specs=[smem] + vm(3),
        out_specs=vm(4),
        compiler_params=params(),
        name="project",
    )(side, x, small, wqkv)
    ctx, lse = pl.pallas_call(
        functools.partial(attend_kernel, n),
        out_shape=[sds((rows, D), BF), sds((n * HEADS // 2, 8, SLOT), F32)],
        in_specs=[smem] + vm(1),
        out_specs=vm(2),
        compiler_params=params(),
        name="attend",
    )(side, qkv)

    tm = SLOT // 2
    tiles = rows // tm
    wsteps = 6
    once = dict(pipeline_mode=pl.Buffered(1))
    tile = lambda i: (jnp.minimum(i, tiles - 1), 0)
    full = lambda i: (0, 0)
    act, gm, gctx, gdown, gup, gout, gs_mlp = pl.pallas_call(
        functools.partial(mlp_kernel, tiles, tm, wsteps),
        grid=(tiles + wsteps,),
        out_shape=[
            sds((rows, D), F32),
            sds((rows, D), F32),
            sds((rows, D), BF),
            sds((FF, D), BF),
            sds((D, FF), BF),
            sds((D, D), BF),
            sds((R_ALL, D), F32),
        ],
        in_specs=[
            smem,
            smem,
            pl.BlockSpec((tm, D), tile),
            pl.BlockSpec((tm, D), tile),
            pl.BlockSpec((tm, D), tile),
            pl.BlockSpec((R_ALL, D), full, **once),
            pl.BlockSpec((D, D), full, **once),
            pl.BlockSpec((D, FF), full, **once),
            pl.BlockSpec((FF, D), full, **once),
        ],
        out_specs=[
            pl.BlockSpec((tm, D), tile),
            pl.BlockSpec((tm, D), tile),
            pl.BlockSpec((tm, D), tile),
            pl.BlockSpec((FF // wsteps, D), lambda i: (jnp.maximum(i - tiles, 0), 0)),
            pl.BlockSpec((D, FF // wsteps), lambda i: (0, jnp.maximum(i - tiles, 0))),
            pl.BlockSpec((D, D), full),
            pl.BlockSpec((R_ALL, D), full),
        ],
        scratch_shapes=[
            pltpu.VMEM((rows, FF), BF),
            pltpu.VMEM((rows, FF), BF),
            pltpu.VMEM((rows, D), BF),
            pltpu.VMEM((rows, D), BF),
            pltpu.VMEM((rows, D), BF),
            pltpu.VMEM((rows, D), BF),
        ],
        compiler_params=params(62),
        name="mlp",
    )(side, scale, x, cot, ctx, small, wo, wu, wd)

    gproj, gs_att = pl.pallas_call(
        functools.partial(attend_back_kernel, n),
        out_shape=[sds((rows, 3 * D), BF), sds((R_ALL, D), F32)],
        in_specs=[smem] + vm(5),
        out_specs=vm(2),
        scratch_shapes=[pltpu.VMEM((8, D), F32)],
        compiler_params=params(),
        name="attend_back",
    )(side, qkv, gctx, lse, cos, sin)
    gqkv, gin, gs_qkv = pl.pallas_call(
        functools.partial(qkv_back_kernel, n),
        out_shape=[sds((D, 3 * D), BF), sds((rows, D), F32), sds((R_ALL, D), F32)],
        in_specs=[smem] + vm(7),
        out_specs=vm(3),
        compiler_params=params(),
        name="project_back",
    )(scale, x, norm1, gproj, gm, small, wqkv, gs_att)

    def reduce(g):
        part = lax.psum_scatter(g, "dp", scatter_dimension=0, tiled=True)
        return lax.psum(part, "group").astype(F32)

    gs = lax.psum(gs_mlp + gs_qkv, ("group", "dp"))

    def own(first, count):
        flat = gs[first : first + count].reshape(dp, -1)
        return lax.dynamic_index_in_dim(flat, p, 0, keepdims=False)

    return (
        act.reshape(images.shape),
        gin.reshape(images.shape),
        own(R_G1, 1),
        own(R_S1, 1),
        reduce(gqkv),
        own(R_QB, 3),
        own(R_FR, 1),
        reduce(gout),
        own(R_OB, 1),
        own(R_G2, 1),
        own(R_S2, 1),
        reduce(gup),
        own(R_UB, 4),
        reduce(gdown),
        own(R_DB, 1),
    )


def solution(mesh):
    batch = P(("group", "dp"), None, None)
    per_image = P(("group", "dp"))
    vec, mat = P("dp"), P("dp", None)
    return jax.shard_map(
        on_device,
        mesh=mesh,
        in_specs=(batch, batch, per_image, per_image, P(), vec, vec, mat, vec, vec, mat, vec, vec, vec, mat, vec, mat, vec),
        out_specs=(batch, batch, vec, vec, mat, vec, vec, mat, vec, vec, vec, mat, vec, mat, vec),
        check_vma=False,
    )
```

```python
import functools
import math

import jax
import jax.numpy as jnp
from jax import lax
from jax.experimental import pallas as pl
from jax.experimental.pallas import tpu as pltpu
from jax.sharding import PartitionSpec as P

HEADS = 12
HD = 64
SIDE_S = 14
SIDE_M = 20
SIDE_L = 24
SLOT = 576
D = 768
FF = 3072
LN_EPS = 1e-06
MASK_FILL = -1e30
BF = jnp.bfloat16
F32 = jnp.float32
NT = (((1,), (1,)), ((), ()))
NN = (((1,), (0,)), ((), ()))
TN = (((0,), (0,)), ((), ()))
R_G1, R_S1, R_QB, R_FR, R_OB, R_G2, R_S2, R_UB, R_DB, R_ALL = 0, 1, 2, 5, 6, 7, 8, 9, 13, 16
THIRD = 256
LOG2E = math.log2(math.e)


def dot(a, b, dims, precision=None):
    return lax.dot_general(a, b, dims, preferred_element_type=F32, precision=precision)


def vm(n):
    return [pl.BlockSpec(memory_space=pltpu.VMEM)] * n


def norm_stats(x):
    mean = jnp.mean(x, axis=-1, keepdims=True)
    cen = x - mean
    var = jnp.mean(cen * cen, axis=-1, keepdims=True)
    inv = lax.rsqrt(var + LN_EPS)
    return cen * inv, inv


def sincos(x):
    n = jnp.floor(x * (2.0 / math.pi) + 0.5)
    r = x - n * 1.5703125
    r = r - n * 4.837512969970703125e-4
    r = r - n * 7.54978995489188216e-8
    q = n.astype(jnp.int32)
    r2 = r * r
    s = r + r * r2 * (-1.6666654611e-1 + r2 * (8.3321608736e-3 + r2 * -1.9515295891e-4))
    c = 1.0 - 0.5 * r2 + r2 * r2 * (
        4.166664568298827e-2 + r2 * (-1.388731625493765e-3 + r2 * 2.443315711809948e-5)
    )
    odd = (q & 1) == 1
    ss = jnp.where(odd, c, s)
    cc = jnp.where(odd, s, c)
    ss = jnp.where((q & 2) == 2, -ss, ss)
    cc = jnp.where(((q + 1) & 2) == 2, -cc, cc)
    return ss, cc


ERFC = (
    0.07314588129520416,
    -0.30809587240219116,
    0.3798876702785492,
    -0.08230462670326233,
    0.245080828666687,
    0.2054724544286728,
    0.24429383873939514,
    0.242519810795784,
)


def gelu_pair(x):
    z = jnp.abs(x)
    t = 1.0 / (1.0 + (0.43 * math.sqrt(0.5)) * z)
    poly = 0.5 * ERFC[0]
    for c in ERFC[1:]:
        poly = poly * t + 0.5 * c
    bell = jnp.exp2((x * x) * (-0.5 * LOG2E))
    half = poly * t * bell
    cdf = jnp.where(x < 0, half, 1.0 - half)
    return x * cdf, cdf + (x * math.sqrt(0.5 / math.pi)) * bell


def swap_halves(x):
    width = x.shape[-1]
    lane = lax.broadcasted_iota(jnp.int32, (1, width), 1)
    ahead = pltpu.roll(x, width - HD // 2, 1)
    behind = pltpu.roll(x, HD // 2, 1)
    return jnp.where(lane % HD < HD // 2, ahead, behind)


def half_sign(width):
    lane = lax.broadcasted_iota(jnp.int32, (1, width), 1)
    return jnp.where(lane % HD < HD // 2, 1.0, -1.0).astype(F32)


def patch_columns(side_ref, image):
    side = side_ref[image].astype(F32)
    slot = lax.broadcasted_iota(jnp.int32, (SLOT, 128), 0).astype(F32)
    row = jnp.floor((slot + 0.5) / side)
    col = slot - row * side
    valid = slot < side * side
    return col, row, valid


def spread(which):
    src = lax.broadcasted_iota(jnp.int32, (D, D), 0)
    lane = lax.broadcasted_iota(jnp.int32, (D, D), 1)
    want = which * (D // 2) + (lane // HD) * (HD // 2) + lane % (HD // 2)
    return (src == want).astype(BF)


class Place:
    def __init__(self):
        self.p = lax.axis_index("dp")
        self.g = lax.axis_index("group")
        self.z, self.y = self.p // 2, self.p % 2
        self.x, self.core = self.g // 2, self.g % 2

    def over(self):
        return (self.g, self.p ^ 1)

    def sibling(self):
        return (self.g ^ 1, self.p)

    def across(self):
        return (self.g ^ 2, self.p)

    def line(self):
        return [(self.g, self.p ^ (2 * k)) for k in (1, 2, 3)]

    def partners(self):
        return [self.sibling(), self.across(), self.over()] + self.line()


def remote(src, dst, send, recv, device):
    return pltpu.make_async_remote_copy(
        src_ref=src, dst_ref=dst, send_sem=send, recv_sem=recv, device_id=device, device_id_type=pl.DeviceIdType.MESH
    )


def load(src, dst, sem):
    copy = pltpu.make_async_copy(src, dst, sem)
    copy.start()
    return copy


def greet(devices):
    barrier = pltpu.get_barrier_semaphore()
    for device in devices:
        pl.semaphore_signal(barrier, inc=1, device_id=device, device_id_type=pl.DeviceIdType.MESH)
    pl.semaphore_wait(barrier, len(devices))


def timetable(plan):
    return sorted(((step, name, stage) for name, steps in plan.items() for stage, step in enumerate(steps)), key=lambda r: r[0])


class Moves:
    def __init__(self, items, plan):
        self.items, self.rows = items, timetable(plan)

    def at(self, step):
        for when, name, stage in self.rows:
            if when == step:
                self.items[name].stage(stage)

    def within(self, step, first, last):
        for when in sorted({r[0] for r in self.rows if first <= r[0] <= last}):
            pl.when(step == when)(functools.partial(self.at, when))


class Gather:
    STAGES = 5

    def __init__(self, place, own, full, sems, recv, index):
        self.w, self.own, self.full = place, own, full
        self.rows = full.shape[0] // 8
        self.t = self.rows // 3 if self.rows % 48 == 0 else self.rows * 3 // 8
        self.e = self.rows - 2 * self.t
        self.send, self.sib = sems.at[2 * index], sems.at[2 * index + 1]
        self.recv = recv.at[index]

    def part(self, block, piece, ref=None):
        ref = self.full if ref is None else ref
        first = block * self.rows + piece * self.t
        return ref.at[pl.ds(pl.multiple_of(first, 16), self.e if isinstance(piece, int) else self.t)]

    def push(self, ref, device, index, src=None):
        remote(ref if src is None else src, ref, self.send, self.recv.at[index], device).start()

    def got(self, ref, index):
        remote(ref, ref, self.send, self.recv.at[index], self.w.sibling()).wait_recv()

    def hand(self, ref):
        remote(ref, ref, self.send, self.sib, self.w.sibling()).start()

    def stage(self, number):
        w = self.w
        pl.when(w.core == 0)(lambda: self.step(number, w.x, True))
        pl.when(w.core == 1)(lambda: self.step(number, 2, False))

    def step(self, number, piece, split):
        w = self.w
        if number == 0:
            src = self.part(0, piece, self.own)
            for k in (1, 3, 2):
                self.push(self.part(w.p, piece), (w.g, w.p ^ (2 * k)), w.z, src)
            self.push(self.part(w.p, piece), w.over(), 4 + w.z, src)
        elif number in (1, 2):
            for k in (1, 3, 2) if number == 1 else (0, 1, 3, 2):
                z = w.z ^ k
                block = 2 * z + (w.y if number == 1 else 1 - w.y)
                ref = self.part(block, piece)
                self.got(ref, z if number == 1 else 4 + z)
                if number == 1:
                    self.push(ref, w.over(), 4 + z)
                if split:
                    self.push(ref, w.across(), 8 + block)
                self.hand(ref)
        elif number == 3:
            if split:
                for k in (2, 6, 4, 1, 3, 7, 5):
                    block = w.p ^ k
                    ref = self.part(block, 1 - w.x)
                    self.got(ref, 8 + block)
                    self.hand(ref)
        else:
            for count in (14 * self.t, 14 * self.t) if split else (14 * self.e,):
                done = self.full.at[pl.ds(0, count)]
                remote(done, done, self.send, self.sib, w.sibling()).wait_send()
            came = self.full.at[pl.ds(0, 7 * self.e if split else 14 * self.t)]
            remote(came, came, self.send, self.sib, w.sibling()).wait_recv()


class Reduce:
    STAGES = 7

    def __init__(self, place, src, bufs, out, local, send, recv):
        self.w, self.src, self.out = place, src, out
        self.mine, self.cbuf, self.ybuf, self.zbuf, self.xbuf, self.fbuf = bufs
        self.rows = src.shape[0] // 8
        self.t, self.e = self.split(self.rows)
        self.local, self.send, self.recv = local, send, recv

    @staticmethod
    def split(rows):
        t = rows // 4 if rows % 64 == 0 else rows // 3
        return t, rows - 2 * t

    @classmethod
    def buffers(cls, rows, width):
        t, e = cls.split(rows)
        big = max(2 * t, e)
        sizes = (8 * big, 8 * big, 4 * max(t, e), 4 * max(t, e), 8 * t, max(t, e))
        return [pltpu.VMEM((n, width), BF) for n in sizes]

    def copy(self, src, dst, index, device):
        return remote(src, dst, self.send, self.recv.at[index], device)

    def took(self, ref, index):
        self.copy(ref, ref, index, self.w.sibling()).wait_recv()

    def rows_of(self, ref, first, count):
        return ref.at[pl.ds(pl.multiple_of(first, 16), count)]

    def add(self, target, *terms):
        total = target[...].astype(F32)
        for term in terms:
            total = total + term[...].astype(F32)
        target[...] = total.astype(BF)

    def each_core(self, first, second):
        pl.when(self.w.core == 0)(first)
        pl.when(self.w.core == 1)(second)

    def exchange(self, theirs, their_rows, ours, our_rows):
        for b in range(8):
            self.copy(
                self.rows_of(self.src, b * self.rows + theirs, their_rows),
                self.rows_of(self.cbuf, b * their_rows, their_rows),
                0,
                self.w.sibling(),
            ).start()
            pltpu.make_async_copy(
                self.rows_of(self.src, b * self.rows + ours, our_rows),
                self.rows_of(self.mine, b * our_rows, our_rows),
                self.local,
            ).start()

    def settle(self, count):
        whole = self.mine.at[pl.ds(0, 8 * count)]
        pltpu.make_async_copy(whole, whole, self.local).wait()
        self.took(self.cbuf.at[pl.ds(0, 8 * count)], 0)

        def body(b, _):
            self.add(self.rows_of(self.mine, b * count, count), self.rows_of(self.cbuf, b * count, count))
            return 0

        lax.fori_loop(0, 8, body, 0)

    def zero_at(self, block, piece):
        return self.rows_of(self.mine, block * 2 * self.t + piece * self.t, self.t)

    def one_at(self, block):
        return self.rows_of(self.mine, block * self.e, self.e)

    def send_y(self, count, at):
        w = self.w
        for z in range(4):
            self.copy(at(2 * z + 1 - w.y), self.rows_of(self.ybuf, z * count, count), 2, w.over()).start()

    def take_y(self, count, at):
        self.took(self.ybuf.at[pl.ds(0, 4 * count)], 2)
        for z in range(4):
            self.add(at(2 * z + self.w.y), self.rows_of(self.ybuf, z * count, count))

    def send_z(self, count, at):
        w = self.w
        for k in (3, 1, 2):
            z = w.z ^ k
            self.copy(at(2 * z + w.y), self.rows_of(self.zbuf, k * count, count), 3, (w.g, 2 * z + w.y)).start()

    def take_z(self, count, at):
        self.took(self.zbuf.at[pl.ds(0, 3 * count)], 3)
        self.add(at(self.w.p), *[self.rows_of(self.zbuf, k * count, count) for k in (1, 2, 3)])

    def give(self, first, count, value):
        ref = self.out.at[pl.ds(pl.multiple_of(first, 8), count)]
        ref[...] = value
        remote(ref, ref, self.send, self.recv.at[5], self.w.sibling()).start()

    def stage(self, number):
        w, t, e = self.w, self.t, self.e
        x_mine = functools.partial(self.zero_at, piece=w.x)
        x_other = functools.partial(self.zero_at, piece=1 - w.x)
        if number == 0:
            self.each_core(lambda: self.exchange(2 * t, e, 0, 2 * t), lambda: self.exchange(0, 2 * t, 2 * t, e))
        elif number == 1:

            def first():
                self.settle(2 * t)
                for b in range(8):
                    self.copy(x_other(b), self.rows_of(self.xbuf, b * t, t), 1, w.across()).start()

            def second():
                self.settle(e)
                self.send_y(e, self.one_at)

            self.each_core(first, second)
        elif number == 2:

            def first():
                self.took(self.xbuf, 1)
                for b in range(8):
                    self.add(x_mine(b), self.rows_of(self.xbuf, b * t, t))
                self.send_y(t, x_mine)

            def second():
                self.take_y(e, self.one_at)
                self.send_z(e, self.one_at)

            self.each_core(first, second)
        elif number == 3:

            def first():
                self.take_y(t, x_mine)
                self.send_z(t, x_mine)

            def second():
                self.take_z(e, self.one_at)
                self.copy(self.one_at(w.p), self.fbuf.at[pl.ds(0, e)], 4, w.across()).start()

            self.each_core(first, second)
        elif number == 4:

            def first():
                self.take_z(t, x_mine)
                self.copy(x_mine(w.p), self.fbuf.at[pl.ds(0, t)], 4, w.across()).start()
                self.give(w.x * t, t, x_mine(w.p)[...].astype(F32))

            def second():
                self.took(self.fbuf.at[pl.ds(0, e)], 4)
                self.give(2 * t, e, self.one_at(w.p)[...].astype(F32) + self.fbuf[pl.ds(0, e)].astype(F32))

            self.each_core(first, second)
        elif number == 5:

            @pl.when(w.core == 0)
            def _():
                self.took(self.fbuf.at[pl.ds(0, t)], 4)
                self.give((1 - w.x) * t, t, self.fbuf[pl.ds(0, t)].astype(F32))

        else:

            def sent(count):
                while count > 0:
                    now = min(count, self.mine.shape[0])
                    part = self.mine.at[pl.ds(0, now)]
                    remote(part, part, self.send, self.recv.at[0], w.sibling()).wait_send()
                    count -= now

            def came(first, count):
                ref = self.out.at[pl.ds(first, count)]
                remote(ref, ref, self.send, self.recv.at[5], w.sibling()).wait_recv()

            def first():
                came(2 * t, e)
                sent(8 * e + 8 * t + 4 * t + 3 * t + t + 4 * t)

            def second():
                came(0, 2 * t)
                sent(16 * t + 4 * e + 3 * e + e + 2 * e)

            self.each_core(first, second)


class SmallSum:
    HOPS = (4, 2, 4)

    def __init__(self, place, value, bufs, send, recv):
        self.w, self.value, self.bufs, self.send, self.recv = place, value, bufs, send, recv

    def copies(self, hop):
        w = self.w
        for k in range(1, self.HOPS[hop]):
            device = ((w.g ^ k, w.p), (w.g, w.p ^ k), (w.g, w.p ^ (2 * k)))[hop]
            ref = self.bufs.at[4 * hop]
            yield remote(ref, self.bufs.at[4 * hop + k], self.send.at[hop, k], self.recv.at[hop, k], device)

    def stage(self, number):
        w = self.w
        if number > 0:
            hop = number - 1
            for copy in self.copies(hop):
                copy.wait()
            mine = (w.g, w.y, w.z)[hop]
            total = self.bufs[4 * hop + mine]
            for k in range(1, self.HOPS[hop]):
                total = total + self.bufs[4 * hop + (mine ^ k)]
        else:
            total = self.value[...]
        if number == 3:
            self.value[...] = total
        else:
            self.bufs[4 * number] = total
            for copy in self.copies(number):
                copy.start()


def mask_column(side_ref, image):
    side = side_ref[image]
    slot = lax.broadcasted_iota(jnp.int32, (SLOT, 1), 0)
    return jnp.where(slot < side * side, 0.0, MASK_FILL).astype(F32)


def head_pair(images, step):
    i, j = step % images, step // images
    rows = pl.ds(pl.multiple_of(i * SLOT, SLOT), SLOT)
    return i, rows, pl.multiple_of(j * 128, 128), pl.multiple_of((j // 2) * D + (j % 2) * 128, 128)


def attend_step(images, step, side_ref, qkv_ref, ctx_ref, lse_ref):
    i, rows, c, at = head_pair(images, step)
    q = qkv_ref[rows, pl.ds(at, 128)]
    k = qkv_ref[rows, pl.ds(at + THIRD, 128)]
    v = qkv_ref[rows, pl.ds(at + 2 * THIRD, 128)]
    lane = lax.broadcasted_iota(jnp.int32, (1, 128), 1)
    mask = mask_column(side_ref, i)
    outs, logs = [], []
    for h in range(2):
        qm = jnp.where(lane // HD == h, q, jnp.zeros_like(q))
        s = dot(k, qm, NT) * (LOG2E / math.sqrt(HD)) + mask
        top = jnp.max(s, axis=0, keepdims=True)
        e = jnp.exp2(s - top)
        total = jnp.sum(e, axis=0, keepdims=True)
        p = (e * (1.0 / total)).astype(BF)
        outs.append(dot(p, v, TN))
        logs.append(top + jnp.log2(total))
    ctx_ref[rows, pl.ds(c, 128)] = jnp.where(lane < HD, outs[0], outs[1]).astype(BF)
    lse_ref[step] = jnp.concatenate(logs + [jnp.zeros((6, SLOT), F32)], axis=0)


def norm_rows(images, x_ref, small, norm_ref):
    def body(step, _):
        rows = pl.ds(pl.multiple_of(step * 192, 192), 192)
        unit, _ = norm_stats(x_ref[rows])
        norm_ref[rows] = (unit * small[R_G1 : R_G1 + 1] + small[R_S1 : R_S1 + 1]).astype(BF)
        return 0

    lax.fori_loop(0, images * SLOT // 192, body, 0)


def angle_tables(images, side_ref, small, cos_ref, sin_ref):
    freq = jnp.broadcast_to(small[R_FR : R_FR + 1], (8, D)).astype(BF)
    fcol = dot(freq, spread(0), NN)
    frow = dot(freq, spread(1), NN)
    for j in range(D // 128):
        fc, fr = fcol[0:1, j * 128 : (j + 1) * 128], frow[0:1, j * 128 : (j + 1) * 128]

        def body(i, _):
            rows = pl.ds(pl.multiple_of(i * SLOT, SLOT), SLOT)
            col, row, _ = patch_columns(side_ref, i)
            sn, cs = sincos(col * fc + row * fr)
            cos_ref[rows, pl.ds(j * 128, 128)] = cs
            sin_ref[rows, pl.ds(j * 128, 128)] = sn * -half_sign(128)
            return 0

        lax.fori_loop(0, images, body, 0)


def project_block(images, c, r, small, w_ref, norm_ref, qkv_ref, cos_ref, sin_ref):
    i, part = r % images, r // images
    rows = pl.ds(pl.multiple_of(i * SLOT, SLOT), SLOT)
    cols = pl.ds(pl.multiple_of(part * THIRD, THIRD), THIRD)
    lanes = pl.ds(pl.multiple_of(c * D + part * THIRD, THIRD), THIRD)
    inner = pl.ds(pl.multiple_of(c * THIRD, THIRD), THIRD)
    raw = dot(norm_ref[rows], w_ref[c, :, cols], NN) + small[pl.ds(R_QB + part, 1), inner]

    @pl.when(part < 2)
    def _():
        turned = raw * cos_ref[rows, inner] + swap_halves(raw) * sin_ref[rows, inner]
        qkv_ref[rows, lanes] = turned.astype(BF)

    @pl.when(part == 2)
    def _():
        qkv_ref[rows, lanes] = raw.astype(BF)


def forward_compute(images, side_ref, x_ref, small, w_ref, qkv, norm, cos, sin, ctx_ref, lse_ref, hooks):
    hooks("start")
    norm_rows(images, x_ref, small, norm)
    hooks("tables")
    angle_tables(images, side_ref, small, cos, sin)
    blocks, pairs = 3 * images, 2 * images

    def body(step, _):
        hooks("step", step)
        c, r = step // (blocks + pairs), step % (blocks + pairs)

        @pl.when(r < blocks)
        def _():
            project_block(images, c, r, small, w_ref, norm, qkv, cos, sin)

        @pl.when(r >= blocks)
        def _():
            attend_step(images, c * pairs + r - blocks, side_ref, qkv, ctx_ref, lse_ref)

        return 0

    lax.fori_loop(0, 3 * (blocks + pairs), body, 0)
    hooks("end")


def forward_plain(images, side_ref, x_ref, small_ref, w_ref, *refs):
    qkv, norm, cos, sin, ctx, lse = refs
    forward_compute(images, side_ref, x_ref, small_ref, w_ref, qkv, norm, cos, sin, ctx, lse, lambda *a: None)


def forward_gather(images, side_ref, x_ref, pack_ref, *refs):
    shards = refs[0:4]
    qkv_out, norm_out, cos_out, sin_out, ctx, lse, small, wq_out, wo, wu, wd, up_later, down_later = refs[4:17]
    qkv, norm, cos, sin, wq, slots, bq, bo, bu, bd, sems, recv, psend, precv, local = refs[17:]
    w = Place()
    pairs = [(bq.at[c], wq.at[c]) for c in range(3)] + [(bo, wo)]
    pairs += [(own.at[c], full.at[c]) for c in range(PARTS - 1) for own, full in ((bu, wu), (bd, wd))]
    gathers = dict(zip(("q0", "q1", "q2", "o", "u0", "d0", "u1", "d1"), pairs))
    gathers = {k: Gather(w, *v, sems, recv, i) for i, (k, v) in enumerate(gathers.items())}
    moves = Moves(gathers, FORWARD_PLAN)
    peers = [w.p ^ k for k in range(1, 8)]
    keep = []

    def store(src, dst):
        keep.append(load(src, dst, local.at[len(keep)]))

    def own_rows(full):
        count = full.shape[0] // 8
        return full.at[pl.ds(pl.multiple_of(w.p * count, 16), count)]

    def pack_copy(k):
        return remote(pack_ref, slots.at[k], psend.at[k - 1], precv.at[k - 1], (w.g, peers[k - 1]))

    def hooks(where, step=None):
        if where == "start":
            for c in range(3):
                for part in range(3):
                    cols = part * D + c * THIRD
                    bq[c, :, part * THIRD : (part + 1) * THIRD] = shards[0][:, cols : cols + THIRD].astype(BF)
            greet([(w.g, q) for q in peers] + [w.sibling(), w.across()])
            for k in range(1, 8):
                pack_copy(k).start()
            moves.at(-1)
            bo[...] = shards[1][...].astype(BF)
            for c in range(PARTS):
                for b in range(8):
                    cols = (b * PARTS + c) * 128
                    bu[c, :, b * 128 : (b + 1) * 128] = shards[2][:, cols : cols + 128].astype(BF)
                bd[c] = shards[3][c * 128 : (c + 1) * 128].astype(BF)
            for own, full in pairs:
                store(own, own_rows(full))
            store(bu.at[PARTS - 1], up_later)
            store(bd.at[PARTS - 1], down_later)
            total = pack_ref[...]
            for k in range(1, 8):
                pack_copy(k).wait()
                total = total + slots[k]
            small[...] = total
            moves.at(0)
        elif where == "tables":
            moves.at(1)
            store(norm, norm_out)
        elif where == "step":

            @pl.when(step == 0)
            def _():
                for copy in keep[:3]:
                    copy.wait()

            moves.within(step + 2, 2, 31)
        else:
            for copy in keep[3:]:
                copy.wait()
            keep.clear()
            moves.at(32)
            for src, dst in ((wq, wq_out), (cos, cos_out), (sin, sin_out), (qkv, qkv_out)):
                store(src, dst)
            for copy in keep:
                copy.wait()

    forward_compute(images, side_ref, x_ref, small, wq, qkv, norm, cos, sin, ctx, lse, hooks)


FORWARD_PLAN = {
    "q0": (-1, 1, 2, 2, 2),
    "q1": (0, 2, 9, 11, 12),
    "q2": (1, 4, 10, 16, 19),
    "o": (1, 7, 14, 29, 31),
    "u0": (3, 11, 17, 25, 26),
    "d0": (5, 16, 21, 27, 31),
    "u1": (17, 21, 28, 31, 32),
    "d1": (10, 16, 24, 30, 31),
}


def bias_at(split, step):
    c, k = step // BLOCKS, step % BLOCKS
    if split:
        return (R_UB + k, c * 128), (R_UB + k, D // 2 + c * 128)
    return (R_UB + step // 3, (step % 3) * 256), (R_UB + step // 3, (step % 3) * 256 + 128)


def mlp_compute(images, split, side_ref, scale, cot_ref, ctx_ref, small, wo_ref, wu, wd, refs, outs, hooks):
    mid, n2, n2t, bl, hid, gpre, ubias, gubias = refs
    act, gm, gctx, gdown, gup, gout, gs = outs
    rows_all = images * SLOT
    tile = SLOT // 2
    hooks("start")
    gain = small[R_G2 : R_G2 + 1]
    gs[...] = jnp.zeros_like(gs)
    for step in range(PARTS * BLOCKS):
        for n, (r, l) in enumerate(bias_at(split, step)):
            ubias[step : step + 1, n * 128 : (n + 1) * 128] = small[r : r + 1, l : l + 128]

    def tile_rows(step):
        side = side_ref[step // 2]
        slot = lax.broadcasted_iota(jnp.int32, (tile, 1), 0) + (step % 2) * tile
        return pl.ds(pl.multiple_of(step * tile, tile), tile), slot < side * side

    def enter(step, _):
        rows, valid = tile_rows(step)
        middle = mid[rows] + (dot(ctx_ref[rows], wo_ref[...], NN) + small[R_OB : R_OB + 1])
        mid[rows] = middle
        act[rows] = middle + small[R_DB : R_DB + 1]
        unit, _ = norm_stats(middle)
        n2[rows] = (unit * gain + small[R_S2 : R_S2 + 1]).astype(BF)
        low = jnp.where(valid, cot_ref[rows], 0.0).astype(BF)
        bl[rows] = low
        gs[R_DB : R_DB + 1] += jnp.sum(low.astype(F32), axis=0, keepdims=True)
        return 0

    lax.fori_loop(0, 2 * images, enter, 0)
    gm[...] = jnp.zeros_like(gm)
    n2t[...] = n2[...].T
    hooks("entered")

    def block(step, _):
        hooks("block", step)
        c, k = step // BLOCKS, step % BLOCKS
        cols = pl.ds(pl.multiple_of(k * 256, 256), 256)
        bias = ubias[pl.ds(step, 1), :]
        wuc = wu[c, :, cols]
        wdc = wd[c, cols, :]
        bsum = None
        for i in range(images):
            rows = pl.ds(i * SLOT, SLOT)
            pre = dot(n2[rows], wuc, NN) + bias
            back = dot(bl[rows], wdc, NT)
            value, slope = gelu_pair(pre)
            hid[rows, cols] = value.astype(BF)
            g = (back * slope).astype(BF)
            gpre[rows, cols] = g
            part = jnp.sum(g.astype(F32), axis=0, keepdims=True)
            bsum = part if bsum is None else bsum + part
        gubias[pl.ds(step, 1), :] = bsum
        gdown[c, cols, :] = (dot(hid[:, cols], bl[...], TN) * scale).astype(BF)
        gup[c, :, cols] = (dot(n2t[...], gpre[:, cols], NN) * scale).astype(BF)

        @pl.when(k == BLOCKS - 1)
        def _():
            def tail(n, _):
                rows = pl.ds(pl.multiple_of(n * tile, tile), tile)
                act[rows] += dot(hid[rows], wd[c], NN)
                gm[rows] += dot(gpre[rows], wu[c], NT)
                return 0

            lax.fori_loop(0, 2 * images, tail, 0)

        return 0

    lax.fori_loop(0, PARTS * BLOCKS, block, 0)
    hooks("blocks")

    def leave(step, _):
        rows, valid = tile_rows(step)
        unit, inv = norm_stats(mid[rows])
        act[rows] = jnp.where(valid, act[rows], 0.0)
        gn = gm[rows]
        gs[R_G2 : R_G2 + 1] += jnp.sum(gn * unit, axis=0, keepdims=True)
        gs[R_S2 : R_S2 + 1] += jnp.sum(gn, axis=0, keepdims=True)
        a = gn * gain
        ma = jnp.mean(a, axis=-1, keepdims=True)
        mu = jnp.mean(a * unit, axis=-1, keepdims=True)
        g = jnp.where(valid, cot_ref[rows], 0.0) + inv * (a - ma - unit * mu)
        gm[rows] = g
        low = g.astype(BF)
        bl[rows] = low
        gs[R_OB : R_OB + 1] += jnp.sum(low.astype(F32), axis=0, keepdims=True)
        gctx[rows] = dot(low, wo_ref[...], NT).astype(BF)
        return 0

    lax.fori_loop(0, 2 * images, leave, 0)
    for step in range(PARTS * BLOCKS):
        for n, (r, l) in enumerate(bias_at(split, step)):
            gs[r : r + 1, l : l + 128] = gubias[step : step + 1, n * 128 : (n + 1) * 128]
    gout[...] = (dot(ctx_ref[...], bl[...], TN) * scale).astype(BF)
    gs[...] = gs[...] * scale
    hooks("end")


def mlp_scratch(rows):
    vmem = pltpu.VMEM
    return (
        [vmem((rows, D), F32), vmem((rows, D), BF), vmem((D, rows), BF), vmem((rows, D), BF)]
        + [vmem((rows, FF // PARTS), BF)] * 2
        + [vmem((16, 256), F32)] * 2
    )


def mlp_plain(images, side_ref, scale_ref, x_ref, cot_ref, ctx_ref, small, wo_ref, wu, wd, *rest):
    outs, refs, sem = rest[0:7], rest[7:15], rest[15]
    load(x_ref, refs[0], sem.at[0]).wait()
    mlp_compute(
        images, False, side_ref, scale_ref[0], cot_ref, ctx_ref, small, wo_ref, wu, wd, refs, outs, lambda *a: None
    )


def mlp_moving(images, side_ref, scale_ref, small, *rest):
    x_in, cot_in, ctx_in, wo_in, wu_in, wd_in, up_later, down_later = rest[0:8]
    act_out, gm_out, gctx_out, gd_out, gu_out, go_out, gs, rd, ru = rest[8:17]
    refs = rest[17:25]
    mid, n2, n2t = refs[0], refs[1], refs[2]
    cot, ctx, wo, wu, wd, act, gm, gd, gu = rest[25:34]
    bufs, (local, sems, recv, rlocal, rsend, rrecv) = rest[34:46], rest[46:52]
    w = Place()
    last = PARTS - 1
    items = {
        "u": Gather(w, up_later, wu.at[last], sems, recv, 0),
        "d": Gather(w, down_later, wd.at[last], sems, recv, 1),
        "rd": Reduce(w, gd.at[0], bufs[0:6], rd, rlocal.at[0], rsend.at[0], rrecv.at[0]),
        "ru": Reduce(w, gu.at[0], bufs[6:12], ru, rlocal.at[1], rsend.at[1], rrecv.at[1]),
    }
    moves = Moves(items, MLP_PLAN)
    keep = []

    def move(src, dst):
        keep.append(load(src, dst, local.at[len(keep)]))
        return keep[-1]

    def hooks(where, step=None):
        if where == "start":
            move(ctx_in, ctx), move(x_in, mid), move(wo_in, wo), move(cot_in, cot)
            for c in range(last):
                move(wu_in.at[c], wu.at[c])
                move(wd_in.at[c], wd.at[c])
            for own, full in ((up_later, wu), (down_later, wd)):
                count = full.shape[1] // 8
                move(own, full.at[last, pl.ds(pl.multiple_of(w.p * count, 16), count)])
            greet(w.partners())
            moves.at(0)
            for copy in keep[:4]:
                copy.wait()
        elif where == "entered":
            for copy in keep[4:]:
                copy.wait()
            keep.clear()
        elif where == "block":
            moves.within(step + 1, 1, 12)
        elif where == "blocks":
            for c in (1, 2):
                move(gd.at[c], gd_out.at[c - 1])
                move(gu.at[c], gu_out.at[c - 1])
            moves.at(13)
        else:
            move(act, act_out)
            move(gm, gm_out)
            move(n2, gctx_out)
            move(n2t.at[:, pl.ds(0, D)], go_out)
            moves.at(14)
            for copy in keep:
                copy.wait()

    mlp_compute(
        images,
        True,
        side_ref,
        scale_ref[0],
        cot,
        ctx,
        small,
        wo,
        wu,
        wd,
        refs,
        (act, gm, n2, gd, gu, n2t.at[:, pl.ds(0, D)], gs),
        hooks,
    )


MLP_PLAN = {
    "u": (1, 4, 7, 9, 9),
    "d": (0, 1, 4, 6, 8),
    "rd": (5, 6, 8, 9, 11, 13, 14),
    "ru": (6, 8, 10, 12, 13, 14, 14),
}


PARTS = 3
BLOCKS = 4


def attend_back_step(images, step, side_ref, qkv_ref, gctx_ref, lse_ref, cos_ref, sin_ref, gproj_ref, gs_ref, gf_ref):
    i, rows, c, at = head_pair(images, step)
    q = qkv_ref[rows, pl.ds(at, 128)]
    k = qkv_ref[rows, pl.ds(at + THIRD, 128)]
    v = qkv_ref[rows, pl.ds(at + 2 * THIRD, 128)]
    go = gctx_ref[rows, pl.ds(c, 128)]
    lane = lax.broadcasted_iota(jnp.int32, (1, 128), 1)
    mask = mask_column(side_ref, i)
    lse = lse_ref[step]
    dq, dk, dv = [], [], []
    for h in range(2):
        mine = lane // HD == h
        qm = jnp.where(mine, q, jnp.zeros_like(q))
        gom = jnp.where(mine, go, jnp.zeros_like(go))
        s = dot(k, qm, NT) * (LOG2E / math.sqrt(HD)) + mask
        p = jnp.exp2(s - lse[h : h + 1])
        dp = dot(v, gom, NT)
        dv.append(dot(p.astype(BF), go, NN))
        t = p * dp
        ds = (t - p * jnp.sum(t, axis=0, keepdims=True)).astype(BF)
        dk.append(dot(ds, q, NN))
        dq.append(dot(ds, k, TN))
    first = lane < HD
    cs = cos_ref[rows, pl.ds(c, 128)]
    sn = sin_ref[rows, pl.ds(c, 128)]
    angle = None
    for n, (pair, rot) in enumerate(((dq, q), (dk, k))):
        e = jnp.where(first, pair[0], pair[1]) * (1.0 / math.sqrt(HD))
        other = swap_halves(e)
        back = (e * cs - other * sn).astype(BF)
        gproj_ref[rows, pl.ds(at + n * THIRD, 128)] = back
        gs_ref[pl.ds(R_QB + n, 1), pl.ds(c, 128)] += jnp.sum(back.astype(F32), axis=0, keepdims=True)
        term = rot.astype(F32) * other
        angle = term if angle is None else angle + term
    gv = jnp.where(first, dv[0], dv[1]).astype(BF)
    gproj_ref[rows, pl.ds(at + 2 * THIRD, 128)] = gv
    gs_ref[R_QB + 2 : R_QB + 3, pl.ds(c, 128)] += jnp.sum(gv.astype(F32), axis=0, keepdims=True)
    angle = angle * half_sign(128)
    col, row, _ = patch_columns(side_ref, i)
    gf_ref[0:1, pl.ds(c, 128)] += jnp.sum(angle * col, axis=0, keepdims=True)
    gf_ref[1:2, pl.ds(c, 128)] += jnp.sum(angle * row, axis=0, keepdims=True)


def freq_row(gf_ref):
    hi = lax.Precision.HIGHEST
    both = gf_ref[...]
    return (
        dot(both[0:8], spread(0).astype(F32), NT, hi)[0:1] + dot(both[0:8], spread(1).astype(F32), NT, hi)[1:2]
    )


def weight_third(c, scale, norm_ref, gproj_ref, gw_ref):
    def block(j, _):
        lanes = pl.ds(pl.multiple_of(j * THIRD, THIRD), THIRD)
        full = pl.ds(pl.multiple_of(c * D + j * THIRD, THIRD), THIRD)
        gw_ref[:, lanes] = (dot(norm_ref[...], gproj_ref[:, full], TN) * scale).astype(BF)
        return 0

    lax.fori_loop(0, 3, block, 0)


def attend_back_compute(images, thirds, side_ref, scale, ins, norm, gproj, gws, gs_ref, gf_ref, hooks):
    hooks("start")
    gs_ref[...] = jnp.zeros_like(gs_ref)
    gf_ref[...] = jnp.zeros_like(gf_ref)

    def body(step, _):
        hooks("step", step)
        attend_back_step(images, step, side_ref, *ins, gproj, gs_ref, gf_ref)
        for c in range(thirds):

            @pl.when(step == 2 * images * (c + 1) - 1)
            def _(c=c):
                weight_third(c, scale, norm, gproj, gws.at[c])

        return 0

    lax.fori_loop(0, images * HEADS // 2, body, 0)
    gs_ref[R_FR : R_FR + 1] = freq_row(gf_ref)
    hooks("end")


def attend_back_plain(images, side_ref, scale_ref, *refs):
    ins, norm, (gproj, gws, gs, gf) = refs[0:5], refs[5], refs[6:10]
    attend_back_compute(images, 3, side_ref, scale_ref[0], ins, norm, gproj, gws, gs, gf, lambda *a: None)


def attend_back_reduce(images, side_ref, scale_ref, *refs):
    ins_in, norm_in, (gd, gu, go) = refs[0:5], refs[5], refs[6:9]
    gproj_out, gs, outs = refs[9], refs[10], refs[11:18]
    ins, norm, gproj, gws, gf = refs[18:23], refs[23], refs[24], refs[25], refs[26]
    bufs, (load_sems, local, send, recv) = refs[27:69], refs[69:73]
    w = Place()
    srcs = (gd.at[0], gu.at[0], gd.at[1], gu.at[1], go, gws.at[0], gws.at[1])
    items = {
        name: Reduce(w, srcs[i], bufs[6 * i : 6 * i + 6], outs[i], local.at[i], send.at[i], recv.at[i])
        for i, name in enumerate(BACK_PLAN)
    }
    moves = Moves(items, BACK_PLAN)

    def hooks(where, step=None):
        if where == "start":
            copies = [load(src, dst, load_sems.at[i]) for i, (src, dst) in enumerate(zip(ins_in + (norm_in,), ins + (norm,)))]
            greet(w.partners())
            moves.at(0)
            for copy in copies:
                copy.wait()
        elif where == "step":
            moves.within(step + 1, 1, 12)
        else:
            copy = load(gproj, gproj_out, load_sems.at[0])
            moves.at(13)
            moves.at(14)
            copy.wait()

    attend_back_compute(images, 2, side_ref, scale_ref[0], ins, norm, gproj, gws, gs, gf, hooks)


BACK_PLAN = {
    "d1": (3, 4, 7, 9, 11, 14, 14),
    "u1": (0, 2, 4, 8, 10, 13, 13),
    "d2": (1, 3, 5, 8, 10, 12, 12),
    "u2": (3, 7, 9, 10, 13, 14, 14),
    "o": (0, 3, 7, 9, 11, 12, 13),
    "q0": (5, 8, 10, 12, 13, 14, 14),
    "q1": (9, 9, 11, 12, 13, 14, 14),
}


def qkv_back_compute(images, x_ref, gproj_ref, gm_ref, small_ref, w_ref, gs_in, gin_ref, gs_ref, hooks):
    hooks("start")
    gain = small_ref[R_G1 : R_G1 + 1]
    gs_ref[...] = gs_in[...]
    for i in range(images):
        rows = pl.ds(i * SLOT, SLOT)
        unit, inv = norm_stats(x_ref[rows])
        gn = None
        for c in range(3):
            term = dot(gproj_ref[rows, c * D : (c + 1) * D], w_ref[c], NT)
            gn = term if gn is None else gn + term
        gs_ref[R_G1 : R_G1 + 1] += jnp.sum(gn * unit, axis=0, keepdims=True)
        gs_ref[R_S1 : R_S1 + 1] += jnp.sum(gn, axis=0, keepdims=True)
        a = gn * gain
        ma = jnp.mean(a, axis=-1, keepdims=True)
        mu = jnp.mean(a * unit, axis=-1, keepdims=True)
        gin_ref[rows] = gm_ref[rows] + inv * (a - ma - unit * mu)
        hooks("image", i)
    hooks("end")


def qkv_back_plain(images, scale_ref, x_ref, gproj_ref, gm_ref, small_ref, w_ref, gs_in, gin, gs):
    def hooks(where, index=None):
        if where == "end":
            gs[...] = gs[...] * scale_ref[0]

    qkv_back_compute(images, x_ref, gproj_ref, gm_ref, small_ref, w_ref, gs_in, gin, gs, hooks)


def qkv_back_reduce(images, scale_ref, small_ref, gs_att, gs_mlp, *refs):
    ins_in, (gin, gs, out) = refs[0:5], refs[5:8]
    norm, gproj, x, w_ref, gm = refs[8:13]
    gw, bufs, tinybufs, (load_sems, local, send, recv, ssend, srecv) = refs[13], refs[14:20], refs[20], refs[21:27]
    w = Place()
    last = Reduce(w, gw, bufs, out, local, send, recv)
    tiny = SmallSum(w, gs, tinybufs, ssend, srecv)

    def hooks(where, index=None):
        if where == "start":
            copies = [load(src, dst, load_sems.at[i]) for i, (src, dst) in enumerate(zip(ins_in, refs[8:13]))]
            greet(w.partners() + [(w.g ^ 3, w.p)])
            copies[0].wait()
            copies[1].wait()
            weight_third(2, scale_ref[0], norm, gproj, gw)
            last.stage(0)
            for copy in copies[2:]:
                copy.wait()
        elif where == "image":
            last.stage(index + 1)
        else:
            gs[...] = gs[...] * scale_ref[0] + gs_mlp[...]
            tiny.stage(0)
            last.stage(3)
            tiny.stage(1)
            last.stage(4)
            tiny.stage(2)
            last.stage(5)
            tiny.stage(3)
            last.stage(6)

    qkv_back_compute(images, x, gproj, gm, small_ref, w_ref, gs_att, gin, gs, hooks)


def params(mb=56):
    return pltpu.CompilerParams(vmem_limit_bytes=mb << 20)


def place_rows(p, dp, vec):
    n = vec.shape[0]
    whole = jnp.tile(vec, dp)
    owner = jnp.arange(n * dp, dtype=jnp.int32) // n
    return jnp.where(owner == p, whole, 0.0).reshape(-1, D)


def on_device(
    fast,
    images,
    cotangent,
    resolution,
    assignment,
    counts,
    ln1_gain,
    ln1_shift,
    qkv_weight,
    qkv_bias,
    rope_freqs,
    out_weight,
    out_bias,
    ln2_gain,
    ln2_shift,
    up_weight,
    up_bias,
    down_weight,
    down_bias,
):
    p = lax.axis_index("dp")
    dp = lax.axis_size("dp")
    n = images.shape[0]
    rows = n * SLOT
    x = images.reshape(rows, D)
    cot = cotangent.reshape(rows, D)
    side = jnp.where(resolution == 0, SIDE_S, jnp.where(resolution == 1, SIDE_M, SIDE_L)).astype(jnp.int32)
    group_total = counts.shape[0]
    cf = counts.astype(F32)
    picked = jnp.sum(jnp.where(assignment[0] == jnp.arange(group_total, dtype=jnp.int32), cf, 0.0))
    scale = group_total * picked / jnp.sum(cf) / math.sqrt(dp * n * SLOT)
    scale = scale.reshape(1)
    packed = jnp.concatenate(
        [
            place_rows(p, dp, lax.reduce_precision(v, 8, 7))
            for v in (ln1_gain, ln1_shift, qkv_bias, rope_freqs, out_bias, ln2_gain, ln2_shift, up_bias, down_bias)
        ]
        + [jnp.zeros((2, D), F32)],
        axis=0,
    )
    sds = jax.ShapeDtypeStruct
    smem = pl.BlockSpec(memory_space=pltpu.SMEM)
    anyw = pl.BlockSpec(memory_space=pl.ANY)
    kept = [
        sds((rows, 3 * D), BF),
        sds((rows, D), BF),
        sds((rows, D), F32),
        sds((rows, D), F32),
        sds((rows, D), BF),
        sds((n * HEADS // 2, 8, SLOT), F32),
    ]
    weights = (qkv_weight, out_weight, up_weight, down_weight)
    dma = pltpu.SemaphoreType.DMA
    vmem = pltpu.VMEM

    def moving(number, mb):
        return pltpu.CompilerParams(vmem_limit_bytes=mb << 20, collective_id=number, has_side_effects=True)

    part = FF // PARTS
    if fast:
        later = [sds((D // dp, part), BF), sds((part // dp, D), BF)]
        fulls = [sds((3, D, D), BF), sds((D, D), BF), sds((PARTS - 1, D, part), BF), sds((PARTS - 1, part, D), BF)]
        outs = pl.pallas_call(
            functools.partial(forward_gather, n),
            out_shape=kept + [sds((R_ALL, D), F32)] + fulls + later,
            in_specs=[smem] + vm(6),
            out_specs=[anyw] * 4 + vm(3) + [anyw] * 6,
            scratch_shapes=[
                vmem((rows, 3 * D), BF),
                vmem((rows, D), BF),
                vmem((rows, D), F32),
                vmem((rows, D), F32),
                vmem((3, D, D), BF),
                vmem((8, R_ALL, D), F32),
                vmem((3, D // dp, D), BF),
                vmem((D // dp, D), BF),
                vmem((PARTS, D // dp, part), BF),
                vmem((PARTS, part // dp, D), BF),
                dma((16,)),
                dma((8, 16)),
                dma((7,)),
                dma((7,)),
                dma((12,)),
            ],
            compiler_params=moving(0, 56),
            name="forward",
        )(side, x, packed, *weights)
        qkv, norm1, cos, sin, ctx, lse, small, wqkv, wo, wu, wd, up_later, down_later = outs
    else:
        small = lax.psum(packed, "dp")
        wqkv, wo, wu, wd = [lax.all_gather(v.astype(BF), "dp", axis=0, tiled=True) for v in weights]
        wqkv = wqkv.reshape(D, 3, 3, THIRD).transpose(2, 0, 1, 3).reshape(3, D, D)
        wu = wu.reshape(D, PARTS, part).transpose(1, 0, 2)
        wd = wd.reshape(PARTS, part, D)
        qkv, norm1, cos, sin, ctx, lse = pl.pallas_call(
            functools.partial(forward_plain, n),
            out_shape=kept,
            in_specs=[smem] + vm(3),
            out_specs=vm(6),
            compiler_params=params(),
            name="forward",
        )(side, x, small, wqkv)

    grads = [sds((PARTS, part, D), BF), sds((PARTS, D, part), BF), sds((D, D), BF)]
    rest = [sds((R_ALL, D), F32)]
    firsts = [sds((rows, D), F32), sds((rows, D), F32), sds((rows, D), BF)]
    tables = [vmem((rows, 3 * D), BF), vmem((rows, D), BF), vmem((n * HEADS // 2, 8, SLOT), F32)]
    tables += [vmem((rows, D), F32)] * 2
    gproj_shape = sds((rows, 3 * D), BF)
    if fast:
        sizes = [(part // dp, D), (D // dp, part)]
        act, gm, gctx, gdown, gup, gout, gs_mlp, rdown0, rup0 = pl.pallas_call(
            functools.partial(mlp_moving, n),
            out_shape=firsts
            + [sds((PARTS - 1,) + g.shape[1:], BF) for g in grads[:2]]
            + grads[2:]
            + rest
            + [sds(z, F32) for z in sizes],
            in_specs=[smem, smem] + vm(1) + [anyw] * 8,
            out_specs=[anyw] * 6 + vm(3),
            scratch_shapes=mlp_scratch(rows)
            + [
                vmem((rows, D), F32),
                vmem((rows, D), BF),
                vmem((D, D), BF),
                vmem((PARTS, D, part), BF),
                vmem((PARTS, part, D), BF),
                vmem((rows, D), F32),
                vmem((rows, D), F32),
                vmem((PARTS, part, D), BF),
                vmem((PARTS, D, part), BF),
            ]
            + sum([Reduce.buffers(*z) for z in sizes], [])
            + [dma((12,)), dma((4,)), dma((2, 16)), dma((2,)), dma((2,)), dma((2, 6))],
            compiler_params=moving(3, 63),
            name="mlp",
        )(side, scale, small, x, cot, ctx, wo, wu, wd, up_later, down_later)
        third = (D // dp, D)
        sizes = sizes + sizes + [third] * 3
        gproj, gs_att, rdown1, rup1, rdown2, rup2, rout, rq0, rq1 = pl.pallas_call(
            functools.partial(attend_back_reduce, n),
            out_shape=[gproj_shape] + rest + [sds(z, F32) for z in sizes],
            in_specs=[smem, smem] + [anyw] * 9,
            out_specs=[anyw] + vm(8),
            scratch_shapes=tables
            + [vmem((rows, D), BF), vmem((rows, 3 * D), BF), vmem((2, D, D), BF), vmem((8, D), F32)]
            + sum([Reduce.buffers(*z) for z in sizes], [])
            + [dma((6,)), dma((7,)), dma((7,)), dma((7, 6))],
            compiler_params=moving(1, 62),
            name="attend_back",
        )(side, scale, qkv, gctx, lse, cos, sin, norm1, gdown, gup, gout)
        gin, gs, rq2 = pl.pallas_call(
            functools.partial(qkv_back_reduce, n),
            out_shape=[sds((rows, D), F32)] + rest + [sds(third, F32)],
            in_specs=[smem] + vm(3) + [anyw] * 5,
            out_specs=vm(3),
            scratch_shapes=[
                vmem((rows, D), BF),
                vmem((rows, 3 * D), BF),
                vmem((rows, D), F32),
                vmem((3, D, D), BF),
                vmem((rows, D), F32),
                vmem((D, D), BF),
            ]
            + Reduce.buffers(*third)
            + [vmem((12, R_ALL, D), F32), dma((5,)), dma, dma, dma((6,)), dma((3, 4)), dma((3, 4))],
            compiler_params=moving(2, 60),
            name="project_back",
        )(scale, small, gs_att, gs_mlp, norm1, gproj, x, wqkv, gm)

        def interleave(parts, count):
            height, width = parts[0].shape
            blocks = [v.reshape(height, count, width // count) for v in parts]
            return jnp.stack(blocks, axis=2).reshape(height, -1)

        rdown = jnp.concatenate([rdown0, rdown1, rdown2], axis=0)
        rup = interleave([rup0, rup1, rup2], dp)
        rqkv = interleave([rq0, rq1, rq2], 3)
    else:
        act, gm, gctx, gdown, gup, gout, gs_mlp = pl.pallas_call(
            functools.partial(mlp_plain, n),
            out_shape=firsts + grads + rest,
            in_specs=[smem, smem, anyw] + vm(6),
            out_specs=vm(7),
            scratch_shapes=mlp_scratch(rows) + [dma((1,))],
            compiler_params=params(63),
            name="mlp",
        )(side, scale, x, cot, ctx, small, wo, wu, wd)
        gproj, gqkv, gs_att = pl.pallas_call(
            functools.partial(attend_back_plain, n),
            out_shape=[gproj_shape, sds((3, D, D), BF)] + rest,
            in_specs=[smem, smem] + vm(6),
            out_specs=vm(3),
            scratch_shapes=[vmem((8, D), F32)],
            compiler_params=params(),
            name="attend_back",
        )(side, scale, qkv, gctx, lse, cos, sin, norm1)
        gin, gs_qkv = pl.pallas_call(
            functools.partial(qkv_back_plain, n),
            out_shape=[sds((rows, D), F32)] + rest,
            in_specs=[smem] + vm(6),
            out_specs=vm(2),
            compiler_params=params(),
            name="project_back",
        )(scale, x, gproj, gm, small, wqkv, gs_att)

        def reduce(g):
            total = lax.psum_scatter(g, "dp", scatter_dimension=0, tiled=True)
            return lax.psum(total, "group").astype(F32)

        gqkv = gqkv.reshape(3, D, 3, THIRD).transpose(1, 2, 0, 3).reshape(D, 3 * D)
        gup = gup.transpose(1, 0, 2).reshape(D, FF)
        rqkv, rout, rup, rdown = [reduce(g) for g in (gqkv, gout, gup, gdown.reshape(FF, D))]
        gs = lax.psum(gs_mlp + gs_qkv, ("group", "dp"))

    def own(first, count):
        flat = gs[first : first + count].reshape(dp, -1)
        return lax.dynamic_index_in_dim(flat, p, 0, keepdims=False)

    return (
        act.reshape(images.shape),
        gin.reshape(images.shape),
        own(R_G1, 1),
        own(R_S1, 1),
        rqkv,
        own(R_QB, 3),
        own(R_FR, 1),
        rout,
        own(R_OB, 1),
        own(R_G2, 1),
        own(R_S2, 1),
        rup,
        own(R_UB, 4),
        rdown,
        own(R_DB, 1),
    )


def solution(mesh):
    batch = P(("group", "dp"), None, None)
    per_image = P(("group", "dp"))
    vec, mat = P("dp"), P("dp", None)
    fast = dict(mesh.shape) == {"group": 4, "dp": 8}
    return jax.shard_map(
        functools.partial(on_device, fast),
        mesh=mesh,
        in_specs=(batch, batch, per_image, per_image, P(), vec, vec, mat, vec, vec, mat, vec, vec, vec, mat, vec, mat, vec),
        out_specs=(batch, batch, vec, vec, mat, vec, vec, mat, vec, vec, vec, mat, vec, mat, vec),
        check_vma=False,
    )
```

```python
import functools
import math

import jax
import jax.numpy as jnp
from jax import lax
from jax.experimental import pallas as pl
from jax.experimental.pallas import tpu as pltpu
from jax.sharding import PartitionSpec as P

HEADS = 12
HD = 64
SIDE_S = 14
SIDE_M = 20
SIDE_L = 24
SLOT = 576
D = 768
FF = 3072
LN_EPS = 1e-06
MASK_FILL = -1e30
BF = jnp.bfloat16
F32 = jnp.float32
NT = (((1,), (1,)), ((), ()))
NN = (((1,), (0,)), ((), ()))
TN = (((0,), (0,)), ((), ()))
R_G1, R_S1, R_QB, R_FR, R_OB, R_G2, R_S2, R_UB, R_DB, R_ALL = 0, 1, 2, 5, 6, 7, 8, 9, 13, 16
THIRD = 256
LOG2E = math.log2(math.e)


def dot(a, b, dims, precision=None):
    return lax.dot_general(a, b, dims, preferred_element_type=F32, precision=precision)


def vm(n):
    return [pl.BlockSpec(memory_space=pltpu.VMEM)] * n


def norm_stats(x):
    mean = jnp.mean(x, axis=-1, keepdims=True)
    cen = x - mean
    var = jnp.mean(cen * cen, axis=-1, keepdims=True)
    inv = lax.rsqrt(var + LN_EPS)
    return cen * inv, inv


def sincos(x):
    n = jnp.floor(x * (2.0 / math.pi) + 0.5)
    r = x - n * 1.5703125
    r = r - n * 4.837512969970703125e-4
    r = r - n * 7.54978995489188216e-8
    q = n.astype(jnp.int32)
    r2 = r * r
    s = r + r * r2 * (-1.6666654611e-1 + r2 * (8.3321608736e-3 + r2 * -1.9515295891e-4))
    c = 1.0 - 0.5 * r2 + r2 * r2 * (
        4.166664568298827e-2 + r2 * (-1.388731625493765e-3 + r2 * 2.443315711809948e-5)
    )
    odd = (q & 1) == 1
    ss = jnp.where(odd, c, s)
    cc = jnp.where(odd, s, c)
    ss = jnp.where((q & 2) == 2, -ss, ss)
    cc = jnp.where(((q + 1) & 2) == 2, -cc, cc)
    return ss, cc


ERFC = (
    0.07314588129520416,
    -0.30809587240219116,
    0.3798876702785492,
    -0.08230462670326233,
    0.245080828666687,
    0.2054724544286728,
    0.24429383873939514,
    0.242519810795784,
)


def gelu_pair(x):
    z = jnp.abs(x)
    t = 1.0 / (1.0 + (0.43 * math.sqrt(0.5)) * z)
    poly = 0.5 * ERFC[0]
    for c in ERFC[1:]:
        poly = poly * t + 0.5 * c
    bell = jnp.exp2((x * x) * (-0.5 * LOG2E))
    half = poly * t * bell
    cdf = jnp.where(x < 0, half, 1.0 - half)
    return x * cdf, cdf + (x * math.sqrt(0.5 / math.pi)) * bell


def swap_halves(x):
    width = x.shape[-1]
    lane = lax.broadcasted_iota(jnp.int32, (1, width), 1)
    ahead = pltpu.roll(x, width - HD // 2, 1)
    behind = pltpu.roll(x, HD // 2, 1)
    return jnp.where(lane % HD < HD // 2, ahead, behind)


def half_sign(width):
    lane = lax.broadcasted_iota(jnp.int32, (1, width), 1)
    return jnp.where(lane % HD < HD // 2, 1.0, -1.0).astype(F32)


def side_of(res_ref, image):
    res = res_ref[image]
    return jnp.where(res == 0, SIDE_S, jnp.where(res == 1, SIDE_M, SIDE_L))


def device_weight(slots, assign_ref, counts_ref):
    groups = counts_ref.shape[0]
    counts = [jnp.full((1, 128), counts_ref[i], jnp.int32).astype(F32) for i in range(groups)]
    mine = jnp.full((1, 128), assign_ref[0], jnp.int32)
    picked = sum(jnp.where(mine == i, counts[i], 0.0) for i in range(groups))
    return (groups * picked / sum(counts) * (1.0 / math.sqrt(slots)))[:, :1]


def patch_columns(side_ref, image):
    side = jnp.full((SLOT, 128), side_of(side_ref, image), jnp.int32).astype(F32)
    slot = lax.broadcasted_iota(jnp.int32, (SLOT, 128), 0).astype(F32)
    row = jnp.floor((slot + 0.5) / side)
    col = slot - row * side
    valid = slot < side * side
    return col, row, valid


def spread(parity):
    src = lax.broadcasted_iota(jnp.int32, (128, 128), 0)
    lane = lax.broadcasted_iota(jnp.int32, (128, 128), 1)
    return (src == parity * HD + (lane // HD) * (HD // 2) + lane % (HD // 2)).astype(BF)


class Place:
    def __init__(self):
        self.p = lax.axis_index("dp")
        self.g = lax.axis_index("group")
        self.z, self.y = self.p // 2, self.p % 2
        self.x, self.core = self.g // 2, self.g % 2

    def over(self):
        return (self.g, self.p ^ 1)

    def sibling(self):
        return (self.g ^ 1, self.p)

    def across(self):
        return (self.g ^ 2, self.p)

    def line(self):
        return [(self.g, self.p ^ (2 * k)) for k in (1, 2, 3)]

    def partners(self):
        return [self.sibling(), self.across(), self.over()] + self.line()


def remote(src, dst, send, recv, device):
    return pltpu.make_async_remote_copy(
        src_ref=src, dst_ref=dst, send_sem=send, recv_sem=recv, device_id=device, device_id_type=pl.DeviceIdType.MESH
    )


def load(src, dst, sem):
    copy = pltpu.make_async_copy(src, dst, sem)
    copy.start()
    return copy


def greet(devices):
    barrier = pltpu.get_barrier_semaphore()
    for device in devices:
        pl.semaphore_signal(barrier, inc=1, device_id=device, device_id_type=pl.DeviceIdType.MESH)
    pl.semaphore_wait(barrier, len(devices))


def timetable(plan):
    return sorted(((step, name, stage) for name, steps in plan.items() for stage, step in enumerate(steps)), key=lambda r: r[0])


class Moves:
    def __init__(self, items, plan):
        self.items, self.rows = items, timetable(plan)

    def at(self, step):
        for when, name, stage in self.rows:
            if when == step:
                self.items[name].stage(stage)

    def within(self, step, first, last):
        for when in sorted({r[0] for r in self.rows if first <= r[0] <= last}):
            pl.when(step == when)(functools.partial(self.at, when))


class Gather:
    STAGES = 5

    def __init__(self, place, own, full, sems, recv, index):
        self.w, self.own, self.full = place, own, full
        self.rows = full.shape[0] // 8
        self.t = self.rows // 3 if self.rows % 48 == 0 else self.rows * 3 // 8
        self.e = self.rows - 2 * self.t
        self.send, self.sib = sems.at[2 * index], sems.at[2 * index + 1]
        self.recv = recv.at[index]

    def part(self, block, piece, ref=None):
        ref = self.full if ref is None else ref
        first = block * self.rows + piece * self.t
        return ref.at[pl.ds(pl.multiple_of(first, 16), self.e if isinstance(piece, int) else self.t)]

    def push(self, ref, device, index, src=None):
        remote(ref if src is None else src, ref, self.send, self.recv.at[index], device).start()

    def got(self, ref, index):
        remote(ref, ref, self.send, self.recv.at[index], self.w.sibling()).wait_recv()

    def hand(self, ref):
        remote(ref, ref, self.send, self.sib, self.w.sibling()).start()

    def stage(self, number):
        w = self.w
        pl.when(w.core == 0)(lambda: self.step(number, w.x, True))
        pl.when(w.core == 1)(lambda: self.step(number, 2, False))

    def step(self, number, piece, split):
        w = self.w
        if number == 0:
            src = self.part(0, piece, self.own)
            for k in (1, 3, 2):
                self.push(self.part(w.p, piece), (w.g, w.p ^ (2 * k)), w.z, src)
            self.push(self.part(w.p, piece), w.over(), 4 + w.z, src)
        elif number in (1, 2):
            for k in (1, 3, 2) if number == 1 else (0, 1, 3, 2):
                z = w.z ^ k
                block = 2 * z + (w.y if number == 1 else 1 - w.y)
                ref = self.part(block, piece)
                self.got(ref, z if number == 1 else 4 + z)
                if number == 1:
                    self.push(ref, w.over(), 4 + z)
                if split:
                    self.push(ref, w.across(), 8 + block)
                self.hand(ref)
        elif number == 3:
            if split:
                for k in (2, 6, 4, 1, 3, 7, 5):
                    block = w.p ^ k
                    ref = self.part(block, 1 - w.x)
                    self.got(ref, 8 + block)
                    self.hand(ref)
        else:
            for count in (14 * self.t, 14 * self.t) if split else (14 * self.e,):
                done = self.full.at[pl.ds(0, count)]
                remote(done, done, self.send, self.sib, w.sibling()).wait_send()
            came = self.full.at[pl.ds(0, 7 * self.e if split else 14 * self.t)]
            remote(came, came, self.send, self.sib, w.sibling()).wait_recv()


class Reduce:
    STAGES = 7

    def __init__(self, place, src, bufs, out, local, send, recv):
        self.w, self.src, self.out = place, src, out
        self.mine, self.cbuf, self.ybuf, self.zbuf, self.xbuf, self.fbuf = bufs
        self.rows = src.shape[0] // 8
        self.t, self.e = self.split(self.rows)
        self.local, self.send, self.recv = local, send, recv

    @staticmethod
    def split(rows):
        t = rows // 4 if rows % 64 == 0 else rows // 3
        return t, rows - 2 * t

    @classmethod
    def buffers(cls, rows, width):
        t, e = cls.split(rows)
        big = max(2 * t, e)
        sizes = (8 * big, 8 * big, 4 * max(t, e), 4 * max(t, e), 8 * t, max(t, e))
        return [pltpu.VMEM((n, width), BF) for n in sizes]

    def copy(self, src, dst, index, device):
        return remote(src, dst, self.send, self.recv.at[index], device)

    def took(self, ref, index):
        self.copy(ref, ref, index, self.w.sibling()).wait_recv()

    def rows_of(self, ref, first, count):
        return ref.at[pl.ds(pl.multiple_of(first, 16), count)]

    def add(self, target, *terms):
        def body(i, _):
            rows = pl.ds(pl.multiple_of(i * 32, 32), 32)
            total = target[rows].astype(F32)
            for term in terms:
                total = total + term[rows].astype(F32)
            target[rows] = total.astype(BF)
            return 0

        lax.fori_loop(0, target.shape[0] // 32, body, 0)

    def each_core(self, first, second):
        pl.when(self.w.core == 0)(first)
        pl.when(self.w.core == 1)(second)

    def exchange(self, theirs, their_rows, ours, our_rows):
        def body(b, _):
            self.copy(
                self.rows_of(self.src, b * self.rows + theirs, their_rows),
                self.rows_of(self.cbuf, b * their_rows, their_rows),
                0,
                self.w.sibling(),
            ).start()
            pltpu.make_async_copy(
                self.rows_of(self.src, b * self.rows + ours, our_rows),
                self.rows_of(self.mine, b * our_rows, our_rows),
                self.local,
            ).start()
            return 0

        lax.fori_loop(0, 8, body, 0)

    def settle(self, count):
        whole = self.mine.at[pl.ds(0, 8 * count)]
        pltpu.make_async_copy(whole, whole, self.local).wait()
        self.took(self.cbuf.at[pl.ds(0, 8 * count)], 0)
        self.add(whole, self.cbuf)

    def zero_at(self, block, piece):
        return self.rows_of(self.mine, block * 2 * self.t + piece * self.t, self.t)

    def one_at(self, block):
        return self.rows_of(self.mine, block * self.e, self.e)

    def send_y(self, count, at):
        w = self.w

        def body(z, _):
            self.copy(at(2 * z + 1 - w.y), self.rows_of(self.ybuf, z * count, count), 2, w.over()).start()
            return 0

        lax.fori_loop(0, 4, body, 0)

    def take_y(self, count, at):
        self.took(self.ybuf.at[pl.ds(0, 4 * count)], 2)

        def body(z, _):
            self.add(at(2 * z + self.w.y), self.rows_of(self.ybuf, z * count, count))
            return 0

        lax.fori_loop(0, 4, body, 0)

    def send_z(self, count, at):
        w = self.w
        for k in (3, 1, 2):
            z = w.z ^ k
            self.copy(at(2 * z + w.y), self.rows_of(self.zbuf, k * count, count), 3, (w.g, 2 * z + w.y)).start()

    def take_z(self, count, at):
        self.took(self.zbuf.at[pl.ds(0, 3 * count)], 3)
        self.add(at(self.w.p), *[self.rows_of(self.zbuf, k * count, count) for k in (1, 2, 3)])

    def give(self, first, count, value):
        ref = self.out.at[pl.ds(pl.multiple_of(first, 8), count)]
        ref[...] = value
        remote(ref, ref, self.send, self.recv.at[5], self.w.sibling()).start()

    def stage(self, number):
        w, t, e = self.w, self.t, self.e
        x_mine = functools.partial(self.zero_at, piece=w.x)
        x_other = functools.partial(self.zero_at, piece=1 - w.x)
        if number == 0:
            self.each_core(lambda: self.exchange(2 * t, e, 0, 2 * t), lambda: self.exchange(0, 2 * t, 2 * t, e))
        elif number == 1:

            def first():
                self.settle(2 * t)

                def body(b, _):
                    self.copy(x_other(b), self.rows_of(self.xbuf, b * t, t), 1, w.across()).start()
                    return 0

                lax.fori_loop(0, 8, body, 0)

            def second():
                self.settle(e)
                self.send_y(e, self.one_at)

            self.each_core(first, second)
        elif number == 2:

            def first():
                self.took(self.xbuf, 1)

                def body(b, _):
                    self.add(x_mine(b), self.rows_of(self.xbuf, b * t, t))
                    return 0

                lax.fori_loop(0, 8, body, 0)
                self.send_y(t, x_mine)

            def second():
                self.take_y(e, self.one_at)
                self.send_z(e, self.one_at)

            self.each_core(first, second)
        elif number == 3:

            def first():
                self.take_y(t, x_mine)
                self.send_z(t, x_mine)

            def second():
                self.take_z(e, self.one_at)
                self.copy(self.one_at(w.p), self.fbuf.at[pl.ds(0, e)], 4, w.across()).start()

            self.each_core(first, second)
        elif number == 4:

            def first():
                self.take_z(t, x_mine)
                self.copy(x_mine(w.p), self.fbuf.at[pl.ds(0, t)], 4, w.across()).start()
                self.give(w.x * t, t, x_mine(w.p)[...].astype(F32))

            def second():
                self.took(self.fbuf.at[pl.ds(0, e)], 4)
                self.give(2 * t, e, self.one_at(w.p)[...].astype(F32) + self.fbuf[pl.ds(0, e)].astype(F32))

            self.each_core(first, second)
        elif number == 5:

            @pl.when(w.core == 0)
            def _():
                self.took(self.fbuf.at[pl.ds(0, t)], 4)
                self.give((1 - w.x) * t, t, self.fbuf[pl.ds(0, t)].astype(F32))

        else:

            def sent(count):
                while count > 0:
                    now = min(count, self.mine.shape[0])
                    part = self.mine.at[pl.ds(0, now)]
                    remote(part, part, self.send, self.recv.at[0], w.sibling()).wait_send()
                    count -= now

            def came(first, count):
                ref = self.out.at[pl.ds(first, count)]
                remote(ref, ref, self.send, self.recv.at[5], w.sibling()).wait_recv()

            def first():
                came(2 * t, e)
                sent(8 * e + 8 * t + 4 * t + 3 * t + t + 4 * t)

            def second():
                came(0, 2 * t)
                sent(16 * t + 4 * e + 3 * e + e + 2 * e)

            self.each_core(first, second)


class SmallSum:
    HOPS = (4, 2, 4)

    def __init__(self, place, value, bufs, send, recv):
        self.w, self.value, self.bufs, self.send, self.recv = place, value, bufs, send, recv

    def copies(self, hop):
        w = self.w
        for k in range(1, self.HOPS[hop]):
            device = ((w.g ^ k, w.p), (w.g, w.p ^ k), (w.g, w.p ^ (2 * k)))[hop]
            ref = self.bufs.at[4 * hop]
            yield remote(ref, self.bufs.at[4 * hop + k], self.send.at[hop, k], self.recv.at[hop, k], device)

    def stage(self, number):
        w = self.w
        if number > 0:
            hop = number - 1
            for copy in self.copies(hop):
                copy.wait()
            mine = (w.g, w.y, w.z)[hop]
            total = self.bufs[4 * hop + mine]
            for k in range(1, self.HOPS[hop]):
                total = total + self.bufs[4 * hop + (mine ^ k)]
        else:
            total = self.value[...]
        if number == 3:
            self.value[...] = total
        else:
            self.bufs[4 * number] = total
            for copy in self.copies(number):
                copy.start()


def mask_column(side_ref, image):
    side = side_of(side_ref, image)
    slot = lax.broadcasted_iota(jnp.int32, (SLOT, 1), 0)
    return jnp.where(slot < side * side, 0.0, MASK_FILL).astype(F32)


def head_pair(images, step):
    i, j = step % images, step // images
    rows = pl.ds(pl.multiple_of(i * SLOT, SLOT), SLOT)
    return i, rows, pl.multiple_of(j * 128, 128), pl.multiple_of((j // 2) * D + (j % 2) * 128, 128)


def attend_step(images, step, side_ref, qkv_ref, ctx_ref, lse_ref):
    i, rows, c, at = head_pair(images, step)
    q = qkv_ref[rows, pl.ds(at, 128)]
    k = qkv_ref[rows, pl.ds(at + THIRD, 128)]
    v = qkv_ref[rows, pl.ds(at + 2 * THIRD, 128)]
    lane = lax.broadcasted_iota(jnp.int32, (1, 128), 1)
    mask = mask_column(side_ref, i)
    outs, logs = [], []
    for h in range(2):
        qm = jnp.where(lane // HD == h, q, jnp.zeros_like(q))
        s = dot(k, qm, NT) * (LOG2E / math.sqrt(HD)) + mask
        top = jnp.max(s, axis=0, keepdims=True)
        e = jnp.exp2(s - top)
        total = jnp.sum(e, axis=0, keepdims=True)
        p = (e * (1.0 / total)).astype(BF)
        outs.append(dot(p, v, TN))
        logs.append(top + jnp.log2(total))
    ctx_ref[rows, pl.ds(c, 128)] = jnp.where(lane < HD, outs[0], outs[1]).astype(BF)
    lse_ref[step] = jnp.concatenate(logs + [jnp.zeros((6, SLOT), F32)], axis=0)


def norm_rows(images, x_ref, small, norm_ref):
    def body(step, _):
        rows = pl.ds(pl.multiple_of(step * 192, 192), 192)
        unit, _ = norm_stats(x_ref[rows])
        norm_ref[rows] = (unit * small[R_G1 : R_G1 + 1] + small[R_S1 : R_S1 + 1]).astype(BF)
        return 0

    lax.fori_loop(0, images * SLOT // 192, body, 0)


def angle_tables(images, side_ref, small, cos_ref, sin_ref):
    for j in range(D // 128):
        flat = [small[R_FR : R_FR + 1, n + j // 2 * 128 : n + j // 2 * 128 + 128] for n in (0, D // 2)]
        fc, fr = [dot(jnp.broadcast_to(v, (8, 128)).astype(BF), spread(j % 2), NN)[0:1] for v in flat]

        def body(i, _):
            rows = pl.ds(pl.multiple_of(i * SLOT, SLOT), SLOT)
            col, row, _ = patch_columns(side_ref, i)
            sn, cs = sincos(col * fc + row * fr)
            cos_ref[rows, pl.ds(j * 128, 128)] = cs
            sin_ref[rows, pl.ds(j * 128, 128)] = sn * -half_sign(128)
            return 0

        lax.fori_loop(0, images, body, 0)


def project_block(images, c, r, small, w_ref, norm_ref, qkv_ref, cos_ref, sin_ref):
    i, part = r % images, r // images
    rows = pl.ds(pl.multiple_of(i * SLOT, SLOT), SLOT)
    cols = pl.ds(pl.multiple_of(part * THIRD, THIRD), THIRD)
    lanes = pl.ds(pl.multiple_of(c * D + part * THIRD, THIRD), THIRD)
    inner = pl.ds(pl.multiple_of(c * THIRD, THIRD), THIRD)
    raw = dot(norm_ref[rows], w_ref[c, :, cols], NN) + small[pl.ds(R_QB + part, 1), inner]

    @pl.when(part < 2)
    def _():
        turned = raw * cos_ref[rows, inner] + swap_halves(raw) * sin_ref[rows, inner]
        qkv_ref[rows, lanes] = turned.astype(BF)

    @pl.when(part == 2)
    def _():
        qkv_ref[rows, lanes] = raw.astype(BF)


def forward_compute(images, side_ref, x_ref, small, w_ref, qkv, norm, cos, sin, ctx_ref, lse_ref, hooks):
    hooks("start")
    norm_rows(images, x_ref, small, norm)
    hooks("tables")
    angle_tables(images, side_ref, small, cos, sin)
    blocks, pairs = 3 * images, 2 * images

    def body(step, _):
        hooks("step", step)
        c, r = step // (blocks + pairs), step % (blocks + pairs)

        @pl.when(r < blocks)
        def _():
            project_block(images, c, r, small, w_ref, norm, qkv, cos, sin)

        @pl.when(r >= blocks)
        def _():
            attend_step(images, c * pairs + r - blocks, side_ref, qkv, ctx_ref, lse_ref)

        return 0

    lax.fori_loop(0, 3 * (blocks + pairs), body, 0)
    hooks("end")


def forward_plain(images, side_ref, x_ref, small_ref, w_ref, *refs):
    qkv, norm, cos, sin, ctx, lse = refs
    forward_compute(images, side_ref, x_ref, small_ref, w_ref, qkv, norm, cos, sin, ctx, lse, lambda *a: None)


def packed_places(p, dp, sizes):
    run = D // dp
    for first, size in zip(SMALL_ROWS, sizes):
        count = size // run
        yield [(first + (p * count + m) // dp, ((p * count + m) % dp) * run) for m in range(count)]


SMALL_ROWS = (R_G1, R_S1, R_QB, R_FR, R_OB, R_G2, R_S2, R_UB, R_DB)


SINGLES = (R_G1, R_S1, R_FR, R_OB, R_G2, R_S2, R_DB)
MORE = ((2, R_QB, 3, 8), (7, R_UB, 4, 11))


def compact(tinies, ref):
    run = tinies[0].shape[1]
    first = {row: i for i, row in enumerate(SMALL_ROWS)}
    for n, row in enumerate(SINGLES):
        ref[n : n + 1, :run] = tinies[first[row]][...].astype(BF).astype(F32)
    for index, _, count, at in MORE:
        for m in range(count):
            ref[at + m : at + m + 1, :run] = tinies[index][:, m * run : (m + 1) * run].astype(BF).astype(F32)


def expand(parts, small, run):
    small[...] = jnp.zeros_like(small)
    lane = lax.broadcasted_iota(jnp.int32, (1, 128), 1)
    total = None
    for owner, ref in parts:
        wide = jnp.concatenate([jnp.where(lane < run, ref[...], 0.0), jnp.zeros((R_ALL, D - 128), F32)], axis=1)
        term = pltpu.roll(wide[0:8], owner * run, 1)
        total = term if total is None else total + term
        for _, row, count, at in MORE:
            for m in range(count):
                place = owner * count + m
                moved = pltpu.roll(jnp.broadcast_to(wide[at + m : at + m + 1], (8, D)), (place % 8) * run, 1)
                small[pl.ds(row + place // 8, 1), :] += moved[0:1]
    for n, row in enumerate(SINGLES):
        small[row : row + 1] = total[n : n + 1]


def forward_gather(images, side_ref, *refs):
    tinies, x_in, shards_in = refs[0:9], refs[9], refs[10:14]
    qkv_out, norm_out, cos_out, sin_out, ctx, lse, small, wq_out, wo, wu, wd, up_later, down_later = refs[14:27]
    x_ref, qkv, norm, cos, sin, wq, slots, bq, bo, bu, bd, sq, so, su, sd = refs[27:42]
    sems, recv, psend, precv, local, ins = refs[42:]
    w = Place()
    pairs = [(bq.at[c], wq.at[c]) for c in range(3)] + [(bo, wo)]
    pairs += [(own.at[c], full.at[c]) for c in range(PARTS - 1) for own, full in ((bu, wu), (bd, wd))]
    gathers = dict(zip(("q0", "q1", "q2", "o", "u0", "d0", "u1", "d1"), pairs))
    gathers = {k: Gather(w, *v, sems, recv, i) for i, (k, v) in enumerate(gathers.items())}
    moves = Moves(gathers, FORWARD_PLAN)
    peers = [w.p ^ k for k in range(1, 8)]
    keep = {}

    def store(name, src, dst):
        keep[name] = load(src, dst, local.at[len(keep)])

    def qkv_third(c):
        lanes = pl.ds(c * D, D)
        return pltpu.make_async_copy(qkv.at[:, lanes], qkv_out.at[:, lanes], local.at[16 + c])

    def late(number):
        src, dst = ((cos, cos_out), (sin, sin_out), (wq, wq_out))[number]
        return pltpu.make_async_copy(src, dst, local.at[19 + number])

    def own_rows(full):
        count = full.shape[0] // 8
        return full.at[pl.ds(pl.multiple_of(w.p * count, 16), count)]

    def pack_copy(k):
        return remote(slots.at[0], slots.at[k], psend.at[k - 1], precv.at[k - 1], (w.g, peers[k - 1]))

    def hooks(where, step=None):
        if where == "start":
            reads = [
                load(src, dst, ins.at[i])
                for i, (src, dst) in enumerate(zip(shards_in[:1] + (x_in,) + shards_in[1:], (sq, x_ref, so, su, sd)))
            ]
            compact(tinies, slots.at[0])
            greet([(w.g, q) for q in peers] + [w.sibling(), w.across()])
            for k in range(1, 8):
                pack_copy(k).start()
            reads[0].wait()
            for c in range(3):
                for part in range(3):
                    cols = part * D + c * THIRD
                    bq[c, :, part * THIRD : (part + 1) * THIRD] = sq[:, cols : cols + THIRD].astype(BF)
                if c == 0:
                    moves.at(-1)
            for copy in reads[1:]:
                copy.wait()
            bo[...] = so[...].astype(BF)
            for c in range(PARTS):
                for b in range(8):
                    cols = (b * PARTS + c) * 128
                    bu[c, :, b * 128 : (b + 1) * 128] = su[:, cols : cols + 128].astype(BF)
                bd[c] = sd[c * 128 : (c + 1) * 128].astype(BF)
            for i, (own, full) in enumerate(pairs):
                store(i, own, own_rows(full))
            store("up", bu.at[PARTS - 1], up_later)
            store("down", bd.at[PARTS - 1], down_later)
            for k in range(1, 8):
                pack_copy(k).wait()
            expand([(w.p, slots.at[0])] + [(peers[k - 1], slots.at[k]) for k in range(1, 8)], small, D // 8)
            moves.at(0)
        elif where == "tables":
            moves.at(1)
            store("norm", norm, norm_out)
        elif where == "step":

            @pl.when(step == 0)
            def _():
                for i in range(3):
                    keep[i].wait()
                for number in (0, 1):
                    late(number).start()

            moves.within(step + 2, 2, 31)
            for c in (1, 2):

                @pl.when(step == 10 * c)
                def _(c=c):
                    qkv_third(c - 1).start()
                    if c == 2:
                        late(2).start()

        else:
            qkv_third(2).start()
            moves.at(32)
            for c in range(3):
                qkv_third(c).wait()
                late(c).wait()
            for name, copy in keep.items():
                if name not in (0, 1, 2):
                    copy.wait()

    forward_compute(images, side_ref, x_ref, small, wq, qkv, norm, cos, sin, ctx, lse, hooks)


FORWARD_PLAN = {
    "q0": (-1, 1, 2, 2, 2),
    "q1": (0, 2, 9, 11, 12),
    "q2": (1, 4, 10, 16, 19),
    "o": (1, 7, 14, 29, 31),
    "u0": (3, 11, 17, 25, 26),
    "d0": (5, 16, 21, 27, 31),
    "u1": (17, 21, 28, 31, 32),
    "d1": (10, 16, 24, 30, 31),
}


def bias_at(split, step):
    c, k = step // BLOCKS, step % BLOCKS
    if split:
        return (R_UB + k, c * 128), (R_UB + k, D // 2 + c * 128)
    return (R_UB + step // 3, (step % 3) * 256), (R_UB + step // 3, (step % 3) * 256 + 128)


def mlp_compute(images, split, side_ref, scale, cot_ref, ctx_ref, small, wo_ref, wu, wd, refs, outs, hooks):
    mid, n2, n2t, bl, hid, gpre, ubias, gubias = refs
    act, gm, gctx, gdown, gup, gout, gs = outs
    rows_all = images * SLOT
    tile = SLOT // 2
    hooks("start")
    gain = small[R_G2 : R_G2 + 1]
    gs[...] = jnp.zeros_like(gs)
    for step in range(PARTS * BLOCKS):
        for n, (r, l) in enumerate(bias_at(split, step)):
            ubias[step : step + 1, n * 128 : (n + 1) * 128] = small[r : r + 1, l : l + 128]

    def tile_rows(step):
        side = side_of(side_ref, step // 2)
        slot = lax.broadcasted_iota(jnp.int32, (tile, 1), 0) + (step % 2) * tile
        return pl.ds(pl.multiple_of(step * tile, tile), tile), slot < side * side

    def enter(step, _):
        rows, valid = tile_rows(step)
        middle = mid[rows] + (dot(ctx_ref[rows], wo_ref[...], NN) + small[R_OB : R_OB + 1])
        mid[rows] = middle
        act[rows] = middle + small[R_DB : R_DB + 1]
        unit, _ = norm_stats(middle)
        n2[rows] = (unit * gain + small[R_S2 : R_S2 + 1]).astype(BF)
        low = jnp.where(valid, cot_ref[rows], 0.0).astype(BF)
        bl[rows] = low
        gs[R_DB : R_DB + 1] += jnp.sum(low.astype(F32), axis=0, keepdims=True)
        return 0

    lax.fori_loop(0, 2 * images, enter, 0)
    gm[...] = jnp.zeros_like(gm)
    n2t[...] = n2[...].T
    hooks("entered")

    def block(step, _):
        hooks("block", step)
        c, k = step // BLOCKS, step % BLOCKS
        cols = pl.ds(pl.multiple_of(k * 256, 256), 256)
        bias = ubias[pl.ds(step, 1), :]
        wuc = wu[c, :, cols]
        wdc = wd[c, cols, :]
        bsum = None
        for i in range(images):
            rows = pl.ds(i * SLOT, SLOT)
            pre = dot(n2[rows], wuc, NN) + bias
            back = dot(bl[rows], wdc, NT)
            value, slope = gelu_pair(pre)
            hid[rows, cols] = value.astype(BF)
            g = (back * slope).astype(BF)
            gpre[rows, cols] = g
            part = jnp.sum(g.astype(F32), axis=0, keepdims=True)
            bsum = part if bsum is None else bsum + part
        gubias[pl.ds(step, 1), :] = bsum
        gdown[c, cols, :] = (dot(hid[:, cols], bl[...], TN) * scale).astype(BF)
        gup[c, :, cols] = (dot(n2t[...], gpre[:, cols], NN) * scale).astype(BF)

        @pl.when(k == BLOCKS - 1)
        def _():
            def tail(n, _):
                rows = pl.ds(pl.multiple_of(n * tile, tile), tile)
                act[rows] += dot(hid[rows], wd[c], NN)
                gm[rows] += dot(gpre[rows], wu[c], NT)
                return 0

            lax.fori_loop(0, 2 * images, tail, 0)

        return 0

    lax.fori_loop(0, PARTS * BLOCKS, block, 0)
    hooks("blocks")

    def leave(step, _):
        rows, valid = tile_rows(step)
        unit, inv = norm_stats(mid[rows])
        act[rows] = jnp.where(valid, act[rows], 0.0)
        gn = gm[rows]
        gs[R_G2 : R_G2 + 1] += jnp.sum(gn * unit, axis=0, keepdims=True)
        gs[R_S2 : R_S2 + 1] += jnp.sum(gn, axis=0, keepdims=True)
        a = gn * gain
        ma = jnp.mean(a, axis=-1, keepdims=True)
        mu = jnp.mean(a * unit, axis=-1, keepdims=True)
        g = jnp.where(valid, cot_ref[rows], 0.0) + inv * (a - ma - unit * mu)
        gm[rows] = g
        low = g.astype(BF)
        bl[rows] = low
        gs[R_OB : R_OB + 1] += jnp.sum(low.astype(F32), axis=0, keepdims=True)
        gctx[rows] = dot(low, wo_ref[...], NT).astype(BF)
        return 0

    lax.fori_loop(0, 2 * images, leave, 0)
    for step in range(PARTS * BLOCKS):
        for n, (r, l) in enumerate(bias_at(split, step)):
            gs[r : r + 1, l : l + 128] = gubias[step : step + 1, n * 128 : (n + 1) * 128]
    gout[...] = (dot(ctx_ref[...], bl[...], TN) * scale).astype(BF)
    gs[...] = gs[...] * scale
    hooks("end")


def mlp_scratch(rows):
    vmem = pltpu.VMEM
    return (
        [vmem((rows, D), F32), vmem((rows, D), BF), vmem((D, rows), BF), vmem((rows, D), BF)]
        + [vmem((rows, FF // PARTS), BF)] * 2
        + [vmem((16, 256), F32)] * 2
    )


def mlp_plain(images, slots, side_ref, assign_ref, counts_ref, x_ref, cot_ref, ctx_ref, small, wo_ref, wu, wd, *rest):
    outs, refs, sem = rest[0:7], rest[7:15], rest[15]
    load(x_ref, refs[0], sem.at[0]).wait()
    mlp_compute(
        images, False, side_ref, device_weight(slots, assign_ref, counts_ref), cot_ref, ctx_ref, small, wo_ref, wu, wd, refs, outs, lambda *a: None
    )


def mlp_moving(images, slots, side_ref, assign_ref, counts_ref, small, *rest):
    x_in, cot_in, ctx_in, wo_in, wu_in, wd_in, up_later, down_later = rest[0:8]
    act_out, gm_out, gctx_out, gd_out, gu_out, go_out, gs, rd, ru = rest[8:17]
    refs = rest[17:25]
    mid, n2, n2t = refs[0], refs[1], refs[2]
    cot, ctx, wo, wu, wd, act, gm, gd, gu = rest[25:34]
    bufs, (local, sems, recv, rlocal, rsend, rrecv) = rest[34:46], rest[46:52]
    w = Place()
    last = PARTS - 1
    items = {
        "u": Gather(w, up_later, wu.at[last], sems, recv, 0),
        "d": Gather(w, down_later, wd.at[last], sems, recv, 1),
        "rd": Reduce(w, gd.at[0], bufs[0:6], rd, rlocal.at[0], rsend.at[0], rrecv.at[0]),
        "ru": Reduce(w, gu.at[0], bufs[6:12], ru, rlocal.at[1], rsend.at[1], rrecv.at[1]),
    }
    moves = Moves(items, MLP_PLAN)
    keep = []

    def move(src, dst):
        keep.append(load(src, dst, local.at[len(keep)]))
        return keep[-1]

    def hooks(where, step=None):
        if where == "start":
            move(ctx_in, ctx), move(x_in, mid), move(wo_in, wo), move(cot_in, cot)
            for c in range(last):
                move(wu_in.at[c], wu.at[c])
                move(wd_in.at[c], wd.at[c])
            for own, full in ((up_later, wu), (down_later, wd)):
                count = full.shape[1] // 8
                move(own, full.at[last, pl.ds(pl.multiple_of(w.p * count, 16), count)])
            greet(w.partners())
            moves.at(0)
            for copy in keep[:4]:
                copy.wait()
        elif where == "entered":
            for copy in keep[4:]:
                copy.wait()
            keep.clear()
        elif where == "block":
            moves.within(step + 1, 1, 12)
        elif where == "blocks":
            for c in (1, 2):
                move(gd.at[c], gd_out.at[c - 1])
                move(gu.at[c], gu_out.at[c - 1])
            moves.at(13)
        else:
            move(act, act_out)
            move(gm, gm_out)
            move(n2, gctx_out)
            move(n2t.at[:, pl.ds(0, D)], go_out)
            moves.at(14)
            for copy in keep:
                copy.wait()

    mlp_compute(
        images,
        True,
        side_ref,
        device_weight(slots, assign_ref, counts_ref),
        cot,
        ctx,
        small,
        wo,
        wu,
        wd,
        refs,
        (act, gm, n2, gd, gu, n2t.at[:, pl.ds(0, D)], gs),
        hooks,
    )


MLP_PLAN = {
    "u": (1, 4, 7, 9, 9),
    "d": (0, 1, 4, 6, 8),
    "rd": (5, 6, 8, 9, 11, 13, 14),
    "ru": (6, 8, 10, 12, 13, 14, 14),
}


PARTS = 3
BLOCKS = 4


def attend_back_step(images, step, side_ref, qkv_ref, gctx_ref, lse_ref, cos_ref, sin_ref, gproj_ref, gs_ref, gf_ref):
    i, rows, c, at = head_pair(images, step)
    q = qkv_ref[rows, pl.ds(at, 128)]
    k = qkv_ref[rows, pl.ds(at + THIRD, 128)]
    v = qkv_ref[rows, pl.ds(at + 2 * THIRD, 128)]
    go = gctx_ref[rows, pl.ds(c, 128)]
    lane = lax.broadcasted_iota(jnp.int32, (1, 128), 1)
    mask = mask_column(side_ref, i)
    lse = lse_ref[step]
    dq, dk, dv = [], [], []
    for h in range(2):
        mine = lane // HD == h
        qm = jnp.where(mine, q, jnp.zeros_like(q))
        gom = jnp.where(mine, go, jnp.zeros_like(go))
        s = dot(k, qm, NT) * (LOG2E / math.sqrt(HD)) + mask
        p = jnp.exp2(s - lse[h : h + 1])
        dp = dot(v, gom, NT)
        dv.append(dot(p.astype(BF), go, NN))
        t = p * dp
        ds = (t - p * jnp.sum(t, axis=0, keepdims=True)).astype(BF)
        dk.append(dot(ds, q, NN))
        dq.append(dot(ds, k, TN))
    first = lane < HD
    cs = cos_ref[rows, pl.ds(c, 128)]
    sn = sin_ref[rows, pl.ds(c, 128)]
    angle = None
    for n, (pair, rot) in enumerate(((dq, q), (dk, k))):
        e = jnp.where(first, pair[0], pair[1]) * (1.0 / math.sqrt(HD))
        other = swap_halves(e)
        back = (e * cs - other * sn).astype(BF)
        gproj_ref[rows, pl.ds(at + n * THIRD, 128)] = back
        gs_ref[pl.ds(R_QB + n, 1), pl.ds(c, 128)] += jnp.sum(back.astype(F32), axis=0, keepdims=True)
        term = rot.astype(F32) * other
        angle = term if angle is None else angle + term
    gv = jnp.where(first, dv[0], dv[1]).astype(BF)
    gproj_ref[rows, pl.ds(at + 2 * THIRD, 128)] = gv
    gs_ref[R_QB + 2 : R_QB + 3, pl.ds(c, 128)] += jnp.sum(gv.astype(F32), axis=0, keepdims=True)
    angle = angle * half_sign(128)
    col, row, _ = patch_columns(side_ref, i)
    gf_ref[0:1, pl.ds(c, 128)] += jnp.sum(angle * col, axis=0, keepdims=True)
    gf_ref[1:2, pl.ds(c, 128)] += jnp.sum(angle * row, axis=0, keepdims=True)


def freq_row(gf_ref, gs_ref):
    for m in range(D // 128):
        which = m // 3
        total = None
        for parity in (0, 1):
            lanes = 2 * (m % 3) + parity
            value = gf_ref[which : which + 1, lanes * 128 : lanes * 128 + 128]
            for _ in range(3):
                term = value.astype(BF)
                value = value - term.astype(F32)
                moved = dot(jnp.broadcast_to(term, (8, 128)), spread(parity), NT)[0:1]
                total = moved if total is None else total + moved
        gs_ref[R_FR : R_FR + 1, m * 128 : m * 128 + 128] = total


def weight_third(c, scale, norm_ref, gproj_ref, gw_ref):
    def block(j, _):
        lanes = pl.ds(pl.multiple_of(j * THIRD, THIRD), THIRD)
        full = pl.ds(pl.multiple_of(c * D + j * THIRD, THIRD), THIRD)
        gw_ref[:, lanes] = (dot(norm_ref[...], gproj_ref[:, full], TN) * scale).astype(BF)
        return 0

    lax.fori_loop(0, 3, block, 0)


def attend_back_compute(images, thirds, side_ref, scale, ins, norm, gproj, gws, gs_ref, gf_ref, hooks):
    hooks("start")
    gs_ref[...] = jnp.zeros_like(gs_ref)
    gf_ref[...] = jnp.zeros_like(gf_ref)

    def body(step, _):
        hooks("step", step)
        attend_back_step(images, step, side_ref, *ins, gproj, gs_ref, gf_ref)
        for c in range(thirds):

            @pl.when(step == 2 * images * (c + 1) - 1)
            def _(c=c):
                weight_third(c, scale, norm, gproj, gws.at[c])

        return 0

    lax.fori_loop(0, images * HEADS // 2, body, 0)
    freq_row(gf_ref, gs_ref)
    hooks("end")


def attend_back_plain(images, slots, side_ref, assign_ref, counts_ref, *refs):
    ins, norm, (gproj, gws, gs, gf) = refs[0:5], refs[5], refs[6:10]
    attend_back_compute(images, 3, side_ref, device_weight(slots, assign_ref, counts_ref), ins, norm, gproj, gws, gs, gf, lambda *a: None)


def attend_back_reduce(images, slots, side_ref, assign_ref, counts_ref, *refs):
    ins_in, norm_in, (gd, gu, go) = refs[0:5], refs[5], refs[6:9]
    gproj_out, gs, outs = refs[9], refs[10], refs[11:18]
    ins, norm, gproj, gws, gf = refs[18:23], refs[23], refs[24], refs[25], refs[26]
    bufs, (load_sems, local, send, recv) = refs[27:69], refs[69:73]
    w = Place()
    srcs = (gd.at[0], gu.at[0], gd.at[1], gu.at[1], go, gws.at[0], gws.at[1])
    items = {
        name: Reduce(w, srcs[i], bufs[6 * i : 6 * i + 6], outs[i], local.at[i], send.at[i], recv.at[i])
        for i, name in enumerate(BACK_PLAN)
    }
    moves = Moves(items, BACK_PLAN)

    def hooks(where, step=None):
        if where == "start":
            copies = [load(src, dst, load_sems.at[i]) for i, (src, dst) in enumerate(zip(ins_in + (norm_in,), ins + (norm,)))]
            greet(w.partners())
            moves.at(0)
            for copy in copies:
                copy.wait()
        elif where == "step":
            moves.within(step + 1, 1, 12)
        else:
            copy = load(gproj, gproj_out, load_sems.at[0])
            moves.at(13)
            moves.at(14)
            copy.wait()

    attend_back_compute(images, 2, side_ref, device_weight(slots, assign_ref, counts_ref), ins, norm, gproj, gws, gs, gf, hooks)


BACK_PLAN = {
    "d1": (3, 4, 7, 9, 11, 14, 14),
    "u1": (0, 2, 4, 8, 10, 13, 13),
    "d2": (1, 3, 5, 8, 10, 12, 12),
    "u2": (3, 7, 9, 10, 13, 14, 14),
    "o": (0, 3, 7, 9, 11, 12, 13),
    "q0": (5, 8, 10, 12, 13, 14, 14),
    "q1": (9, 9, 11, 12, 13, 14, 14),
}


def qkv_back_compute(images, x_ref, gproj_ref, gm_ref, small_ref, w_ref, gs_in, gin_ref, gs_ref, hooks):
    hooks("start")
    gain = small_ref[R_G1 : R_G1 + 1]
    gs_ref[...] = gs_in[...]
    tile = SLOT // 2

    def body(step, _):
        hooks("tile", step)
        rows = pl.ds(pl.multiple_of(step * tile, tile), tile)
        unit, inv = norm_stats(x_ref[rows])
        gn = None
        for c in range(3):
            term = dot(gproj_ref[rows, c * D : (c + 1) * D], w_ref[c], NT)
            gn = term if gn is None else gn + term
        gs_ref[R_G1 : R_G1 + 1] += jnp.sum(gn * unit, axis=0, keepdims=True)
        gs_ref[R_S1 : R_S1 + 1] += jnp.sum(gn, axis=0, keepdims=True)
        a = gn * gain
        ma = jnp.mean(a, axis=-1, keepdims=True)
        mu = jnp.mean(a * unit, axis=-1, keepdims=True)
        gin_ref[rows] = gm_ref[rows] + inv * (a - ma - unit * mu)
        return 0

    lax.fori_loop(0, 2 * images, body, 0)
    hooks("end")


def qkv_back_plain(images, slots, assign_ref, counts_ref, x_ref, gproj_ref, gm_ref, small_ref, w_ref, gs_in, gin, gs):
    def hooks(where, index=None):
        if where == "end":
            gs[...] = gs[...] * device_weight(slots, assign_ref, counts_ref)

    qkv_back_compute(images, x_ref, gproj_ref, gm_ref, small_ref, w_ref, gs_in, gin, gs, hooks)


def qkv_back_reduce(images, slots, assign_ref, counts_ref, small_ref, gs_att, gs_mlp, *refs):
    ins_in, (gin, gs, out) = refs[0:5], refs[5:8]
    norm, gproj, x, w_ref, gm = refs[8:13]
    gw, bufs, tinybufs, (load_sems, local, send, recv, ssend, srecv) = refs[13], refs[14:20], refs[20], refs[21:27]
    w = Place()
    last = Reduce(w, gw, bufs, out, local, send, recv)
    tiny = SmallSum(w, gs, tinybufs, ssend, srecv)
    weight = device_weight(slots, assign_ref, counts_ref)

    def hooks(where, index=None):
        if where == "start":
            copies = [load(src, dst, load_sems.at[i]) for i, (src, dst) in enumerate(zip(ins_in, refs[8:13]))]
            greet(w.partners() + [(w.g ^ 3, w.p)])
            copies[0].wait()
            copies[1].wait()
            weight_third(2, weight, norm, gproj, gw)
            last.stage(0)
            for copy in copies[2:]:
                copy.wait()
        elif where == "tile":
            for number, when in ((1, 1), (2, 3)):

                @pl.when(index == when)
                def _(number=number):
                    last.stage(number)

        else:
            gs[...] = gs[...] * weight + gs_mlp[...]
            tiny.stage(0)
            last.stage(3)
            tiny.stage(1)
            last.stage(4)
            tiny.stage(2)
            last.stage(5)
            tiny.stage(3)
            last.stage(6)

    qkv_back_compute(images, x, gproj, gm, small_ref, w_ref, gs_att, gin, gs, hooks)


def finish_kernel(dp, p_axis, gs, act_in, gin_in, rout_in, *refs):
    rd, ru, rq = refs[0:3], refs[3:6], refs[6:9]
    act, gin, rqkv, rout, rup, rdown, sems = refs[9], refs[10], *refs[11:15], refs[-1]
    tinies = refs[15:-2]
    stage = refs[-2]
    ins = [load(act_in, stage.at[0], sems.at[0]), load(gin_in, stage.at[1], sems.at[1])]
    p = lax.axis_index(p_axis)
    run = D // dp
    for out, places in zip(tinies, packed_places(p, dp, [t.shape[0] for t in tinies])):
        for m, (row, lane) in enumerate(places):
            whole = jnp.broadcast_to(gs[pl.ds(row, 1), :], (8, D))
            out[pl.ds(m * run, run)] = pltpu.roll(whole, D - lane, 1)[0, :run]
    copies = []
    for n, dst in enumerate((act, gin)):
        ins[n].wait()
        copies.append(load(stage.at[n], dst, sems.at[n]))
    rout[...] = rout_in[...]
    for c in range(3):
        rdown[c * rd[c].shape[0] : (c + 1) * rd[c].shape[0]] = rd[c][...]
        for b in range(dp):
            rup[:, (b * 3 + c) * 128 : (b * 3 + c + 1) * 128] = ru[c][:, b * 128 : (b + 1) * 128]
        for part in range(3):
            cols = part * D + c * THIRD
            rqkv[:, cols : cols + THIRD] = rq[c][:, part * THIRD : (part + 1) * THIRD]
    for copy in copies:
        copy.wait()


def params(mb=56):
    return pltpu.CompilerParams(vmem_limit_bytes=mb << 20)


def place_rows(p, dp, vec):
    n = vec.shape[0]
    whole = jnp.tile(vec, dp)
    owner = jnp.arange(n * dp, dtype=jnp.int32) // n
    return jnp.where(owner == p, whole, 0.0).reshape(-1, D)


def on_device(
    fast,
    images,
    cotangent,
    resolution,
    assignment,
    counts,
    ln1_gain,
    ln1_shift,
    qkv_weight,
    qkv_bias,
    rope_freqs,
    out_weight,
    out_bias,
    ln2_gain,
    ln2_shift,
    up_weight,
    up_bias,
    down_weight,
    down_bias,
):
    p = lax.axis_index("dp")
    dp = lax.axis_size("dp")
    n = images.shape[0]
    rows = n * SLOT
    x = images.reshape(rows, D)
    cot = cotangent.reshape(rows, D)
    vectors = (ln1_gain, ln1_shift, qkv_bias, rope_freqs, out_bias, ln2_gain, ln2_shift, up_bias, down_bias)
    slots = dp * rows
    sds = jax.ShapeDtypeStruct
    smem = pl.BlockSpec(memory_space=pltpu.SMEM)
    anyw = pl.BlockSpec(memory_space=pl.ANY)
    kept = [
        sds((rows, 3 * D), BF),
        sds((rows, D), BF),
        sds((rows, D), F32),
        sds((rows, D), F32),
        sds((rows, D), BF),
        sds((n * HEADS // 2, 8, SLOT), F32),
    ]
    weights = (qkv_weight, out_weight, up_weight, down_weight)
    dma = pltpu.SemaphoreType.DMA
    vmem = pltpu.VMEM

    def moving(number, mb):
        return pltpu.CompilerParams(vmem_limit_bytes=mb << 20, collective_id=number, has_side_effects=True)

    part = FF // PARTS
    if fast:
        later = [sds((D // dp, part), BF), sds((part // dp, D), BF)]
        fulls = [sds((3, D, D), BF), sds((D, D), BF), sds((PARTS - 1, D, part), BF), sds((PARTS - 1, part, D), BF)]
        outs = pl.pallas_call(
            functools.partial(forward_gather, n),
            out_shape=kept + [sds((R_ALL, D), F32)] + fulls + later,
            in_specs=[smem] + vm(9) + [anyw] * 5,
            out_specs=[anyw] * 4 + vm(3) + [anyw] * 6,
            scratch_shapes=[
                vmem((rows, D), F32),
                vmem((rows, 3 * D), BF),
                vmem((rows, D), BF),
                vmem((rows, D), F32),
                vmem((rows, D), F32),
                vmem((3, D, D), BF),
                vmem((8, R_ALL, 128), F32),
                vmem((3, D // dp, D), BF),
                vmem((D // dp, D), BF),
                vmem((PARTS, D // dp, part), BF),
                vmem((PARTS, part // dp, D), BF),
            ]
            + [vmem(v.shape, F32) for v in weights]
            + [
                dma((16,)),
                dma((8, 16)),
                dma((7,)),
                dma((7,)),
                dma((22,)),
                dma((5,)),
            ],
            compiler_params=moving(0, 56),
            name="forward",
        )(resolution, *[v.reshape(1, -1) for v in vectors], x, *weights)
        qkv, norm1, cos, sin, ctx, lse, small, wqkv, wo, wu, wd, up_later, down_later = outs
    else:
        packed = [place_rows(p, dp, lax.reduce_precision(v, 8, 7)) for v in vectors]
        small = lax.psum(jnp.concatenate(packed + [jnp.zeros((2, D), F32)], axis=0), "dp")
        wqkv, wo, wu, wd = [lax.all_gather(v.astype(BF), "dp", axis=0, tiled=True) for v in weights]
        wqkv = wqkv.reshape(D, 3, 3, THIRD).transpose(2, 0, 1, 3).reshape(3, D, D)
        wu = wu.reshape(D, PARTS, part).transpose(1, 0, 2)
        wd = wd.reshape(PARTS, part, D)
        qkv, norm1, cos, sin, ctx, lse = pl.pallas_call(
            functools.partial(forward_plain, n),
            out_shape=kept,
            in_specs=[smem] + vm(3),
            out_specs=vm(6),
            compiler_params=params(),
            name="forward",
        )(resolution, x, small, wqkv)

    grads = [sds((PARTS, part, D), BF), sds((PARTS, D, part), BF), sds((D, D), BF)]
    rest = [sds((R_ALL, D), F32)]
    firsts = [sds((rows, D), F32), sds((rows, D), F32), sds((rows, D), BF)]
    tables = [vmem((rows, 3 * D), BF), vmem((rows, D), BF), vmem((n * HEADS // 2, 8, SLOT), F32)]
    tables += [vmem((rows, D), F32)] * 2
    gproj_shape = sds((rows, 3 * D), BF)
    if fast:
        sizes = [(part // dp, D), (D // dp, part)]
        act, gm, gctx, gdown, gup, gout, gs_mlp, rdown0, rup0 = pl.pallas_call(
            functools.partial(mlp_moving, n, slots),
            out_shape=firsts
            + [sds((PARTS - 1,) + g.shape[1:], BF) for g in grads[:2]]
            + grads[2:]
            + rest
            + [sds(z, F32) for z in sizes],
            in_specs=[smem] * 3 + vm(1) + [anyw] * 8,
            out_specs=[anyw] * 6 + vm(3),
            scratch_shapes=mlp_scratch(rows)
            + [
                vmem((rows, D), F32),
                vmem((rows, D), BF),
                vmem((D, D), BF),
                vmem((PARTS, D, part), BF),
                vmem((PARTS, part, D), BF),
                vmem((rows, D), F32),
                vmem((rows, D), F32),
                vmem((PARTS, part, D), BF),
                vmem((PARTS, D, part), BF),
            ]
            + sum([Reduce.buffers(*z) for z in sizes], [])
            + [dma((12,)), dma((4,)), dma((2, 16)), dma((2,)), dma((2,)), dma((2, 6))],
            compiler_params=moving(3, 63),
            name="mlp",
        )(resolution, assignment, counts, small, x, cot, ctx, wo, wu, wd, up_later, down_later)
        third = (D // dp, D)
        sizes = sizes + sizes + [third] * 3
        gproj, gs_att, rdown1, rup1, rdown2, rup2, rout, rq0, rq1 = pl.pallas_call(
            functools.partial(attend_back_reduce, n, slots),
            out_shape=[gproj_shape] + rest + [sds(z, F32) for z in sizes],
            in_specs=[smem] * 3 + [anyw] * 9,
            out_specs=[anyw] + vm(8),
            scratch_shapes=tables
            + [vmem((rows, D), BF), vmem((rows, 3 * D), BF), vmem((2, D, D), BF), vmem((8, D), F32)]
            + sum([Reduce.buffers(*z) for z in sizes], [])
            + [dma((6,)), dma((7,)), dma((7,)), dma((7, 6))],
            compiler_params=moving(1, 62),
            name="attend_back",
        )(resolution, assignment, counts, qkv, gctx, lse, cos, sin, norm1, gdown, gup, gout)
        gin, gs, rq2 = pl.pallas_call(
            functools.partial(qkv_back_reduce, n, slots),
            out_shape=[sds((rows, D), F32)] + rest + [sds(third, F32)],
            in_specs=[smem] * 2 + vm(3) + [anyw] * 5,
            out_specs=vm(3),
            scratch_shapes=[
                vmem((rows, D), BF),
                vmem((rows, 3 * D), BF),
                vmem((rows, D), F32),
                vmem((3, D, D), BF),
                vmem((rows, D), F32),
                vmem((D, D), BF),
            ]
            + Reduce.buffers(*third)
            + [vmem((12, R_ALL, D), F32), dma((5,)), dma, dma, dma((6,)), dma((3, 4)), dma((3, 4))],
            compiler_params=moving(2, 60),
            name="project_back",
        )(assignment, counts, small, gs_att, gs_mlp, norm1, gproj, x, wqkv, gm)

        matrices = (qkv_weight, out_weight, up_weight, down_weight)
        act, gin, rqkv, rout, rup, rdown, *tinies = pl.pallas_call(
            functools.partial(finish_kernel, dp, "dp"),
            out_shape=[sds((rows, D), F32)] * 2 + [sds(v.shape, F32) for v in matrices + vectors],
            in_specs=vm(1) + [anyw] * 2 + vm(10),
            out_specs=[anyw] * 2 + vm(13),
            scratch_shapes=[vmem((2, rows, D), F32), dma((2,))],
            compiler_params=params(),
            name="finish",
        )(gs, act, gin, rout, rdown0, rdown1, rdown2, rup0, rup1, rup2, rq0, rq1, rq2)
    else:
        act, gm, gctx, gdown, gup, gout, gs_mlp = pl.pallas_call(
            functools.partial(mlp_plain, n, slots),
            out_shape=firsts + grads + rest,
            in_specs=[smem] * 3 + [anyw] + vm(6),
            out_specs=vm(7),
            scratch_shapes=mlp_scratch(rows) + [dma((1,))],
            compiler_params=params(63),
            name="mlp",
        )(resolution, assignment, counts, x, cot, ctx, small, wo, wu, wd)
        gproj, gqkv, gs_att = pl.pallas_call(
            functools.partial(attend_back_plain, n, slots),
            out_shape=[gproj_shape, sds((3, D, D), BF)] + rest,
            in_specs=[smem] * 3 + vm(6),
            out_specs=vm(3),
            scratch_shapes=[vmem((8, D), F32)],
            compiler_params=params(),
            name="attend_back",
        )(resolution, assignment, counts, qkv, gctx, lse, cos, sin, norm1)
        gin, gs_qkv = pl.pallas_call(
            functools.partial(qkv_back_plain, n, slots),
            out_shape=[sds((rows, D), F32)] + rest,
            in_specs=[smem] * 2 + vm(6),
            out_specs=vm(2),
            compiler_params=params(),
            name="project_back",
        )(assignment, counts, x, gproj, gm, small, wqkv, gs_att)

        def reduce(g):
            total = lax.psum_scatter(g, "dp", scatter_dimension=0, tiled=True)
            return lax.psum(total, "group").astype(F32)

        gqkv = gqkv.reshape(3, D, 3, THIRD).transpose(1, 2, 0, 3).reshape(D, 3 * D)
        gup = gup.transpose(1, 0, 2).reshape(D, FF)
        rqkv, rout, rup, rdown = [reduce(g) for g in (gqkv, gout, gup, gdown.reshape(FF, D))]
        gs = lax.psum(gs_mlp + gs_qkv, ("group", "dp"))

        def own(first, count):
            flat = gs[first : first + count].reshape(dp, -1)
            return lax.dynamic_index_in_dim(flat, p, 0, keepdims=False)

        tinies = [own(first, v.shape[0] * dp // D) for first, v in zip(SMALL_ROWS, vectors)]

    g1, s1, qb, fr, ob, g2, s2, ub, db = tinies
    act, gin = act.reshape(images.shape), gin.reshape(images.shape)
    return (act, gin, g1, s1, rqkv, qb, fr, rout, ob, g2, s2, rup, ub, rdown, db)


def solution(mesh):
    batch = P(("group", "dp"), None, None)
    per_image = P(("group", "dp"))
    vec, mat = P("dp"), P("dp", None)
    fast = dict(mesh.shape) == {"group": 4, "dp": 8}
    return jax.shard_map(
        functools.partial(on_device, fast),
        mesh=mesh,
        in_specs=(batch, batch, per_image, per_image, P(), vec, vec, mat, vec, vec, mat, vec, vec, vec, mat, vec, mat, vec),
        out_specs=(batch, batch, vec, vec, mat, vec, vec, mat, vec, vec, vec, mat, vec, mat, vec),
        check_vma=False,
    )
```

```python
import functools
import math

import jax
import jax.numpy as jnp
from jax import lax
from jax.experimental import pallas as pl
from jax.experimental.pallas import tpu as pltpu
from jax.sharding import PartitionSpec as P

HEADS = 12
HD = 64
SIDE_S = 14
SIDE_M = 20
SIDE_L = 24
SLOT = 576
D = 768
FF = 3072
LN_EPS = 1e-06
MASK_FILL = -1e30
BF = jnp.bfloat16
F32 = jnp.float32
NT = (((1,), (1,)), ((), ()))
NN = (((1,), (0,)), ((), ()))
TN = (((0,), (0,)), ((), ()))
R_G1, R_S1, R_QB, R_FR, R_OB, R_G2, R_S2, R_UB, R_DB, R_ALL = 0, 1, 2, 5, 6, 7, 8, 9, 13, 16
THIRD = 256
LOG2E = math.log2(math.e)


def dot(a, b, dims, precision=None):
    return lax.dot_general(a, b, dims, preferred_element_type=F32, precision=precision)


def vm(n):
    return [pl.BlockSpec(memory_space=pltpu.VMEM)] * n


def norm_stats(x):
    mean = jnp.mean(x, axis=-1, keepdims=True)
    cen = x - mean
    var = jnp.mean(cen * cen, axis=-1, keepdims=True)
    inv = lax.rsqrt(var + LN_EPS)
    return cen * inv, inv


def sincos(x):
    n = jnp.floor(x * (2.0 / math.pi) + 0.5)
    r = x - n * 1.5703125
    r = r - n * 4.837512969970703125e-4
    r = r - n * 7.54978995489188216e-8
    q = n.astype(jnp.int32)
    r2 = r * r
    s = r + r * r2 * (-1.6666654611e-1 + r2 * (8.3321608736e-3 + r2 * -1.9515295891e-4))
    c = 1.0 - 0.5 * r2 + r2 * r2 * (
        4.166664568298827e-2 + r2 * (-1.388731625493765e-3 + r2 * 2.443315711809948e-5)
    )
    odd = (q & 1) == 1
    ss = jnp.where(odd, c, s)
    cc = jnp.where(odd, s, c)
    ss = jnp.where((q & 2) == 2, -ss, ss)
    cc = jnp.where(((q + 1) & 2) == 2, -cc, cc)
    return ss, cc


ERFC = (
    0.07314588129520416,
    -0.30809587240219116,
    0.3798876702785492,
    -0.08230462670326233,
    0.245080828666687,
    0.2054724544286728,
    0.24429383873939514,
    0.242519810795784,
)


def gelu_pair(x):
    z = jnp.abs(x)
    t = 1.0 / (1.0 + (0.43 * math.sqrt(0.5)) * z)
    poly = 0.5 * ERFC[0]
    for c in ERFC[1:]:
        poly = poly * t + 0.5 * c
    bell = jnp.exp2((x * x) * (-0.5 * LOG2E))
    half = poly * t * bell
    cdf = jnp.where(x < 0, half, 1.0 - half)
    return x * cdf, cdf + (x * math.sqrt(0.5 / math.pi)) * bell


def swap_halves(x):
    width = x.shape[-1]
    lane = lax.broadcasted_iota(jnp.int32, (1, width), 1)
    ahead = pltpu.roll(x, width - HD // 2, 1)
    behind = pltpu.roll(x, HD // 2, 1)
    return jnp.where(lane % HD < HD // 2, ahead, behind)


def half_sign(width):
    lane = lax.broadcasted_iota(jnp.int32, (1, width), 1)
    return jnp.where(lane % HD < HD // 2, 1.0, -1.0).astype(F32)


def side_of(res_ref, image):
    res = res_ref[image]
    return jnp.where(res == 0, SIDE_S, jnp.where(res == 1, SIDE_M, SIDE_L))


def device_weight(slots, assign_ref, counts_ref):
    groups = counts_ref.shape[0]
    counts = [jnp.full((1, 128), counts_ref[i], jnp.int32).astype(F32) for i in range(groups)]
    mine = jnp.full((1, 128), assign_ref[0], jnp.int32)
    picked = sum(jnp.where(mine == i, counts[i], 0.0) for i in range(groups))
    return (groups * picked / sum(counts) * (1.0 / math.sqrt(slots)))[:, :1]


def patch_columns(side_ref, image):
    side = jnp.full((SLOT, 128), side_of(side_ref, image), jnp.int32).astype(F32)
    slot = lax.broadcasted_iota(jnp.int32, (SLOT, 128), 0).astype(F32)
    row = jnp.floor((slot + 0.5) / side)
    col = slot - row * side
    valid = slot < side * side
    return col, row, valid


def spread(parity):
    src = lax.broadcasted_iota(jnp.int32, (128, 128), 0)
    lane = lax.broadcasted_iota(jnp.int32, (128, 128), 1)
    return (src == parity * HD + (lane // HD) * (HD // 2) + lane % (HD // 2)).astype(BF)


class Place:
    def __init__(self):
        self.p = lax.axis_index("dp")
        self.g = lax.axis_index("group")
        self.z, self.y = self.p // 2, self.p % 2
        self.x, self.core = self.g // 2, self.g % 2

    def over(self):
        return (self.g, self.p ^ 1)

    def sibling(self):
        return (self.g ^ 1, self.p)

    def across(self):
        return (self.g ^ 2, self.p)

    def line(self):
        return [(self.g, self.p ^ (2 * k)) for k in (1, 2, 3)]

    def partners(self):
        return [self.sibling(), self.across(), self.over()] + self.line()


def remote(src, dst, send, recv, device):
    return pltpu.make_async_remote_copy(
        src_ref=src, dst_ref=dst, send_sem=send, recv_sem=recv, device_id=device, device_id_type=pl.DeviceIdType.MESH
    )


def load(src, dst, sem):
    copy = pltpu.make_async_copy(src, dst, sem)
    copy.start()
    return copy


def greet(devices):
    barrier = pltpu.get_barrier_semaphore()
    for device in devices:
        pl.semaphore_signal(barrier, inc=1, device_id=device, device_id_type=pl.DeviceIdType.MESH)
    pl.semaphore_wait(barrier, len(devices))


def timetable(plan):
    return sorted(((step, name, stage) for name, steps in plan.items() for stage, step in enumerate(steps)), key=lambda r: r[0])


class Moves:
    def __init__(self, items, plan):
        self.items, self.rows = items, timetable(plan)

    def at(self, step):
        for when, name, stage in self.rows:
            if when == step:
                self.items[name].stage(stage)

    def within(self, step, first, last):
        for when in sorted({r[0] for r in self.rows if first <= r[0] <= last}):
            pl.when(step == when)(functools.partial(self.at, when))


class Gather:
    STAGES = 5

    def __init__(self, place, own, full, sems, recv, index):
        self.w, self.own, self.full = place, own, full
        self.rows = full.shape[0] // 8
        self.t = self.rows // 3 if self.rows % 48 == 0 else self.rows * 3 // 8
        self.e = self.rows - 2 * self.t
        self.send, self.sib = sems.at[2 * index], sems.at[2 * index + 1]
        self.recv = recv.at[index]

    def part(self, block, piece, ref=None):
        ref = self.full if ref is None else ref
        first = block * self.rows + piece * self.t
        return ref.at[pl.ds(pl.multiple_of(first, 16), self.e if isinstance(piece, int) else self.t)]

    def push(self, ref, device, index, src=None):
        remote(ref if src is None else src, ref, self.send, self.recv.at[index], device).start()

    def got(self, ref, index):
        remote(ref, ref, self.send, self.recv.at[index], self.w.sibling()).wait_recv()

    def hand(self, ref):
        remote(ref, ref, self.send, self.sib, self.w.sibling()).start()

    def stage(self, number):
        w = self.w
        pl.when(w.core == 0)(lambda: self.step(number, w.x, True))
        pl.when(w.core == 1)(lambda: self.step(number, 2, False))

    def step(self, number, piece, split):
        w = self.w
        if number == 0:
            src = self.part(0, piece, self.own)
            for k in (1, 3, 2):
                self.push(self.part(w.p, piece), (w.g, w.p ^ (2 * k)), w.z, src)
            self.push(self.part(w.p, piece), w.over(), 4 + w.z, src)
        elif number in (1, 2):
            for k in (1, 3, 2) if number == 1 else (0, 1, 3, 2):
                z = w.z ^ k
                block = 2 * z + (w.y if number == 1 else 1 - w.y)
                ref = self.part(block, piece)
                self.got(ref, z if number == 1 else 4 + z)
                if number == 1:
                    self.push(ref, w.over(), 4 + z)
                if split:
                    self.push(ref, w.across(), 8 + block)
                self.hand(ref)
        elif number == 3:
            if split:
                for k in (2, 6, 4, 1, 3, 7, 5):
                    block = w.p ^ k
                    ref = self.part(block, 1 - w.x)
                    self.got(ref, 8 + block)
                    self.hand(ref)
        else:
            for count in (14 * self.t, 14 * self.t) if split else (14 * self.e,):
                done = self.full.at[pl.ds(0, count)]
                remote(done, done, self.send, self.sib, w.sibling()).wait_send()
            came = self.full.at[pl.ds(0, 7 * self.e if split else 14 * self.t)]
            remote(came, came, self.send, self.sib, w.sibling()).wait_recv()


class Reduce:
    STAGES = 7

    def __init__(self, place, src, bufs, out, local, send, recv):
        self.w, self.src, self.out = place, src, out
        self.mine, self.cbuf, self.ybuf, self.zbuf, self.xbuf, self.fbuf = bufs
        self.rows = src.shape[0] // 8
        self.t, self.e = self.split(self.rows)
        self.local, self.send, self.recv = local, send, recv

    @staticmethod
    def split(rows):
        t = rows // 4 if rows % 64 == 0 else rows // 3
        return t, rows - 2 * t

    @classmethod
    def buffers(cls, rows, width):
        t, e = cls.split(rows)
        big = max(2 * t, e)
        sizes = (8 * big, 8 * big, 4 * max(t, e), 4 * max(t, e), 8 * t, max(t, e))
        return [pltpu.VMEM((n, width), BF) for n in sizes]

    def copy(self, src, dst, index, device):
        return remote(src, dst, self.send, self.recv.at[index], device)

    def took(self, ref, index):
        self.copy(ref, ref, index, self.w.sibling()).wait_recv()

    def rows_of(self, ref, first, count):
        return ref.at[pl.ds(pl.multiple_of(first, 16), count)]

    def add(self, target, *terms):
        def body(i, _):
            rows = pl.ds(pl.multiple_of(i * 32, 32), 32)
            total = target[rows].astype(F32)
            for term in terms:
                total = total + term[rows].astype(F32)
            target[rows] = total.astype(BF)
            return 0

        lax.fori_loop(0, target.shape[0] // 32, body, 0)

    def each_core(self, first, second):
        pl.when(self.w.core == 0)(first)
        pl.when(self.w.core == 1)(second)

    def exchange(self, theirs, their_rows, ours, our_rows):
        def body(b, _):
            self.copy(
                self.rows_of(self.src, b * self.rows + theirs, their_rows),
                self.rows_of(self.cbuf, b * their_rows, their_rows),
                0,
                self.w.sibling(),
            ).start()
            pltpu.make_async_copy(
                self.rows_of(self.src, b * self.rows + ours, our_rows),
                self.rows_of(self.mine, b * our_rows, our_rows),
                self.local,
            ).start()
            return 0

        lax.fori_loop(0, 8, body, 0)

    def settle(self, count):
        whole = self.mine.at[pl.ds(0, 8 * count)]
        pltpu.make_async_copy(whole, whole, self.local).wait()
        self.took(self.cbuf.at[pl.ds(0, 8 * count)], 0)
        self.add(whole, self.cbuf)

    def zero_at(self, block, piece):
        return self.rows_of(self.mine, block * 2 * self.t + piece * self.t, self.t)

    def one_at(self, block):
        return self.rows_of(self.mine, block * self.e, self.e)

    def send_y(self, count, at):
        w = self.w

        def body(z, _):
            self.copy(at(2 * z + 1 - w.y), self.rows_of(self.ybuf, z * count, count), 2, w.over()).start()
            return 0

        lax.fori_loop(0, 4, body, 0)

    def take_y(self, count, at):
        self.took(self.ybuf.at[pl.ds(0, 4 * count)], 2)

        def body(z, _):
            self.add(at(2 * z + self.w.y), self.rows_of(self.ybuf, z * count, count))
            return 0

        lax.fori_loop(0, 4, body, 0)

    def send_z(self, count, at):
        w = self.w
        for k in (3, 1, 2):
            z = w.z ^ k
            self.copy(at(2 * z + w.y), self.rows_of(self.zbuf, k * count, count), 3, (w.g, 2 * z + w.y)).start()

    def take_z(self, count, at):
        self.took(self.zbuf.at[pl.ds(0, 3 * count)], 3)
        self.add(at(self.w.p), *[self.rows_of(self.zbuf, k * count, count) for k in (1, 2, 3)])

    def give(self, first, count, value):
        ref = self.out.at[pl.ds(pl.multiple_of(first, 8), count)]
        ref[...] = value
        remote(ref, ref, self.send, self.recv.at[5], self.w.sibling()).start()

    def stage(self, number):
        w, t, e = self.w, self.t, self.e
        x_mine = functools.partial(self.zero_at, piece=w.x)
        x_other = functools.partial(self.zero_at, piece=1 - w.x)
        if number == 0:
            self.each_core(lambda: self.exchange(2 * t, e, 0, 2 * t), lambda: self.exchange(0, 2 * t, 2 * t, e))
        elif number == 1:

            def first():
                self.settle(2 * t)

                def body(b, _):
                    self.copy(x_other(b), self.rows_of(self.xbuf, b * t, t), 1, w.across()).start()
                    return 0

                lax.fori_loop(0, 8, body, 0)

            def second():
                self.settle(e)
                self.send_y(e, self.one_at)

            self.each_core(first, second)
        elif number == 2:

            def first():
                self.took(self.xbuf, 1)

                def body(b, _):
                    self.add(x_mine(b), self.rows_of(self.xbuf, b * t, t))
                    return 0

                lax.fori_loop(0, 8, body, 0)
                self.send_y(t, x_mine)

            def second():
                self.take_y(e, self.one_at)
                self.send_z(e, self.one_at)

            self.each_core(first, second)
        elif number == 3:

            def first():
                self.take_y(t, x_mine)
                self.send_z(t, x_mine)

            def second():
                self.take_z(e, self.one_at)
                self.copy(self.one_at(w.p), self.fbuf.at[pl.ds(0, e)], 4, w.across()).start()

            self.each_core(first, second)
        elif number == 4:

            def first():
                self.take_z(t, x_mine)
                self.copy(x_mine(w.p), self.fbuf.at[pl.ds(0, t)], 4, w.across()).start()
                self.give(w.x * t, t, x_mine(w.p)[...].astype(F32))

            def second():
                self.took(self.fbuf.at[pl.ds(0, e)], 4)
                self.give(2 * t, e, self.one_at(w.p)[...].astype(F32) + self.fbuf[pl.ds(0, e)].astype(F32))

            self.each_core(first, second)
        elif number == 5:

            @pl.when(w.core == 0)
            def _():
                self.took(self.fbuf.at[pl.ds(0, t)], 4)
                self.give((1 - w.x) * t, t, self.fbuf[pl.ds(0, t)].astype(F32))

        else:

            def sent(count):
                while count > 0:
                    now = min(count, self.mine.shape[0])
                    part = self.mine.at[pl.ds(0, now)]
                    remote(part, part, self.send, self.recv.at[0], w.sibling()).wait_send()
                    count -= now

            def came(first, count):
                ref = self.out.at[pl.ds(first, count)]
                remote(ref, ref, self.send, self.recv.at[5], w.sibling()).wait_recv()

            def first():
                came(2 * t, e)
                sent(8 * e + 8 * t + 4 * t + 3 * t + t + 4 * t)

            def second():
                came(0, 2 * t)
                sent(16 * t + 4 * e + 3 * e + e + 2 * e)

            self.each_core(first, second)


class SmallSum:
    HOPS = (4, 2, 4)

    def __init__(self, place, value, bufs, send, recv):
        self.w, self.value, self.bufs, self.send, self.recv = place, value, bufs, send, recv

    def copies(self, hop):
        w = self.w
        for k in range(1, self.HOPS[hop]):
            device = ((w.g ^ k, w.p), (w.g, w.p ^ k), (w.g, w.p ^ (2 * k)))[hop]
            ref = self.bufs.at[4 * hop]
            yield remote(ref, self.bufs.at[4 * hop + k], self.send.at[hop, k], self.recv.at[hop, k], device)

    def stage(self, number):
        w = self.w
        if number > 0:
            hop = number - 1
            for copy in self.copies(hop):
                copy.wait()
            mine = (w.g, w.y, w.z)[hop]
            total = self.bufs[4 * hop + mine]
            for k in range(1, self.HOPS[hop]):
                total = total + self.bufs[4 * hop + (mine ^ k)]
        else:
            total = self.value[...]
        if number == 3:
            self.value[...] = total
        else:
            self.bufs[4 * number] = total
            for copy in self.copies(number):
                copy.start()


def mask_column(side_ref, image):
    side = side_of(side_ref, image)
    slot = lax.broadcasted_iota(jnp.int32, (SLOT, 1), 0)
    return jnp.where(slot < side * side, 0.0, MASK_FILL).astype(F32)


def head_pair(images, step):
    i, j = step % images, step // images
    rows = pl.ds(pl.multiple_of(i * SLOT, SLOT), SLOT)
    return i, rows, pl.multiple_of(j * 128, 128), pl.multiple_of((j // 2) * D + (j % 2) * 128, 128)


def attend_step(images, step, side_ref, qkv_ref, ctx_ref, lse_ref):
    i, rows, c, at = head_pair(images, step)
    q = qkv_ref[rows, pl.ds(at, 128)]
    k = qkv_ref[rows, pl.ds(at + THIRD, 128)]
    v = qkv_ref[rows, pl.ds(at + 2 * THIRD, 128)]
    lane = lax.broadcasted_iota(jnp.int32, (1, 128), 1)
    mask = mask_column(side_ref, i)
    outs, logs = [], []
    for h in range(2):
        qm = jnp.where(lane // HD == h, q, jnp.zeros_like(q))
        s = dot(k, qm, NT) * (LOG2E / math.sqrt(HD)) + mask
        top = jnp.max(s, axis=0, keepdims=True)
        e = jnp.exp2(s - top)
        total = jnp.sum(e, axis=0, keepdims=True)
        p = (e * (1.0 / total)).astype(BF)
        outs.append(dot(p, v, TN))
        logs.append(top + jnp.log2(total))
    ctx_ref[rows, pl.ds(c, 128)] = jnp.where(lane < HD, outs[0], outs[1]).astype(BF)
    lse_ref[step] = jnp.concatenate(logs + [jnp.zeros((6, SLOT), F32)], axis=0)


def norm_rows(images, x_ref, small, norm_ref):
    def body(step, _):
        rows = pl.ds(pl.multiple_of(step * 192, 192), 192)
        unit, _ = norm_stats(x_ref[rows])
        norm_ref[rows] = (unit * small[R_G1 : R_G1 + 1] + small[R_S1 : R_S1 + 1]).astype(BF)
        return 0

    lax.fori_loop(0, images * SLOT // 192, body, 0)


def angle_tables(images, side_ref, small, cos_ref, sin_ref):
    for j in range(D // 128):
        flat = [small[R_FR : R_FR + 1, n + j // 2 * 128 : n + j // 2 * 128 + 128] for n in (0, D // 2)]
        fc, fr = [dot(jnp.broadcast_to(v, (8, 128)).astype(BF), spread(j % 2), NN)[0:1] for v in flat]

        def body(i, _):
            rows = pl.ds(pl.multiple_of(i * SLOT, SLOT), SLOT)
            col, row, _ = patch_columns(side_ref, i)
            sn, cs = sincos(col * fc + row * fr)
            cos_ref[rows, pl.ds(j * 128, 128)] = cs
            sin_ref[rows, pl.ds(j * 128, 128)] = sn * -half_sign(128)
            return 0

        lax.fori_loop(0, images, body, 0)


def project_block(images, c, r, small, w_ref, norm_ref, qkv_ref, cos_ref, sin_ref):
    i, part = r % images, r // images
    rows = pl.ds(pl.multiple_of(i * SLOT, SLOT), SLOT)
    cols = pl.ds(pl.multiple_of(part * THIRD, THIRD), THIRD)
    lanes = pl.ds(pl.multiple_of(c * D + part * THIRD, THIRD), THIRD)
    inner = pl.ds(pl.multiple_of(c * THIRD, THIRD), THIRD)
    raw = dot(norm_ref[rows], w_ref[c, :, cols], NN) + small[pl.ds(R_QB + part, 1), inner]

    @pl.when(part < 2)
    def _():
        turned = raw * cos_ref[rows, inner] + swap_halves(raw) * sin_ref[rows, inner]
        qkv_ref[rows, lanes] = turned.astype(BF)

    @pl.when(part == 2)
    def _():
        qkv_ref[rows, lanes] = raw.astype(BF)


def forward_compute(images, side_ref, x_ref, small, w_ref, qkv, norm, cos, sin, ctx_ref, lse_ref, hooks):
    hooks("start")
    norm_rows(images, x_ref, small, norm)
    hooks("tables")
    angle_tables(images, side_ref, small, cos, sin)
    blocks, pairs = 3 * images, 2 * images

    def body(step, _):
        hooks("step", step)
        c, r = step // (blocks + pairs), step % (blocks + pairs)

        @pl.when(r < blocks)
        def _():
            project_block(images, c, r, small, w_ref, norm, qkv, cos, sin)

        @pl.when(r >= blocks)
        def _():
            attend_step(images, c * pairs + r - blocks, side_ref, qkv, ctx_ref, lse_ref)

        return 0

    lax.fori_loop(0, 3 * (blocks + pairs), body, 0)
    hooks("end")


def forward_plain(images, side_ref, x_ref, small_ref, w_ref, *refs):
    qkv, norm, cos, sin, ctx, lse = refs
    forward_compute(images, side_ref, x_ref, small_ref, w_ref, qkv, norm, cos, sin, ctx, lse, lambda *a: None)


def packed_places(p, dp, sizes):
    run = D // dp
    for first, size in zip(SMALL_ROWS, sizes):
        count = size // run
        yield [(first + (p * count + m) // dp, ((p * count + m) % dp) * run) for m in range(count)]


SMALL_ROWS = (R_G1, R_S1, R_QB, R_FR, R_OB, R_G2, R_S2, R_UB, R_DB)


SINGLES = (R_G1, R_S1, R_FR, R_OB, R_G2, R_S2, R_DB)
MORE = ((2, R_QB, 3, 8), (7, R_UB, 4, 11))


def compact(tinies, ref):
    run = tinies[0].shape[1]
    first = {row: i for i, row in enumerate(SMALL_ROWS)}
    for n, row in enumerate(SINGLES):
        ref[n : n + 1, :run] = tinies[first[row]][...].astype(BF).astype(F32)
    for index, _, count, at in MORE:
        for m in range(count):
            ref[at + m : at + m + 1, :run] = tinies[index][:, m * run : (m + 1) * run].astype(BF).astype(F32)


def expand(parts, small, run):
    small[...] = jnp.zeros_like(small)
    lane = lax.broadcasted_iota(jnp.int32, (1, 128), 1)
    total = None
    for owner, ref in parts:
        wide = jnp.concatenate([jnp.where(lane < run, ref[...], 0.0), jnp.zeros((R_ALL, D - 128), F32)], axis=1)
        term = pltpu.roll(wide[0:8], owner * run, 1)
        total = term if total is None else total + term
        for _, row, count, at in MORE:
            for m in range(count):
                place = owner * count + m
                moved = pltpu.roll(jnp.broadcast_to(wide[at + m : at + m + 1], (8, D)), (place % 8) * run, 1)
                small[pl.ds(row + place // 8, 1), :] += moved[0:1]
    for n, row in enumerate(SINGLES):
        small[row : row + 1] = total[n : n + 1]


def forward_gather(images, side_ref, *refs):
    tinies, x_in, shards_in = refs[0:9], refs[9], refs[10:14]
    qkv_out, norm_out, cos_out, sin_out, ctx, lse, small, wq_out, wo, wu, wd, up_later, down_later = refs[14:27]
    x_ref, qkv, norm, cos, sin, wq, slots, bq, bo, bu, bd, sq, so, su, sd = refs[27:42]
    sems, recv, psend, precv, local, ins = refs[42:]
    w = Place()
    pairs = [(bq.at[c], wq.at[c]) for c in range(3)] + [(bo, wo)]
    pairs += [(own.at[c], full.at[c]) for c in range(PARTS - 1) for own, full in ((bu, wu), (bd, wd))]
    gathers = dict(zip(("q0", "q1", "q2", "o", "u0", "d0", "u1", "d1"), pairs))
    gathers = {k: Gather(w, *v, sems, recv, i) for i, (k, v) in enumerate(gathers.items())}
    moves = Moves(gathers, FORWARD_PLAN)
    peers = [w.p ^ k for k in range(1, 8)]
    keep = {}

    def store(name, src, dst):
        keep[name] = load(src, dst, local.at[len(keep)])

    def qkv_third(c):
        lanes = pl.ds(c * D, D)
        return pltpu.make_async_copy(qkv.at[:, lanes], qkv_out.at[:, lanes], local.at[16 + c])

    def late(number):
        src, dst = ((cos, cos_out), (sin, sin_out), (wq, wq_out))[number]
        return pltpu.make_async_copy(src, dst, local.at[19 + number])

    def own_rows(full):
        count = full.shape[0] // 8
        return full.at[pl.ds(pl.multiple_of(w.p * count, 16), count)]

    def pack_copy(k):
        return remote(slots.at[0], slots.at[k], psend.at[k - 1], precv.at[k - 1], (w.g, peers[k - 1]))

    def hooks(where, step=None):
        if where == "start":
            reads = [
                load(src, dst, ins.at[i])
                for i, (src, dst) in enumerate(zip(shards_in[:1] + (x_in,) + shards_in[1:], (sq, x_ref, so, su, sd)))
            ]
            compact(tinies, slots.at[0])
            greet([(w.g, q) for q in peers] + [w.sibling(), w.across()])
            for k in range(1, 8):
                pack_copy(k).start()
            reads[0].wait()
            for c in range(3):
                for part in range(3):
                    cols = part * D + c * THIRD
                    bq[c, :, part * THIRD : (part + 1) * THIRD] = sq[:, cols : cols + THIRD].astype(BF)
                if c == 0:
                    moves.at(-1)
            for copy in reads[1:]:
                copy.wait()
            bo[...] = so[...].astype(BF)
            for c in range(PARTS):
                for b in range(8):
                    cols = (b * PARTS + c) * 128
                    bu[c, :, b * 128 : (b + 1) * 128] = su[:, cols : cols + 128].astype(BF)
                bd[c] = sd[c * 128 : (c + 1) * 128].astype(BF)
            for i, (own, full) in enumerate(pairs):
                store(i, own, own_rows(full))
            store("up", bu.at[PARTS - 1], up_later)
            store("down", bd.at[PARTS - 1], down_later)
            for k in range(1, 8):
                pack_copy(k).wait()
            expand([(w.p, slots.at[0])] + [(peers[k - 1], slots.at[k]) for k in range(1, 8)], small, D // 8)
            moves.at(0)
        elif where == "tables":
            moves.at(1)
            store("norm", norm, norm_out)
        elif where == "step":

            @pl.when(step == 0)
            def _():
                for i in range(3):
                    keep[i].wait()
                for number in (0, 1):
                    late(number).start()

            moves.within(step + 2, 2, 31)
            for c in (1, 2):

                @pl.when(step == 10 * c)
                def _(c=c):
                    qkv_third(c - 1).start()
                    if c == 2:
                        late(2).start()

        else:
            qkv_third(2).start()
            moves.at(32)
            for c in range(3):
                qkv_third(c).wait()
                late(c).wait()
            for name, copy in keep.items():
                if name not in (0, 1, 2):
                    copy.wait()

    forward_compute(images, side_ref, x_ref, small, wq, qkv, norm, cos, sin, ctx, lse, hooks)


FORWARD_PLAN = {
    "q0": (-1, 1, 2, 2, 2),
    "q1": (0, 2, 9, 11, 12),
    "q2": (1, 4, 10, 16, 19),
    "o": (1, 7, 14, 29, 31),
    "u0": (3, 11, 17, 25, 26),
    "d0": (5, 16, 21, 27, 31),
    "u1": (17, 21, 28, 31, 32),
    "d1": (10, 16, 24, 30, 31),
}


def bias_at(split, step):
    c, k = step // BLOCKS, step % BLOCKS
    if split:
        return (R_UB + k, c * 128), (R_UB + k, D // 2 + c * 128)
    return (R_UB + step // 3, (step % 3) * 256), (R_UB + step // 3, (step % 3) * 256 + 128)


def mlp_compute(images, split, side_ref, scale, cot_ref, ctx_ref, small, wo_ref, wu, wd, refs, outs, hooks):
    mid, n2, n2t, bl, hid, gpre, ubias, gubias = refs
    act, gm, gctx, gdown, gup, gout, gs = outs
    rows_all = images * SLOT
    tile = SLOT // 2
    hooks("start")
    gain = small[R_G2 : R_G2 + 1]
    gs[...] = jnp.zeros_like(gs)
    for step in range(PARTS * BLOCKS):
        for n, (r, l) in enumerate(bias_at(split, step)):
            ubias[step : step + 1, n * 128 : (n + 1) * 128] = small[r : r + 1, l : l + 128]

    def tile_rows(step):
        side = side_of(side_ref, step // 2)
        slot = lax.broadcasted_iota(jnp.int32, (tile, 1), 0) + (step % 2) * tile
        return pl.ds(pl.multiple_of(step * tile, tile), tile), slot < side * side

    def enter(step, _):
        rows, valid = tile_rows(step)
        middle = mid[rows] + (dot(ctx_ref[rows], wo_ref[...], NN) + small[R_OB : R_OB + 1])
        mid[rows] = middle
        act[rows] = middle + small[R_DB : R_DB + 1]
        unit, _ = norm_stats(middle)
        n2[rows] = (unit * gain + small[R_S2 : R_S2 + 1]).astype(BF)
        low = jnp.where(valid, cot_ref[rows], 0.0).astype(BF)
        bl[rows] = low
        gs[R_DB : R_DB + 1] += jnp.sum(low.astype(F32), axis=0, keepdims=True)
        return 0

    lax.fori_loop(0, 2 * images, enter, 0)
    gm[...] = jnp.zeros_like(gm)
    n2t[...] = n2[...].T
    hooks("entered")

    first = pl.ds(0, 256)
    hid[:, first] = jnp.zeros((rows_all, 256), BF)
    gpre[:, first] = jnp.zeros((rows_all, 256), BF)

    def weights(step):
        c = step // BLOCKS
        cols = pl.ds(pl.multiple_of((step % BLOCKS) * 256, 256), 256)
        gdown[c, cols, :] = (dot(hid[:, cols], bl[...], TN) * scale).astype(BF)
        gup[c, :, cols] = (dot(n2t[...], gpre[:, cols], NN) * scale).astype(BF)

    def block(step, _):
        hooks("block", step)
        c, k = step // BLOCKS, step % BLOCKS
        cols = pl.ds(pl.multiple_of(k * 256, 256), 256)
        bias = ubias[pl.ds(step, 1), :]
        wuc = wu[c, :, cols]
        wdc = wd[c, cols, :]
        weights(jnp.maximum(step - 1, 0))
        pieces = [pl.ds(i * tile, tile) for i in range(2 * images)]
        pres = [dot(n2[rows], wuc, NN) + bias for rows in pieces]
        backs = [dot(bl[rows], wdc, NT) for rows in pieces]
        bsum = None
        for rows, pre, back in zip(pieces, pres, backs):
            value, slope = gelu_pair(pre)
            hid[rows, cols] = value.astype(BF)
            g = (back * slope).astype(BF)
            gpre[rows, cols] = g
            part = jnp.sum(g.astype(F32), axis=0, keepdims=True)
            bsum = part if bsum is None else bsum + part
        gubias[pl.ds(step, 1), :] = bsum

        @pl.when(k == BLOCKS - 1)
        def _():
            def tail(n, _):
                rows = pl.ds(pl.multiple_of(n * SLOT, SLOT), SLOT)
                act[rows] += dot(hid[rows], wd[c], NN)
                gm[rows] += dot(gpre[rows], wu[c], NT)
                return 0

            lax.fori_loop(0, images, tail, 0)

        return 0

    lax.fori_loop(0, PARTS * BLOCKS, block, 0)
    weights(PARTS * BLOCKS - 1)
    hooks("blocks")

    def leave(step, _):
        rows, valid = tile_rows(step)
        unit, inv = norm_stats(mid[rows])
        act[rows] = jnp.where(valid, act[rows], 0.0)
        gn = gm[rows]
        gs[R_G2 : R_G2 + 1] += jnp.sum(gn * unit, axis=0, keepdims=True)
        gs[R_S2 : R_S2 + 1] += jnp.sum(gn, axis=0, keepdims=True)
        a = gn * gain
        ma = jnp.mean(a, axis=-1, keepdims=True)
        mu = jnp.mean(a * unit, axis=-1, keepdims=True)
        g = jnp.where(valid, cot_ref[rows], 0.0) + inv * (a - ma - unit * mu)
        gm[rows] = g
        low = g.astype(BF)
        bl[rows] = low
        gs[R_OB : R_OB + 1] += jnp.sum(low.astype(F32), axis=0, keepdims=True)
        gctx[rows] = dot(low, wo_ref[...], NT).astype(BF)
        return 0

    lax.fori_loop(0, 2 * images, leave, 0)
    for step in range(PARTS * BLOCKS):
        for n, (r, l) in enumerate(bias_at(split, step)):
            gs[r : r + 1, l : l + 128] = gubias[step : step + 1, n * 128 : (n + 1) * 128]
    gout[...] = (dot(ctx_ref[...], bl[...], TN) * scale).astype(BF)
    gs[...] = gs[...] * scale
    hooks("end")


def mlp_scratch(rows):
    vmem = pltpu.VMEM
    return (
        [vmem((rows, D), F32), vmem((rows, D), BF), vmem((D, rows), BF), vmem((rows, D), BF)]
        + [vmem((rows, FF // PARTS), BF)] * 2
        + [vmem((16, 256), F32)] * 2
    )


def mlp_plain(images, slots, side_ref, assign_ref, counts_ref, x_ref, cot_ref, ctx_ref, small, wo_ref, wu, wd, *rest):
    outs, refs, sem = rest[0:7], rest[7:15], rest[15]
    load(x_ref, refs[0], sem.at[0]).wait()
    mlp_compute(
        images, False, side_ref, device_weight(slots, assign_ref, counts_ref), cot_ref, ctx_ref, small, wo_ref, wu, wd, refs, outs, lambda *a: None
    )


def mlp_moving(images, slots, side_ref, assign_ref, counts_ref, small, *rest):
    x_in, cot_in, ctx_in, wo_in, wu_in, wd_in, up_later, down_later = rest[0:8]
    act_out, gm_out, gctx_out, gd_out, gu_out, go_out, gs, rd, ru = rest[8:17]
    refs = rest[17:25]
    mid, n2, n2t = refs[0], refs[1], refs[2]
    cot, ctx, wo, wu, wd, act, gm, gd, gu = rest[25:34]
    bufs, (local, sems, recv, rlocal, rsend, rrecv) = rest[34:46], rest[46:52]
    w = Place()
    last = PARTS - 1
    items = {
        "u": Gather(w, up_later, wu.at[last], sems, recv, 0),
        "d": Gather(w, down_later, wd.at[last], sems, recv, 1),
        "rd": Reduce(w, gd.at[0], bufs[0:6], rd, rlocal.at[0], rsend.at[0], rrecv.at[0]),
        "ru": Reduce(w, gu.at[0], bufs[6:12], ru, rlocal.at[1], rsend.at[1], rrecv.at[1]),
    }
    moves = Moves(items, MLP_PLAN)
    keep = []

    def move(src, dst):
        keep.append(load(src, dst, local.at[len(keep)]))
        return keep[-1]

    def hooks(where, step=None):
        if where == "start":
            move(ctx_in, ctx), move(x_in, mid), move(wo_in, wo), move(cot_in, cot)
            for c in range(last):
                move(wu_in.at[c], wu.at[c])
                move(wd_in.at[c], wd.at[c])
            for own, full in ((up_later, wu), (down_later, wd)):
                count = full.shape[1] // 8
                move(own, full.at[last, pl.ds(pl.multiple_of(w.p * count, 16), count)])
            greet(w.partners())
            moves.at(0)
            for copy in keep[:4]:
                copy.wait()
        elif where == "entered":
            for copy in keep[4:]:
                copy.wait()
            keep.clear()
        elif where == "block":
            moves.within(step + 1, 1, 12)
        elif where == "blocks":
            for c in (1, 2):
                move(gd.at[c], gd_out.at[c - 1])
                move(gu.at[c], gu_out.at[c - 1])
            moves.at(13)
        else:
            move(act, act_out)
            move(gm, gm_out)
            move(n2, gctx_out)
            move(n2t.at[:, pl.ds(0, D)], go_out)
            moves.at(14)
            for copy in keep:
                copy.wait()

    mlp_compute(
        images,
        True,
        side_ref,
        device_weight(slots, assign_ref, counts_ref),
        cot,
        ctx,
        small,
        wo,
        wu,
        wd,
        refs,
        (act, gm, n2, gd, gu, n2t.at[:, pl.ds(0, D)], gs),
        hooks,
    )


MLP_PLAN = {
    "u": (0, 2, 4, 5, 7),
    "d": (1, 4, 5, 7, 8),
    "rd": (6, 8, 10, 12, 13, 14, 14),
    "ru": (6, 7, 9, 11, 13, 14, 14),
}


PARTS = 3
BLOCKS = 4


def attend_back_step(images, step, side_ref, qkv_ref, gctx_ref, lse_ref, cos_ref, sin_ref, gproj_ref, gs_ref, gf_ref):
    i, rows, c, at = head_pair(images, step)
    q = qkv_ref[rows, pl.ds(at, 128)]
    k = qkv_ref[rows, pl.ds(at + THIRD, 128)]
    v = qkv_ref[rows, pl.ds(at + 2 * THIRD, 128)]
    go = gctx_ref[rows, pl.ds(c, 128)]
    lane = lax.broadcasted_iota(jnp.int32, (1, 128), 1)
    mask = mask_column(side_ref, i)
    lse = lse_ref[step]
    dq, dk, dv = [], [], []
    for h in range(2):
        mine = lane // HD == h
        qm = jnp.where(mine, q, jnp.zeros_like(q))
        gom = jnp.where(mine, go, jnp.zeros_like(go))
        s = dot(k, qm, NT) * (LOG2E / math.sqrt(HD)) + mask
        p = jnp.exp2(s - lse[h : h + 1])
        dp = dot(v, gom, NT)
        dv.append(dot(p.astype(BF), go, NN))
        t = p * dp
        ds = (t - p * jnp.sum(t, axis=0, keepdims=True)).astype(BF)
        dk.append(dot(ds, q, NN))
        dq.append(dot(ds, k, TN))
    first = lane < HD
    cs = cos_ref[rows, pl.ds(c, 128)]
    sn = sin_ref[rows, pl.ds(c, 128)]
    angle = None
    for n, (pair, rot) in enumerate(((dq, q), (dk, k))):
        e = jnp.where(first, pair[0], pair[1]) * (1.0 / math.sqrt(HD))
        other = swap_halves(e)
        back = (e * cs - other * sn).astype(BF)
        gproj_ref[rows, pl.ds(at + n * THIRD, 128)] = back
        gs_ref[pl.ds(R_QB + n, 1), pl.ds(c, 128)] += jnp.sum(back.astype(F32), axis=0, keepdims=True)
        term = rot.astype(F32) * other
        angle = term if angle is None else angle + term
    gv = jnp.where(first, dv[0], dv[1]).astype(BF)
    gproj_ref[rows, pl.ds(at + 2 * THIRD, 128)] = gv
    gs_ref[R_QB + 2 : R_QB + 3, pl.ds(c, 128)] += jnp.sum(gv.astype(F32), axis=0, keepdims=True)
    angle = angle * half_sign(128)
    col, row, _ = patch_columns(side_ref, i)
    gf_ref[0:1, pl.ds(c, 128)] += jnp.sum(angle * col, axis=0, keepdims=True)
    gf_ref[1:2, pl.ds(c, 128)] += jnp.sum(angle * row, axis=0, keepdims=True)


def freq_row(gf_ref, gs_ref):
    for m in range(D // 128):
        which = m // 3
        total = None
        for parity in (0, 1):
            lanes = 2 * (m % 3) + parity
            value = gf_ref[which : which + 1, lanes * 128 : lanes * 128 + 128]
            for _ in range(3):
                term = value.astype(BF)
                value = value - term.astype(F32)
                moved = dot(jnp.broadcast_to(term, (8, 128)), spread(parity), NT)[0:1]
                total = moved if total is None else total + moved
        gs_ref[R_FR : R_FR + 1, m * 128 : m * 128 + 128] = total


def weight_third(c, scale, norm_ref, gproj_ref, gw_ref):
    def block(j, _):
        lanes = pl.ds(pl.multiple_of(j * THIRD, THIRD), THIRD)
        full = pl.ds(pl.multiple_of(c * D + j * THIRD, THIRD), THIRD)
        gw_ref[:, lanes] = (dot(norm_ref[...], gproj_ref[:, full], TN) * scale).astype(BF)
        return 0

    lax.fori_loop(0, 3, block, 0)


def attend_back_compute(images, thirds, side_ref, scale, ins, norm, gproj, gws, gs_ref, gf_ref, hooks):
    hooks("start")
    gs_ref[...] = jnp.zeros_like(gs_ref)
    gf_ref[...] = jnp.zeros_like(gf_ref)

    def body(step, _):
        hooks("step", step)
        attend_back_step(images, step, side_ref, *ins, gproj, gs_ref, gf_ref)
        for c in range(thirds):

            @pl.when(step == 2 * images * (c + 1) - 1)
            def _(c=c):
                weight_third(c, scale, norm, gproj, gws.at[c])

        return 0

    lax.fori_loop(0, images * HEADS // 2, body, 0)
    freq_row(gf_ref, gs_ref)
    hooks("end")


def attend_back_plain(images, slots, side_ref, assign_ref, counts_ref, *refs):
    ins, norm, (gproj, gws, gs, gf) = refs[0:5], refs[5], refs[6:10]
    attend_back_compute(images, 3, side_ref, device_weight(slots, assign_ref, counts_ref), ins, norm, gproj, gws, gs, gf, lambda *a: None)


def qkv_back_compute(images, x_ref, gproj_ref, gm_ref, small_ref, w_ref, gs_in, gin_ref, gs_ref, hooks):
    hooks("start")
    gain = small_ref[R_G1 : R_G1 + 1]
    gs_ref[...] = gs_in[...]
    tile = SLOT // 2

    def body(step, _):
        hooks("tile", step)
        rows = pl.ds(pl.multiple_of(step * tile, tile), tile)
        unit, inv = norm_stats(x_ref[rows])
        gn = None
        for c in range(3):
            term = dot(gproj_ref[rows, c * D : (c + 1) * D], w_ref[c][...], NT)
            gn = term if gn is None else gn + term
        gs_ref[R_G1 : R_G1 + 1] += jnp.sum(gn * unit, axis=0, keepdims=True)
        gs_ref[R_S1 : R_S1 + 1] += jnp.sum(gn, axis=0, keepdims=True)
        a = gn * gain
        ma = jnp.mean(a, axis=-1, keepdims=True)
        mu = jnp.mean(a * unit, axis=-1, keepdims=True)
        gin_ref[rows] = gm_ref[rows] + inv * (a - ma - unit * mu)
        return 0

    lax.fori_loop(0, 2 * images, body, 0)
    hooks("end")


def qkv_back_plain(images, slots, assign_ref, counts_ref, x_ref, gproj_ref, gm_ref, small_ref, w_ref, gs_in, gin, gs):
    def hooks(where, index=None):
        if where == "end":
            gs[...] = gs[...] * device_weight(slots, assign_ref, counts_ref)

    parts = [w_ref.at[c] for c in range(3)]
    qkv_back_compute(images, x_ref, gproj_ref, gm_ref, small_ref, parts, gs_in, gin, gs, hooks)


def backward_reduce(images, slots, side_ref, assign_ref, counts_ref, small_ref, gs_mlp, *refs):
    ins_in, (gd, gu, go), (x_in, gm_in, w_in) = refs[0:6], refs[6:9], refs[9:12]
    gin_out, gs, outs = refs[12], refs[13], refs[14:22]
    ins, gproj, gws, gf, gs_own = refs[22:28], refs[28], refs[29], refs[30], refs[31]
    bufs, tinybufs, (loads, local, send, recv, ssend, srecv) = refs[32:80], refs[80], refs[81:87]
    qkv, cos, sin, norm = ins[0], ins[3], ins[4], ins[5]
    w = Place()
    weight = device_weight(slots, assign_ref, counts_ref)
    srcs = (gd.at[0], gu.at[0], gd.at[1], gu.at[1], go, gws.at[0], gws.at[1], gws.at[2])
    items = {
        name: Reduce(w, srcs[i], bufs[6 * i : 6 * i + 6], outs[i], local.at[i], send.at[i], recv.at[i])
        for i, name in enumerate(BACK_PLAN)
    }
    moves = Moves(items, BACK_PLAN)
    tiny = SmallSum(w, gs, tinybufs, ssend, srecv)

    def hooks(where, step=None):
        if where == "start":
            copies = [load(src, dst, loads.at[i]) for i, (src, dst) in enumerate(zip(ins_in, ins))]
            greet(w.partners() + [(w.g ^ 3, w.p)])
            moves.at(0)
            for copy in copies:
                copy.wait()
        elif where == "step":
            moves.within(step + 1, 1, 12)

    attend_back_compute(images, 3, side_ref, weight, ins[0:5], norm, gproj, gws, gs_own, gf, hooks)
    copies = [load(x_in, cos, loads.at[0]), load(gm_in, sin, loads.at[1])]
    wide = [qkv.at[pl.ds(0, D), pl.ds(c * D, D)] for c in range(3)]
    copies += [load(w_in.at[c], wide[c], loads.at[2 + c]) for c in range(3)]
    moves.at(13)
    for copy in copies:
        copy.wait()

    def tiles(where, step=None):
        if where == "tile":
            moves.within(step + 14, 14, 17)

    qkv_back_compute(images, cos, gproj, sin, small_ref, wide, gs_own, sin, gs, tiles)
    copy = load(sin, gin_out, loads.at[0])
    gs[...] = gs[...] * weight + gs_mlp[...]
    for number in range(4):
        tiny.stage(number)
        moves.at(18 + number)
    copy.wait()


BACK_PLAN = {
    "d1": (1, 3, 6, 9, 17, 19, 19),
    "u1": (1, 7, 11, 14, 18, 19, 21),
    "d2": (2, 4, 6, 9, 13, 15, 19),
    "u2": (2, 5, 8, 11, 14, 18, 20),
    "o": (0, 4, 7, 13, 16, 18, 21),
    "q0": (6, 7, 11, 15, 18, 19, 20),
    "q1": (9, 10, 14, 16, 18, 19, 20),
    "q2": (13, 14, 17, 18, 19, 20, 21),
}


def finish_kernel(dp, p_axis, gs, act_in, gin_in, rout_in, *refs):
    rd, ru, rq = refs[0:3], refs[3:6], refs[6:9]
    act, gin, rqkv, rout, rup, rdown, sems = refs[9], refs[10], *refs[11:15], refs[-1]
    tinies = refs[15:-2]
    stage = refs[-2]
    ins = [load(act_in, stage.at[0], sems.at[0]), load(gin_in, stage.at[1], sems.at[1])]
    p = lax.axis_index(p_axis)
    run = D // dp
    for out, places in zip(tinies, packed_places(p, dp, [t.shape[0] for t in tinies])):
        for m, (row, lane) in enumerate(places):
            whole = jnp.broadcast_to(gs[pl.ds(row, 1), :], (8, D))
            out[pl.ds(m * run, run)] = pltpu.roll(whole, D - lane, 1)[0, :run]
    copies = []
    for n, dst in enumerate((act, gin)):
        ins[n].wait()
        copies.append(load(stage.at[n], dst, sems.at[n]))
    rout[...] = rout_in[...]
    for c in range(3):
        rdown[c * rd[c].shape[0] : (c + 1) * rd[c].shape[0]] = rd[c][...]
        for b in range(dp):
            rup[:, (b * 3 + c) * 128 : (b * 3 + c + 1) * 128] = ru[c][:, b * 128 : (b + 1) * 128]
        for part in range(3):
            cols = part * D + c * THIRD
            rqkv[:, cols : cols + THIRD] = rq[c][:, part * THIRD : (part + 1) * THIRD]
    for copy in copies:
        copy.wait()


def params(mb=56):
    return pltpu.CompilerParams(vmem_limit_bytes=mb << 20)


def place_rows(p, dp, vec):
    n = vec.shape[0]
    whole = jnp.tile(vec, dp)
    owner = jnp.arange(n * dp, dtype=jnp.int32) // n
    return jnp.where(owner == p, whole, 0.0).reshape(-1, D)


def on_device(
    fast,
    images,
    cotangent,
    resolution,
    assignment,
    counts,
    ln1_gain,
    ln1_shift,
    qkv_weight,
    qkv_bias,
    rope_freqs,
    out_weight,
    out_bias,
    ln2_gain,
    ln2_shift,
    up_weight,
    up_bias,
    down_weight,
    down_bias,
):
    p = lax.axis_index("dp")
    dp = lax.axis_size("dp")
    n = images.shape[0]
    rows = n * SLOT
    x = images.reshape(rows, D)
    cot = cotangent.reshape(rows, D)
    vectors = (ln1_gain, ln1_shift, qkv_bias, rope_freqs, out_bias, ln2_gain, ln2_shift, up_bias, down_bias)
    slots = dp * rows
    sds = jax.ShapeDtypeStruct
    smem = pl.BlockSpec(memory_space=pltpu.SMEM)
    anyw = pl.BlockSpec(memory_space=pl.ANY)
    kept = [
        sds((rows, 3 * D), BF),
        sds((rows, D), BF),
        sds((rows, D), F32),
        sds((rows, D), F32),
        sds((rows, D), BF),
        sds((n * HEADS // 2, 8, SLOT), F32),
    ]
    weights = (qkv_weight, out_weight, up_weight, down_weight)
    dma = pltpu.SemaphoreType.DMA
    vmem = pltpu.VMEM

    def moving(number, mb):
        return pltpu.CompilerParams(vmem_limit_bytes=mb << 20, collective_id=number, has_side_effects=True)

    part = FF // PARTS
    if fast:
        later = [sds((D // dp, part), BF), sds((part // dp, D), BF)]
        fulls = [sds((3, D, D), BF), sds((D, D), BF), sds((PARTS - 1, D, part), BF), sds((PARTS - 1, part, D), BF)]
        outs = pl.pallas_call(
            functools.partial(forward_gather, n),
            out_shape=kept + [sds((R_ALL, D), F32)] + fulls + later,
            in_specs=[smem] + vm(9) + [anyw] * 5,
            out_specs=[anyw] * 4 + vm(3) + [anyw] * 6,
            scratch_shapes=[
                vmem((rows, D), F32),
                vmem((rows, 3 * D), BF),
                vmem((rows, D), BF),
                vmem((rows, D), F32),
                vmem((rows, D), F32),
                vmem((3, D, D), BF),
                vmem((8, R_ALL, 128), F32),
                vmem((3, D // dp, D), BF),
                vmem((D // dp, D), BF),
                vmem((PARTS, D // dp, part), BF),
                vmem((PARTS, part // dp, D), BF),
            ]
            + [vmem(v.shape, F32) for v in weights]
            + [
                dma((16,)),
                dma((8, 16)),
                dma((7,)),
                dma((7,)),
                dma((22,)),
                dma((5,)),
            ],
            compiler_params=moving(0, 56),
            name="forward",
        )(resolution, *[v.reshape(1, -1) for v in vectors], x, *weights)
        qkv, norm1, cos, sin, ctx, lse, small, wqkv, wo, wu, wd, up_later, down_later = outs
    else:
        packed = [place_rows(p, dp, lax.reduce_precision(v, 8, 7)) for v in vectors]
        small = lax.psum(jnp.concatenate(packed + [jnp.zeros((2, D), F32)], axis=0), "dp")
        wqkv, wo, wu, wd = [lax.all_gather(v.astype(BF), "dp", axis=0, tiled=True) for v in weights]
        wqkv = wqkv.reshape(D, 3, 3, THIRD).transpose(2, 0, 1, 3).reshape(3, D, D)
        wu = wu.reshape(D, PARTS, part).transpose(1, 0, 2)
        wd = wd.reshape(PARTS, part, D)
        qkv, norm1, cos, sin, ctx, lse = pl.pallas_call(
            functools.partial(forward_plain, n),
            out_shape=kept,
            in_specs=[smem] + vm(3),
            out_specs=vm(6),
            compiler_params=params(),
            name="forward",
        )(resolution, x, small, wqkv)

    grads = [sds((PARTS, part, D), BF), sds((PARTS, D, part), BF), sds((D, D), BF)]
    rest = [sds((R_ALL, D), F32)]
    firsts = [sds((rows, D), F32), sds((rows, D), F32), sds((rows, D), BF)]
    tables = [vmem((rows, 3 * D), BF), vmem((rows, D), BF), vmem((n * HEADS // 2, 8, SLOT), F32)]
    tables += [vmem((rows, D), F32)] * 2
    gproj_shape = sds((rows, 3 * D), BF)
    if fast:
        sizes = [(part // dp, D), (D // dp, part)]
        act, gm, gctx, gdown, gup, gout, gs_mlp, rdown0, rup0 = pl.pallas_call(
            functools.partial(mlp_moving, n, slots),
            out_shape=firsts
            + [sds((PARTS - 1,) + g.shape[1:], BF) for g in grads[:2]]
            + grads[2:]
            + rest
            + [sds(z, F32) for z in sizes],
            in_specs=[smem] * 3 + vm(1) + [anyw] * 8,
            out_specs=[anyw] * 6 + vm(3),
            scratch_shapes=mlp_scratch(rows)
            + [
                vmem((rows, D), F32),
                vmem((rows, D), BF),
                vmem((D, D), BF),
                vmem((PARTS, D, part), BF),
                vmem((PARTS, part, D), BF),
                vmem((rows, D), F32),
                vmem((rows, D), F32),
                vmem((PARTS, part, D), BF),
                vmem((PARTS, D, part), BF),
            ]
            + sum([Reduce.buffers(*z) for z in sizes], [])
            + [dma((12,)), dma((4,)), dma((2, 16)), dma((2,)), dma((2,)), dma((2, 6))],
            compiler_params=moving(3, 63),
            name="mlp",
        )(resolution, assignment, counts, small, x, cot, ctx, wo, wu, wd, up_later, down_later)
        third = (D // dp, D)
        sizes = sizes + sizes + [third] * 4
        gin, gs, rdown1, rup1, rdown2, rup2, rout, rq0, rq1, rq2 = pl.pallas_call(
            functools.partial(backward_reduce, n, slots),
            out_shape=[sds((rows, D), F32)] + rest + [sds(z, F32) for z in sizes],
            in_specs=[smem] * 3 + vm(2) + [anyw] * 12,
            out_specs=[anyw] + vm(9),
            scratch_shapes=tables
            + [vmem((rows, D), BF), vmem((rows, 3 * D), BF), vmem((3, D, D), BF), vmem((8, D), F32)]
            + [vmem((R_ALL, D), F32)]
            + sum([Reduce.buffers(*z) for z in sizes], [])
            + [vmem((12, R_ALL, D), F32), dma((6,)), dma((8,)), dma((8,)), dma((8, 6)), dma((3, 4)), dma((3, 4))],
            compiler_params=moving(1, 62),
            name="backward",
        )(resolution, assignment, counts, small, gs_mlp, qkv, gctx, lse, cos, sin, norm1, gdown, gup, gout, x, gm, wqkv)

        matrices = (qkv_weight, out_weight, up_weight, down_weight)
        act, gin, rqkv, rout, rup, rdown, *tinies = pl.pallas_call(
            functools.partial(finish_kernel, dp, "dp"),
            out_shape=[sds((rows, D), F32)] * 2 + [sds(v.shape, F32) for v in matrices + vectors],
            in_specs=vm(1) + [anyw] * 2 + vm(10),
            out_specs=[anyw] * 2 + vm(13),
            scratch_shapes=[vmem((2, rows, D), F32), dma((2,))],
            compiler_params=params(),
            name="finish",
        )(gs, act, gin, rout, rdown0, rdown1, rdown2, rup0, rup1, rup2, rq0, rq1, rq2)
    else:
        act, gm, gctx, gdown, gup, gout, gs_mlp = pl.pallas_call(
            functools.partial(mlp_plain, n, slots),
            out_shape=firsts + grads + rest,
            in_specs=[smem] * 3 + [anyw] + vm(6),
            out_specs=vm(7),
            scratch_shapes=mlp_scratch(rows) + [dma((1,))],
            compiler_params=params(63),
            name="mlp",
        )(resolution, assignment, counts, x, cot, ctx, small, wo, wu, wd)
        gproj, gqkv, gs_att = pl.pallas_call(
            functools.partial(attend_back_plain, n, slots),
            out_shape=[gproj_shape, sds((3, D, D), BF)] + rest,
            in_specs=[smem] * 3 + vm(6),
            out_specs=vm(3),
            scratch_shapes=[vmem((8, D), F32)],
            compiler_params=params(),
            name="attend_back",
        )(resolution, assignment, counts, qkv, gctx, lse, cos, sin, norm1)
        gin, gs_qkv = pl.pallas_call(
            functools.partial(qkv_back_plain, n, slots),
            out_shape=[sds((rows, D), F32)] + rest,
            in_specs=[smem] * 2 + vm(6),
            out_specs=vm(2),
            compiler_params=params(),
            name="project_back",
        )(assignment, counts, x, gproj, gm, small, wqkv, gs_att)

        def reduce(g):
            total = lax.psum_scatter(g, "dp", scatter_dimension=0, tiled=True)
            return lax.psum(total, "group").astype(F32)

        gqkv = gqkv.reshape(3, D, 3, THIRD).transpose(1, 2, 0, 3).reshape(D, 3 * D)
        gup = gup.transpose(1, 0, 2).reshape(D, FF)
        rqkv, rout, rup, rdown = [reduce(g) for g in (gqkv, gout, gup, gdown.reshape(FF, D))]
        gs = lax.psum(gs_mlp + gs_qkv, ("group", "dp"))

        def own(first, count):
            flat = gs[first : first + count].reshape(dp, -1)
            return lax.dynamic_index_in_dim(flat, p, 0, keepdims=False)

        tinies = [own(first, v.shape[0] * dp // D) for first, v in zip(SMALL_ROWS, vectors)]

    g1, s1, qb, fr, ob, g2, s2, ub, db = tinies
    act, gin = act.reshape(images.shape), gin.reshape(images.shape)
    return (act, gin, g1, s1, rqkv, qb, fr, rout, ob, g2, s2, rup, ub, rdown, db)


def solution(mesh):
    batch = P(("group", "dp"), None, None)
    per_image = P(("group", "dp"))
    vec, mat = P("dp"), P("dp", None)
    fast = dict(mesh.shape) == {"group": 4, "dp": 8}
    return jax.shard_map(
        functools.partial(on_device, fast),
        mesh=mesh,
        in_specs=(batch, batch, per_image, per_image, P(), vec, vec, mat, vec, vec, mat, vec, vec, vec, mat, vec, mat, vec),
        out_specs=(batch, batch, vec, vec, mat, vec, vec, mat, vec, vec, vec, mat, vec, mat, vec),
        check_vma=False,
    )
```

```python
import functools
import math

import jax
import jax.numpy as jnp
from jax import lax
from jax.experimental import pallas as pl
from jax.experimental.pallas import tpu as pltpu
from jax.sharding import PartitionSpec as P

HEADS = 12
HD = 64
SIDE_S = 14
SIDE_M = 20
SIDE_L = 24
SLOT = 576
D = 768
FF = 3072
LN_EPS = 1e-06
MASK_FILL = -1e30
BF = jnp.bfloat16
F32 = jnp.float32
NT = (((1,), (1,)), ((), ()))
NN = (((1,), (0,)), ((), ()))
TN = (((0,), (0,)), ((), ()))
R_G1, R_S1, R_QB, R_FR, R_OB, R_G2, R_S2, R_UB, R_DB, R_ALL = 0, 1, 2, 5, 6, 7, 8, 9, 13, 16
THIRD = 256
LOG2E = math.log2(math.e)


def dot(a, b, dims, precision=None):
    return lax.dot_general(a, b, dims, preferred_element_type=F32, precision=precision)


def vm(n):
    return [pl.BlockSpec(memory_space=pltpu.VMEM)] * n


def norm_stats(x):
    mean = jnp.mean(x, axis=-1, keepdims=True)
    cen = x - mean
    var = jnp.mean(cen * cen, axis=-1, keepdims=True)
    inv = lax.rsqrt(var + LN_EPS)
    return cen * inv, inv


def sincos(x):
    n = jnp.floor(x * (2.0 / math.pi) + 0.5)
    r = x - n * 1.5703125
    r = r - n * 4.837512969970703125e-4
    r = r - n * 7.54978995489188216e-8
    q = n.astype(jnp.int32)
    r2 = r * r
    s = r + r * r2 * (-1.6666654611e-1 + r2 * (8.3321608736e-3 + r2 * -1.9515295891e-4))
    c = 1.0 - 0.5 * r2 + r2 * r2 * (
        4.166664568298827e-2 + r2 * (-1.388731625493765e-3 + r2 * 2.443315711809948e-5)
    )
    odd = (q & 1) == 1
    ss = jnp.where(odd, c, s)
    cc = jnp.where(odd, s, c)
    ss = jnp.where((q & 2) == 2, -ss, ss)
    cc = jnp.where(((q + 1) & 2) == 2, -cc, cc)
    return ss, cc


ERFC = (
    0.07314588129520416,
    -0.30809587240219116,
    0.3798876702785492,
    -0.08230462670326233,
    0.245080828666687,
    0.2054724544286728,
    0.24429383873939514,
    0.242519810795784,
)


def gelu_pair(x):
    z = jnp.abs(x)
    t = 1.0 / (1.0 + (0.43 * math.sqrt(0.5)) * z)
    poly = 0.5 * ERFC[0]
    for c in ERFC[1:]:
        poly = poly * t + 0.5 * c
    bell = jnp.exp2((x * x) * (-0.5 * LOG2E))
    half = poly * t * bell
    cdf = jnp.where(x < 0, half, 1.0 - half)
    return x * cdf, cdf + (x * math.sqrt(0.5 / math.pi)) * bell


def swap_halves(x):
    width = x.shape[-1]
    lane = lax.broadcasted_iota(jnp.int32, (1, width), 1)
    ahead = pltpu.roll(x, width - HD // 2, 1)
    behind = pltpu.roll(x, HD // 2, 1)
    return jnp.where(lane % HD < HD // 2, ahead, behind)


def half_sign(width):
    lane = lax.broadcasted_iota(jnp.int32, (1, width), 1)
    return jnp.where(lane % HD < HD // 2, 1.0, -1.0).astype(F32)


def side_of(res_ref, image):
    res = res_ref[image]
    return jnp.where(res == 0, SIDE_S, jnp.where(res == 1, SIDE_M, SIDE_L))


def device_weight(slots, assign_ref, counts_ref):
    groups = counts_ref.shape[0]
    counts = [jnp.full((1, 128), counts_ref[i], jnp.int32).astype(F32) for i in range(groups)]
    mine = jnp.full((1, 128), assign_ref[0], jnp.int32)
    picked = sum(jnp.where(mine == i, counts[i], 0.0) for i in range(groups))
    return (groups * picked / sum(counts) * (1.0 / math.sqrt(slots)))[:, :1]


def patch_columns(side_ref, image):
    side = jnp.full((SLOT, 128), side_of(side_ref, image), jnp.int32).astype(F32)
    slot = lax.broadcasted_iota(jnp.int32, (SLOT, 128), 0).astype(F32)
    row = jnp.floor((slot + 0.5) / side)
    col = slot - row * side
    valid = slot < side * side
    return col, row, valid


def spread(parity):
    src = lax.broadcasted_iota(jnp.int32, (128, 128), 0)
    lane = lax.broadcasted_iota(jnp.int32, (128, 128), 1)
    return (src == parity * HD + (lane // HD) * (HD // 2) + lane % (HD // 2)).astype(BF)


class Place:
    def __init__(self):
        self.p = lax.axis_index("dp")
        self.g = lax.axis_index("group")
        self.z, self.y = self.p // 2, self.p % 2
        self.x, self.core = self.g // 2, self.g % 2

    def over(self):
        return (self.g, self.p ^ 1)

    def sibling(self):
        return (self.g ^ 1, self.p)

    def across(self):
        return (self.g ^ 2, self.p)

    def line(self):
        return [(self.g, self.p ^ (2 * k)) for k in (1, 2, 3)]

    def partners(self):
        return [self.sibling(), self.across(), self.over()] + self.line()


def remote(src, dst, send, recv, device):
    return pltpu.make_async_remote_copy(
        src_ref=src, dst_ref=dst, send_sem=send, recv_sem=recv, device_id=device, device_id_type=pl.DeviceIdType.MESH
    )


def load(src, dst, sem):
    copy = pltpu.make_async_copy(src, dst, sem)
    copy.start()
    return copy


def greet(devices):
    barrier = pltpu.get_barrier_semaphore()
    for device in devices:
        pl.semaphore_signal(barrier, inc=1, device_id=device, device_id_type=pl.DeviceIdType.MESH)
    pl.semaphore_wait(barrier, len(devices))


def timetable(plan):
    return sorted(((step, name, stage) for name, steps in plan.items() for stage, step in enumerate(steps)), key=lambda r: r[0])


class Moves:
    def __init__(self, items, plan):
        self.items, self.rows = items, timetable(plan)

    def at(self, step):
        for when, name, stage in self.rows:
            if when == step:
                self.items[name].stage(stage)

    def within(self, step, first, last):
        for when in sorted({r[0] for r in self.rows if first <= r[0] <= last}):
            pl.when(step == when)(functools.partial(self.at, when))


class Gather:
    STAGES = 5

    def __init__(self, place, own, full, sems, recv, index):
        self.w, self.own, self.full = place, own, full
        self.rows = full.shape[0] // 8
        self.t = self.rows // 3 if self.rows % 48 == 0 else self.rows * 3 // 8
        self.e = self.rows - 2 * self.t
        self.send, self.sib = sems.at[2 * index], sems.at[2 * index + 1]
        self.recv = recv.at[index]

    def part(self, block, piece, ref=None):
        ref = self.full if ref is None else ref
        first = block * self.rows + piece * self.t
        return ref.at[pl.ds(pl.multiple_of(first, 16), self.e if isinstance(piece, int) else self.t)]

    def push(self, ref, device, index, src=None):
        remote(ref if src is None else src, ref, self.send, self.recv.at[index], device).start()

    def got(self, ref, index):
        remote(ref, ref, self.send, self.recv.at[index], self.w.sibling()).wait_recv()

    def hand(self, ref):
        remote(ref, ref, self.send, self.sib, self.w.sibling()).start()

    def stage(self, number):
        w = self.w
        pl.when(w.core == 0)(lambda: self.step(number, w.x, True))
        pl.when(w.core == 1)(lambda: self.step(number, 2, False))

    def step(self, number, piece, split):
        w = self.w
        if number == 0:
            src = self.part(0, piece, self.own)
            for k in (1, 3, 2):
                self.push(self.part(w.p, piece), (w.g, w.p ^ (2 * k)), w.z, src)
            self.push(self.part(w.p, piece), w.over(), 4 + w.z, src)
        elif number in (1, 2):
            for k in (1, 3, 2) if number == 1 else (0, 1, 3, 2):
                z = w.z ^ k
                block = 2 * z + (w.y if number == 1 else 1 - w.y)
                ref = self.part(block, piece)
                self.got(ref, z if number == 1 else 4 + z)
                if number == 1:
                    self.push(ref, w.over(), 4 + z)
                if split:
                    self.push(ref, w.across(), 8 + block)
                self.hand(ref)
        elif number == 3:
            if split:
                for k in (2, 6, 4, 1, 3, 7, 5):
                    block = w.p ^ k
                    ref = self.part(block, 1 - w.x)
                    self.got(ref, 8 + block)
                    self.hand(ref)
        else:
            for count in (14 * self.t, 14 * self.t) if split else (14 * self.e,):
                done = self.full.at[pl.ds(0, count)]
                remote(done, done, self.send, self.sib, w.sibling()).wait_send()
            came = self.full.at[pl.ds(0, 7 * self.e if split else 14 * self.t)]
            remote(came, came, self.send, self.sib, w.sibling()).wait_recv()


class Reduce:
    STAGES = 7

    def __init__(self, place, src, bufs, out, local, send, recv):
        self.w, self.src, self.out = place, src, out
        self.mine, self.cbuf, self.ybuf, self.zbuf, self.xbuf, self.fbuf = bufs
        self.rows = src.shape[0] // 8
        self.t, self.e = self.split(self.rows)
        self.local, self.send, self.recv = local, send, recv

    @staticmethod
    def split(rows):
        t = rows // 4 if rows % 64 == 0 else rows // 3
        return t, rows - 2 * t

    @classmethod
    def buffers(cls, rows, width):
        t, e = cls.split(rows)
        big = max(2 * t, e)
        sizes = (8 * big, 8 * big, 4 * max(t, e), 4 * max(t, e), 8 * t, max(t, e))
        return [pltpu.VMEM((n, width), BF) for n in sizes]

    def copy(self, src, dst, index, device):
        return remote(src, dst, self.send, self.recv.at[index], device)

    def took(self, ref, index):
        self.copy(ref, ref, index, self.w.sibling()).wait_recv()

    def rows_of(self, ref, first, count):
        return ref.at[pl.ds(pl.multiple_of(first, 16), count)]

    def add(self, target, *terms):
        def body(i, _):
            rows = pl.ds(pl.multiple_of(i * 32, 32), 32)
            if len(terms) == 1:
                target[rows] = target[rows] + terms[0][rows]
                return 0
            total = target[rows].astype(F32)
            for term in terms:
                total = total + term[rows].astype(F32)
            target[rows] = total.astype(BF)
            return 0

        lax.fori_loop(0, target.shape[0] // 32, body, 0)

    def each_core(self, first, second):
        pl.when(self.w.core == 0)(first)
        pl.when(self.w.core == 1)(second)

    def exchange(self, theirs, their_rows, ours, our_rows):
        def body(b, _):
            self.copy(
                self.rows_of(self.src, b * self.rows + theirs, their_rows),
                self.rows_of(self.cbuf, b * their_rows, their_rows),
                0,
                self.w.sibling(),
            ).start()
            pltpu.make_async_copy(
                self.rows_of(self.src, b * self.rows + ours, our_rows),
                self.rows_of(self.mine, b * our_rows, our_rows),
                self.local,
            ).start()
            return 0

        lax.fori_loop(0, 8, body, 0)

    def settle(self, count):
        whole = self.mine.at[pl.ds(0, 8 * count)]
        pltpu.make_async_copy(whole, whole, self.local).wait()
        self.took(self.cbuf.at[pl.ds(0, 8 * count)], 0)
        self.add(whole, self.cbuf)

    def zero_at(self, block, piece):
        return self.rows_of(self.mine, block * 2 * self.t + piece * self.t, self.t)

    def one_at(self, block):
        return self.rows_of(self.mine, block * self.e, self.e)

    def send_y(self, count, at):
        w = self.w

        def body(z, _):
            self.copy(at(2 * z + 1 - w.y), self.rows_of(self.ybuf, z * count, count), 2, w.over()).start()
            return 0

        lax.fori_loop(0, 4, body, 0)

    def take_y(self, count, at):
        self.took(self.ybuf.at[pl.ds(0, 4 * count)], 2)

        def body(z, _):
            self.add(at(2 * z + self.w.y), self.rows_of(self.ybuf, z * count, count))
            return 0

        lax.fori_loop(0, 4, body, 0)

    def send_z(self, count, at):
        w = self.w
        for k in (3, 1, 2):
            z = w.z ^ k
            self.copy(at(2 * z + w.y), self.rows_of(self.zbuf, k * count, count), 3, (w.g, 2 * z + w.y)).start()

    def take_z(self, count, at):
        self.took(self.zbuf.at[pl.ds(0, 3 * count)], 3)
        self.add(at(self.w.p), *[self.rows_of(self.zbuf, k * count, count) for k in (1, 2, 3)])

    def give(self, first, count, value):
        ref = self.out.at[pl.ds(pl.multiple_of(first, 8), count)]
        ref[...] = value
        remote(ref, ref, self.send, self.recv.at[5], self.w.sibling()).start()

    def stage(self, number):
        w, t, e = self.w, self.t, self.e
        x_mine = functools.partial(self.zero_at, piece=w.x)
        x_other = functools.partial(self.zero_at, piece=1 - w.x)
        if number == 0:
            self.each_core(lambda: self.exchange(2 * t, e, 0, 2 * t), lambda: self.exchange(0, 2 * t, 2 * t, e))
        elif number == 1:

            def first():
                self.settle(2 * t)

                def body(b, _):
                    self.copy(x_other(b), self.rows_of(self.xbuf, b * t, t), 1, w.across()).start()
                    return 0

                lax.fori_loop(0, 8, body, 0)

            def second():
                self.settle(e)
                self.send_y(e, self.one_at)

            self.each_core(first, second)
        elif number == 2:

            def first():
                self.took(self.xbuf, 1)

                def body(b, _):
                    self.add(x_mine(b), self.rows_of(self.xbuf, b * t, t))
                    return 0

                lax.fori_loop(0, 8, body, 0)
                self.send_y(t, x_mine)

            def second():
                self.take_y(e, self.one_at)
                self.send_z(e, self.one_at)

            self.each_core(first, second)
        elif number == 3:

            def first():
                self.take_y(t, x_mine)
                self.send_z(t, x_mine)

            def second():
                self.take_z(e, self.one_at)
                self.copy(self.one_at(w.p), self.fbuf.at[pl.ds(0, e)], 4, w.across()).start()

            self.each_core(first, second)
        elif number == 4:

            def first():
                self.take_z(t, x_mine)
                self.copy(x_mine(w.p), self.fbuf.at[pl.ds(0, t)], 4, w.across()).start()
                self.give(w.x * t, t, x_mine(w.p)[...].astype(F32))

            def second():
                self.took(self.fbuf.at[pl.ds(0, e)], 4)
                self.give(2 * t, e, self.one_at(w.p)[...].astype(F32) + self.fbuf[pl.ds(0, e)].astype(F32))

            self.each_core(first, second)
        elif number == 5:

            @pl.when(w.core == 0)
            def _():
                self.took(self.fbuf.at[pl.ds(0, t)], 4)
                self.give((1 - w.x) * t, t, self.fbuf[pl.ds(0, t)].astype(F32))

        else:

            def sent(count):
                while count > 0:
                    now = min(count, self.mine.shape[0])
                    part = self.mine.at[pl.ds(0, now)]
                    remote(part, part, self.send, self.recv.at[0], w.sibling()).wait_send()
                    count -= now

            def came(first, count):
                ref = self.out.at[pl.ds(first, count)]
                remote(ref, ref, self.send, self.recv.at[5], w.sibling()).wait_recv()

            def first():
                came(2 * t, e)
                sent(8 * e + 8 * t + 4 * t + 3 * t + t + 4 * t)

            def second():
                came(0, 2 * t)
                sent(16 * t + 4 * e + 3 * e + e + 2 * e)

            self.each_core(first, second)


class SmallSum:
    HOPS = (4, 2, 4)

    def __init__(self, place, value, bufs, send, recv):
        self.w, self.value, self.bufs, self.send, self.recv = place, value, bufs, send, recv

    def copies(self, hop):
        w = self.w
        for k in range(1, self.HOPS[hop]):
            device = ((w.g ^ k, w.p), (w.g, w.p ^ k), (w.g, w.p ^ (2 * k)))[hop]
            ref = self.bufs.at[4 * hop]
            yield remote(ref, self.bufs.at[4 * hop + k], self.send.at[hop, k], self.recv.at[hop, k], device)

    def stage(self, number):
        w = self.w
        if number > 0:
            hop = number - 1
            for copy in self.copies(hop):
                copy.wait()
            mine = (w.g, w.y, w.z)[hop]
            total = self.bufs[4 * hop + mine]
            for k in range(1, self.HOPS[hop]):
                total = total + self.bufs[4 * hop + (mine ^ k)]
        else:
            total = self.value[...]
        if number == 3:
            self.value[...] = total
        else:
            self.bufs[4 * number] = total
            for copy in self.copies(number):
                copy.start()


def mask_column(side_ref, image):
    side = side_of(side_ref, image)
    slot = lax.broadcasted_iota(jnp.int32, (SLOT, 1), 0)
    return jnp.where(slot < side * side, 0.0, MASK_FILL).astype(F32)


def head_pair(images, step):
    i, j = step % images, step // images
    rows = pl.ds(pl.multiple_of(i * SLOT, SLOT), SLOT)
    return i, rows, pl.multiple_of(j * 128, 128), pl.multiple_of((j // 2) * D + (j % 2) * 128, 128)


def attend_step(images, step, side_ref, qkv_ref, ctx_ref, lse_ref):
    i, rows, c, at = head_pair(images, step)
    q = qkv_ref[rows, pl.ds(at, 128)]
    k = qkv_ref[rows, pl.ds(at + THIRD, 128)]
    v = qkv_ref[rows, pl.ds(at + 2 * THIRD, 128)]
    lane = lax.broadcasted_iota(jnp.int32, (1, 128), 1)
    mask = mask_column(side_ref, i)
    outs, logs = [], []
    for h in range(2):
        qm = jnp.where(lane // HD == h, q, jnp.zeros_like(q))
        s = dot(k, qm, NT) * (LOG2E / math.sqrt(HD)) + mask
        top = jnp.max(s, axis=0, keepdims=True)
        e = jnp.exp2(s - top)
        total = jnp.sum(e, axis=0, keepdims=True)
        p = (e * (1.0 / total)).astype(BF)
        outs.append(dot(p, v, TN))
        logs.append(top + jnp.log2(total))
    ctx_ref[rows, pl.ds(c, 128)] = jnp.where(lane < HD, outs[0], outs[1]).astype(BF)
    lse_ref[step] = jnp.concatenate(logs + [jnp.zeros((6, SLOT), F32)], axis=0)


def norm_rows(images, x_ref, small, norm_ref):
    def body(step, _):
        rows = pl.ds(pl.multiple_of(step * 192, 192), 192)
        unit, _ = norm_stats(x_ref[rows])
        norm_ref[rows] = (unit * small[R_G1 : R_G1 + 1] + small[R_S1 : R_S1 + 1]).astype(BF)
        return 0

    lax.fori_loop(0, images * SLOT // 192, body, 0)


def angle_tables(images, side_ref, small, cos_ref, sin_ref):
    for j in range(D // 128):
        flat = [small[R_FR : R_FR + 1, n + j // 2 * 128 : n + j // 2 * 128 + 128] for n in (0, D // 2)]
        fc, fr = [dot(jnp.broadcast_to(v, (8, 128)).astype(BF), spread(j % 2), NN)[0:1] for v in flat]

        def body(i, _):
            rows = pl.ds(pl.multiple_of(i * SLOT, SLOT), SLOT)
            col, row, _ = patch_columns(side_ref, i)
            sn, cs = sincos(col * fc + row * fr)
            cos_ref[rows, pl.ds(j * 128, 128)] = cs
            sin_ref[rows, pl.ds(j * 128, 128)] = sn * -half_sign(128)
            return 0

        lax.fori_loop(0, images, body, 0)


def project_block(images, c, r, small, w_ref, norm_ref, qkv_ref, cos_ref, sin_ref):
    i, part = r % images, r // images
    rows = pl.ds(pl.multiple_of(i * SLOT, SLOT), SLOT)
    cols = pl.ds(pl.multiple_of(part * THIRD, THIRD), THIRD)
    lanes = pl.ds(pl.multiple_of(c * D + part * THIRD, THIRD), THIRD)
    inner = pl.ds(pl.multiple_of(c * THIRD, THIRD), THIRD)
    raw = dot(norm_ref[rows], w_ref[c, :, cols], NN) + small[pl.ds(R_QB + part, 1), inner]

    @pl.when(part < 2)
    def _():
        turned = raw * cos_ref[rows, inner] + swap_halves(raw) * sin_ref[rows, inner]
        qkv_ref[rows, lanes] = turned.astype(BF)

    @pl.when(part == 2)
    def _():
        qkv_ref[rows, lanes] = raw.astype(BF)


def forward_compute(images, side_ref, x_ref, small, w_ref, qkv, norm, cos, sin, ctx_ref, lse_ref, hooks):
    hooks("start")
    norm_rows(images, x_ref, small, norm)
    hooks("tables")
    angle_tables(images, side_ref, small, cos, sin)
    blocks, pairs = 3 * images, 2 * images

    def body(step, _):
        hooks("step", step)
        c, r = step // (blocks + pairs), step % (blocks + pairs)

        @pl.when(r < blocks)
        def _():
            project_block(images, c, r, small, w_ref, norm, qkv, cos, sin)

        @pl.when(r >= blocks)
        def _():
            attend_step(images, c * pairs + r - blocks, side_ref, qkv, ctx_ref, lse_ref)

        return 0

    lax.fori_loop(0, 3 * (blocks + pairs), body, 0)
    hooks("end")


def forward_plain(images, side_ref, x_ref, small_ref, w_ref, *refs):
    qkv, norm, cos, sin, ctx, lse = refs
    forward_compute(images, side_ref, x_ref, small_ref, w_ref, qkv, norm, cos, sin, ctx, lse, lambda *a: None)


def packed_places(p, dp, sizes):
    run = D // dp
    for first, size in zip(SMALL_ROWS, sizes):
        count = size // run
        yield [(first + (p * count + m) // dp, ((p * count + m) % dp) * run) for m in range(count)]


SMALL_ROWS = (R_G1, R_S1, R_QB, R_FR, R_OB, R_G2, R_S2, R_UB, R_DB)


SINGLES = (R_G1, R_S1, R_FR, R_OB, R_G2, R_S2, R_DB)
MORE = ((2, R_QB, 3, 8), (7, R_UB, 4, 11))


def compact(tinies, ref):
    run = tinies[0].shape[0]
    first = {row: i for i, row in enumerate(SMALL_ROWS)}
    for n, row in enumerate(SINGLES):
        ref[n, pl.ds(0, run)] = tinies[first[row]][...].astype(BF).astype(F32)
    for index, _, count, at in MORE:
        for m in range(count):
            ref[at + m, pl.ds(0, run)] = tinies[index][pl.ds(m * run, run)].astype(BF).astype(F32)


def expand(parts, small, run):
    small[...] = jnp.zeros_like(small)
    lane = lax.broadcasted_iota(jnp.int32, (1, 128), 1)
    total = None
    for owner, ref in parts:
        wide = jnp.concatenate([jnp.where(lane < run, ref[...], 0.0), jnp.zeros((R_ALL, D - 128), F32)], axis=1)
        term = pltpu.roll(wide[0:8], owner * run, 1)
        total = term if total is None else total + term
        for _, row, count, at in MORE:
            for m in range(count):
                place = owner * count + m
                moved = pltpu.roll(jnp.broadcast_to(wide[at + m : at + m + 1], (8, D)), (place % 8) * run, 1)
                small[pl.ds(row + place // 8, 1), :] += moved[0:1]
    for n, row in enumerate(SINGLES):
        small[row : row + 1] = total[n : n + 1]


def forward_gather(images, side_ref, *refs):
    tinies, x_in, shards_in = refs[0:9], refs[9], refs[10:14]
    qkv_out, norm_out, cos_out, sin_out, ctx, lse, small, wq_out, wo, wu, wd, up_later, down_later = refs[14:27]
    x_ref, qkv, norm, cos, sin, wq, slots, bq, bo, bu, bd, sq, so, su, sd = refs[27:42]
    sems, recv, psend, precv, local, ins = refs[42:]
    w = Place()
    pairs = [(bq.at[c], wq.at[c]) for c in range(3)] + [(bo, wo)]
    pairs += [(own.at[c], full.at[c]) for c in range(PARTS - 1) for own, full in ((bu, wu), (bd, wd))]
    gathers = dict(zip(("q0", "q1", "q2", "o", "u0", "d0", "u1", "d1"), pairs))
    gathers = {k: Gather(w, *v, sems, recv, i) for i, (k, v) in enumerate(gathers.items())}
    moves = Moves(gathers, FORWARD_PLAN)
    peers = [w.p ^ k for k in range(1, 8)]
    keep = {}

    def store(name, src, dst):
        keep[name] = load(src, dst, local.at[len(keep)])

    def qkv_third(c):
        lanes = pl.ds(c * D, D)
        return pltpu.make_async_copy(qkv.at[:, lanes], qkv_out.at[:, lanes], local.at[16 + c])

    def late(number):
        src, dst = ((cos, cos_out), (sin, sin_out), (wq, wq_out))[number]
        return pltpu.make_async_copy(src, dst, local.at[19 + number])

    def own_rows(full):
        count = full.shape[0] // 8
        return full.at[pl.ds(pl.multiple_of(w.p * count, 16), count)]

    def pack_copy(k):
        return remote(slots.at[0], slots.at[k], psend.at[k - 1], precv.at[k - 1], (w.g, peers[k - 1]))

    def hooks(where, step=None):
        if where == "start":
            reads = [
                load(src, dst, ins.at[i])
                for i, (src, dst) in enumerate(zip(shards_in[:1] + (x_in,) + shards_in[1:], (sq, x_ref, so, su, sd)))
            ]
            compact(tinies, slots.at[0])
            greet([(w.g, q) for q in peers] + [w.sibling(), w.across()])
            for k in range(1, 8):
                pack_copy(k).start()
            reads[0].wait()
            for c in range(3):
                for part in range(3):
                    cols = part * D + c * THIRD
                    bq[c, :, part * THIRD : (part + 1) * THIRD] = sq[:, cols : cols + THIRD].astype(BF)
                if c == 0:
                    moves.at(-1)
            for copy in reads[1:]:
                copy.wait()
            bo[...] = so[...].astype(BF)
            for c in range(PARTS):
                for b in range(8):
                    cols = (b * PARTS + c) * 128
                    bu[c, :, b * 128 : (b + 1) * 128] = su[:, cols : cols + 128].astype(BF)
                bd[c] = sd[c * 128 : (c + 1) * 128].astype(BF)
            for i, (own, full) in enumerate(pairs):
                store(i, own, own_rows(full))
            store("up", bu.at[PARTS - 1], up_later)
            store("down", bd.at[PARTS - 1], down_later)
            for k in range(1, 8):
                pack_copy(k).wait()
            expand([(w.p, slots.at[0])] + [(peers[k - 1], slots.at[k]) for k in range(1, 8)], small, D // 8)
            moves.at(0)
        elif where == "tables":
            moves.at(1)
            store("norm", norm, norm_out)
        elif where == "step":

            @pl.when(step == 0)
            def _():
                for i in range(3):
                    keep[i].wait()
                for number in (0, 1):
                    late(number).start()

            moves.within(step + 2, 2, 31)
            for c in (1, 2):

                @pl.when(step == 10 * c)
                def _(c=c):
                    qkv_third(c - 1).start()
                    if c == 2:
                        late(2).start()

        else:
            qkv_third(2).start()
            moves.at(32)
            for c in range(3):
                qkv_third(c).wait()
                late(c).wait()
            for name, copy in keep.items():
                if name not in (0, 1, 2):
                    copy.wait()

    forward_compute(images, side_ref, x_ref, small, wq, qkv, norm, cos, sin, ctx, lse, hooks)


FORWARD_PLAN = {
    "q0": (-1, 1, 2, 2, 2),
    "q1": (0, 2, 9, 11, 12),
    "q2": (1, 4, 10, 16, 19),
    "o": (1, 7, 14, 29, 31),
    "u0": (3, 11, 17, 25, 26),
    "d0": (5, 16, 21, 27, 31),
    "u1": (17, 21, 28, 31, 32),
    "d1": (10, 16, 24, 30, 31),
}


def bias_at(split, step):
    c, k = step // BLOCKS, step % BLOCKS
    if split:
        return (R_UB + k, c * 128), (R_UB + k, D // 2 + c * 128)
    return (R_UB + step // 3, (step % 3) * 256), (R_UB + step // 3, (step % 3) * 256 + 128)


def mlp_compute(images, split, side_ref, scale, cot_ref, ctx_ref, small, wo_ref, wu, wd, refs, outs, hooks):
    mid, n2, n2t, bl, hid, gpre, ubias, gubias = refs
    act, gm, gctx, gdown, gup, gout, gs = outs
    rows_all = images * SLOT
    tile = SLOT // 2
    hooks("start")
    gain = small[R_G2 : R_G2 + 1]
    gs[...] = jnp.zeros_like(gs)
    for step in range(PARTS * BLOCKS):
        for n, (r, l) in enumerate(bias_at(split, step)):
            ubias[step : step + 1, n * 128 : (n + 1) * 128] = small[r : r + 1, l : l + 128]

    def tile_rows(step):
        side = side_of(side_ref, step // 2)
        slot = lax.broadcasted_iota(jnp.int32, (tile, 1), 0) + (step % 2) * tile
        return pl.ds(pl.multiple_of(step * tile, tile), tile), slot < side * side

    def enter(step, _):
        hooks("enter", step)
        rows, valid = tile_rows(step)
        middle = mid[rows] + (dot(ctx_ref[rows], wo_ref[...], NN) + small[R_OB : R_OB + 1])
        mid[rows] = middle
        act[rows] = middle + small[R_DB : R_DB + 1]
        unit, _ = norm_stats(middle)
        n2[rows] = (unit * gain + small[R_S2 : R_S2 + 1]).astype(BF)
        low = jnp.where(valid, cot_ref[rows], 0.0).astype(BF)
        bl[rows] = low
        gs[R_DB : R_DB + 1] += jnp.sum(low.astype(F32), axis=0, keepdims=True)
        return 0

    lax.fori_loop(0, 2 * images, enter, 0)
    gm[...] = jnp.zeros_like(gm)
    n2t[...] = n2[...].T
    hooks("entered")

    first = pl.ds(0, 256)
    hid[:, first] = jnp.zeros((rows_all, 256), BF)
    gpre[:, first] = jnp.zeros((rows_all, 256), BF)

    def weights(step):
        c = step // BLOCKS
        cols = pl.ds(pl.multiple_of((step % BLOCKS) * 256, 256), 256)
        gdown[c, cols, :] = (dot(hid[:, cols], bl[...], TN) * scale).astype(BF)
        gup[c, :, cols] = (dot(n2t[...], gpre[:, cols], NN) * scale).astype(BF)

    def block(step, _):
        hooks("block", step)
        c, k = step // BLOCKS, step % BLOCKS
        cols = pl.ds(pl.multiple_of(k * 256, 256), 256)
        bias = ubias[pl.ds(step, 1), :]
        wuc = wu[c, :, cols]
        wdc = wd[c, cols, :]
        weights(jnp.maximum(step - 1, 0))
        pieces = [pl.ds(i * tile, tile) for i in range(2 * images)]
        pres = [dot(n2[rows], wuc, NN) + bias for rows in pieces]
        backs = [dot(bl[rows], wdc, NT) for rows in pieces]
        bsum = None
        for rows, pre, back in zip(pieces, pres, backs):
            value, slope = gelu_pair(pre)
            hid[rows, cols] = value.astype(BF)
            g = (back * slope).astype(BF)
            gpre[rows, cols] = g
            part = jnp.sum(g.astype(F32), axis=0, keepdims=True)
            bsum = part if bsum is None else bsum + part
        gubias[pl.ds(step, 1), :] = bsum

        @pl.when(k == BLOCKS - 1)
        def _():
            def tail(n, _):
                rows = pl.ds(pl.multiple_of(n * SLOT, SLOT), SLOT)
                act[rows] += dot(hid[rows], wd[c], NN)
                gm[rows] += dot(gpre[rows], wu[c], NT)
                return 0

            lax.fori_loop(0, images, tail, 0)

        return 0

    lax.fori_loop(0, PARTS * BLOCKS, block, 0)
    weights(PARTS * BLOCKS - 1)
    hooks("blocks")

    def leave(step, _):
        rows, valid = tile_rows(step)
        unit, inv = norm_stats(mid[rows])
        act[rows] = jnp.where(valid, act[rows], 0.0)
        gn = gm[rows]
        gs[R_G2 : R_G2 + 1] += jnp.sum(gn * unit, axis=0, keepdims=True)
        gs[R_S2 : R_S2 + 1] += jnp.sum(gn, axis=0, keepdims=True)
        a = gn * gain
        ma = jnp.mean(a, axis=-1, keepdims=True)
        mu = jnp.mean(a * unit, axis=-1, keepdims=True)
        g = jnp.where(valid, cot_ref[rows], 0.0) + inv * (a - ma - unit * mu)
        gm[rows] = g
        low = g.astype(BF)
        bl[rows] = low
        gs[R_OB : R_OB + 1] += jnp.sum(low.astype(F32), axis=0, keepdims=True)
        gctx[rows] = dot(low, wo_ref[...], NT).astype(BF)
        hooks("left", step)
        return 0

    lax.fori_loop(0, 2 * images, leave, 0)
    for step in range(PARTS * BLOCKS):
        for n, (r, l) in enumerate(bias_at(split, step)):
            gs[r : r + 1, l : l + 128] = gubias[step : step + 1, n * 128 : (n + 1) * 128]
    gout[...] = (dot(ctx_ref[...], bl[...], TN) * scale).astype(BF)
    gs[...] = gs[...] * scale
    hooks("end")


def mlp_scratch(rows):
    vmem = pltpu.VMEM
    return (
        [vmem((rows, D), F32), vmem((rows, D), BF), vmem((D, rows), BF), vmem((rows, D), BF)]
        + [vmem((rows, FF // PARTS), BF)] * 2
        + [vmem((16, 256), F32)] * 2
    )


def mlp_plain(images, slots, side_ref, assign_ref, counts_ref, x_ref, cot_ref, ctx_ref, small, wo_ref, wu, wd, *rest):
    outs, refs, sem = rest[0:7], rest[7:15], rest[15]
    load(x_ref, refs[0], sem.at[0]).wait()
    mlp_compute(
        images, False, side_ref, device_weight(slots, assign_ref, counts_ref), cot_ref, ctx_ref, small, wo_ref, wu, wd, refs, outs, lambda *a: None
    )


def mlp_moving(images, slots, side_ref, assign_ref, counts_ref, small, *rest):
    x_in, cot_in, ctx_in, wo_in, wu_in, wd_in, up_later, down_later = rest[0:8]
    act_out, gm_out, gctx_out, gd_out, gu_out, go_out, gs, rd, ru = rest[8:17]
    refs = rest[17:25]
    mid, n2, n2t = refs[0], refs[1], refs[2]
    cot, ctx, wo, wu, wd, act, gm, gd, gu = rest[25:34]
    bufs, (local, sems, recv, rlocal, rsend, rrecv, tile_in, tile_out) = rest[34:46], rest[46:54]
    w = Place()
    last = PARTS - 1
    items = {
        "u": Gather(w, up_later, wu.at[last], sems, recv, 0),
        "d": Gather(w, down_later, wd.at[last], sems, recv, 1),
        "rd": Reduce(w, gd.at[0], bufs[0:6], rd, rlocal.at[0], rsend.at[0], rrecv.at[0]),
        "ru": Reduce(w, gu.at[0], bufs[6:12], ru, rlocal.at[1], rsend.at[1], rrecv.at[1]),
    }
    moves = Moves(items, MLP_PLAN)
    keep = []

    def move(src, dst):
        keep.append(load(src, dst, local.at[len(keep)]))
        return keep[-1]

    tile = SLOT // 2

    def by_tile(step, pairs, sem):
        rows = pl.ds(pl.multiple_of(step * tile, tile), tile)
        return [pltpu.make_async_copy(src.at[rows], dst.at[rows], sem.at[i, step]) for i, (src, dst) in enumerate(pairs)]

    def arriving(step):
        return by_tile(step, ((ctx_in, ctx), (x_in, mid), (cot_in, cot)), tile_in)

    def leaving(step):
        return by_tile(step, ((act, act_out), (gm, gm_out), (n2, gctx_out)), tile_out)

    def hooks(where, step=None):
        if where == "start":
            move(wo_in, wo)
            for i in range(2 * images):
                for copy in arriving(i):
                    copy.start()
            for c in range(last):
                move(wu_in.at[c], wu.at[c])
                move(wd_in.at[c], wd.at[c])
            for own, full in ((up_later, wu), (down_later, wd)):
                count = full.shape[1] // 8
                move(own, full.at[last, pl.ds(pl.multiple_of(w.p * count, 16), count)])
            greet(w.partners())
            moves.at(0)
            keep[0].wait()
        elif where == "enter":
            for copy in arriving(step):
                copy.wait()
        elif where == "left":
            for copy in leaving(step):
                copy.start()
        elif where == "entered":
            for copy in keep[1:]:
                copy.wait()
            keep.clear()
        elif where == "block":
            moves.within(step + 1, 1, 12)
        elif where == "blocks":
            for c in (1, 2):
                move(gd.at[c], gd_out.at[c - 1])
                move(gu.at[c], gu_out.at[c - 1])
            moves.at(13)
        else:
            move(n2t.at[:, pl.ds(0, D)], go_out)
            moves.at(14)
            for i in range(2 * images):
                for copy in leaving(i):
                    copy.wait()
            for copy in keep:
                copy.wait()

    mlp_compute(
        images,
        True,
        side_ref,
        device_weight(slots, assign_ref, counts_ref),
        cot,
        ctx,
        small,
        wo,
        wu,
        wd,
        refs,
        (act, gm, n2, gd, gu, n2t.at[:, pl.ds(0, D)], gs),
        hooks,
    )


MLP_PLAN = {
    "u": (0, 2, 4, 5, 7),
    "d": (1, 4, 5, 7, 8),
    "rd": (6, 8, 10, 12, 13, 14, 14),
    "ru": (6, 7, 9, 11, 13, 14, 14),
}


PARTS = 3
BLOCKS = 4


def attend_back_step(images, step, side_ref, qkv_ref, gctx_ref, lse_ref, cos_ref, sin_ref, gproj_ref, gs_ref, gf_ref):
    i, rows, c, at = head_pair(images, step)
    q = qkv_ref[rows, pl.ds(at, 128)]
    k = qkv_ref[rows, pl.ds(at + THIRD, 128)]
    v = qkv_ref[rows, pl.ds(at + 2 * THIRD, 128)]
    go = gctx_ref[rows, pl.ds(c, 128)]
    lane = lax.broadcasted_iota(jnp.int32, (1, 128), 1)
    mask = mask_column(side_ref, i)
    lse = lse_ref[step]
    dq, dk, dv = [], [], []
    for h in range(2):
        mine = lane // HD == h
        qm = jnp.where(mine, q, jnp.zeros_like(q))
        gom = jnp.where(mine, go, jnp.zeros_like(go))
        s = dot(k, qm, NT) * (LOG2E / math.sqrt(HD)) + mask
        p = jnp.exp2(s - lse[h : h + 1])
        dp = dot(v, gom, NT)
        dv.append(dot(p.astype(BF), go, NN))
        t = p * dp
        ds = (t - p * jnp.sum(t, axis=0, keepdims=True)).astype(BF)
        dk.append(dot(ds, q, NN))
        dq.append(dot(ds, k, TN))
    first = lane < HD
    cs = cos_ref[rows, pl.ds(c, 128)]
    sn = sin_ref[rows, pl.ds(c, 128)]
    angle = None
    for n, (pair, rot) in enumerate(((dq, q), (dk, k))):
        e = jnp.where(first, pair[0], pair[1]) * (1.0 / math.sqrt(HD))
        other = swap_halves(e)
        back = (e * cs - other * sn).astype(BF)
        gproj_ref[rows, pl.ds(at + n * THIRD, 128)] = back
        gs_ref[pl.ds(R_QB + n, 1), pl.ds(c, 128)] += jnp.sum(back.astype(F32), axis=0, keepdims=True)
        term = rot.astype(F32) * other
        angle = term if angle is None else angle + term
    gv = jnp.where(first, dv[0], dv[1]).astype(BF)
    gproj_ref[rows, pl.ds(at + 2 * THIRD, 128)] = gv
    gs_ref[R_QB + 2 : R_QB + 3, pl.ds(c, 128)] += jnp.sum(gv.astype(F32), axis=0, keepdims=True)
    angle = angle * half_sign(128)
    col, row, _ = patch_columns(side_ref, i)
    gf_ref[0:1, pl.ds(c, 128)] += jnp.sum(angle * col, axis=0, keepdims=True)
    gf_ref[1:2, pl.ds(c, 128)] += jnp.sum(angle * row, axis=0, keepdims=True)


def freq_row(gf_ref, gs_ref):
    for m in range(D // 128):
        which = m // 3
        total = None
        for parity in (0, 1):
            lanes = 2 * (m % 3) + parity
            value = gf_ref[which : which + 1, lanes * 128 : lanes * 128 + 128]
            for _ in range(3):
                term = value.astype(BF)
                value = value - term.astype(F32)
                moved = dot(jnp.broadcast_to(term, (8, 128)), spread(parity), NT)[0:1]
                total = moved if total is None else total + moved
        gs_ref[R_FR : R_FR + 1, m * 128 : m * 128 + 128] = total


def weight_third(c, scale, norm_ref, gproj_ref, gw_ref):
    def block(j, _):
        lanes = pl.ds(pl.multiple_of(j * THIRD, THIRD), THIRD)
        full = pl.ds(pl.multiple_of(c * D + j * THIRD, THIRD), THIRD)
        gw_ref[:, lanes] = (dot(norm_ref[...], gproj_ref[:, full], TN) * scale).astype(BF)
        return 0

    lax.fori_loop(0, 3, block, 0)


def attend_back_compute(images, thirds, side_ref, scale, ins, norm, gproj, gws, gs_ref, gf_ref, hooks):
    hooks("start")
    gs_ref[...] = jnp.zeros_like(gs_ref)
    gf_ref[...] = jnp.zeros_like(gf_ref)

    def body(step, _):
        hooks("step", step)
        attend_back_step(images, step, side_ref, *ins, gproj, gs_ref, gf_ref)
        for c in range(thirds):

            @pl.when(step == 2 * images * (c + 1) - 1)
            def _(c=c):
                weight_third(c, scale, norm, gproj, gws.at[c])

        return 0

    lax.fori_loop(0, images * HEADS // 2, body, 0)
    freq_row(gf_ref, gs_ref)
    hooks("end")


def attend_back_plain(images, slots, side_ref, assign_ref, counts_ref, *refs):
    ins, norm, (gproj, gws, gs, gf) = refs[0:5], refs[5], refs[6:10]
    attend_back_compute(images, 3, side_ref, device_weight(slots, assign_ref, counts_ref), ins, norm, gproj, gws, gs, gf, lambda *a: None)


def qkv_back_compute(images, x_ref, gproj_ref, gm_ref, small_ref, w_ref, gs_in, gin_ref, gs_ref, hooks):
    hooks("start")
    gain = small_ref[R_G1 : R_G1 + 1]
    gs_ref[...] = gs_in[...]
    tile = SLOT // 2

    def body(step, _):
        hooks("tile", step)
        rows = pl.ds(pl.multiple_of(step * tile, tile), tile)
        unit, inv = norm_stats(x_ref[rows])
        gn = None
        for c in range(3):
            term = dot(gproj_ref[rows, c * D : (c + 1) * D], w_ref[c][...], NT)
            gn = term if gn is None else gn + term
        gs_ref[R_G1 : R_G1 + 1] += jnp.sum(gn * unit, axis=0, keepdims=True)
        gs_ref[R_S1 : R_S1 + 1] += jnp.sum(gn, axis=0, keepdims=True)
        a = gn * gain
        ma = jnp.mean(a, axis=-1, keepdims=True)
        mu = jnp.mean(a * unit, axis=-1, keepdims=True)
        gin_ref[rows] = gm_ref[rows] + inv * (a - ma - unit * mu)
        return 0

    lax.fori_loop(0, 2 * images, body, 0)
    hooks("end")


def qkv_back_plain(images, slots, assign_ref, counts_ref, x_ref, gproj_ref, gm_ref, small_ref, w_ref, gs_in, gin, gs):
    def hooks(where, index=None):
        if where == "end":
            gs[...] = gs[...] * device_weight(slots, assign_ref, counts_ref)

    parts = [w_ref.at[c] for c in range(3)]
    qkv_back_compute(images, x_ref, gproj_ref, gm_ref, small_ref, parts, gs_in, gin, gs, hooks)


def backward_reduce(images, slots, side_ref, assign_ref, counts_ref, small_ref, gs_mlp, *refs):
    ins_in, (gd, gu, go), (x_in, gm_in, w_in) = refs[0:6], refs[6:9], refs[9:12]
    gin_out, gs, outs = refs[12], refs[13], refs[14:22]
    ins, gproj, gws, gf, gs_own = refs[22:28], refs[28], refs[29], refs[30], refs[31]
    bufs, tinybufs, (loads, local, send, recv, ssend, srecv) = refs[32:80], refs[80], refs[81:87]
    qkv, cos, sin, norm = ins[0], ins[3], ins[4], ins[5]
    w = Place()
    weight = device_weight(slots, assign_ref, counts_ref)
    srcs = (gd.at[0], gu.at[0], gd.at[1], gu.at[1], go, gws.at[0], gws.at[1], gws.at[2])
    items = {
        name: Reduce(w, srcs[i], bufs[6 * i : 6 * i + 6], outs[i], local.at[i], send.at[i], recv.at[i])
        for i, name in enumerate(BACK_PLAN)
    }
    moves = Moves(items, BACK_PLAN)
    tiny = SmallSum(w, gs, tinybufs, ssend, srecv)

    def third(c):
        copies = []
        for i, width in ((0, D), (1, THIRD), (3, THIRD), (4, THIRD)):
            lanes = pl.ds(c * width, width)
            copies.append(pltpu.make_async_copy(ins_in[i].at[:, lanes], ins[i].at[:, lanes], loads.at[c, i]))
        whole = {0: 2, 1: 5}.get(c)
        if whole is not None:
            copies.append(pltpu.make_async_copy(ins_in[whole], ins[whole], loads.at[c, 5]))
        return copies

    def hooks(where, step=None):
        if where == "start":
            for c in range(3):
                for copy in third(c):
                    copy.start()
            greet(w.partners() + [(w.g ^ 3, w.p)])
            moves.at(0)
            for copy in third(0):
                copy.wait()
        elif where == "step":
            for c, when in ((1, 2 * images - 1), (2, 4 * images)):

                @pl.when(step == when)
                def _(c=c):
                    for copy in third(c):
                        copy.wait()

            moves.within(step + 1, 1, 12)

    attend_back_compute(images, 3, side_ref, weight, ins[0:5], norm, gproj, gws, gs_own, gf, hooks)
    copies = [load(x_in, cos, loads.at[0, 0]), load(gm_in, sin, loads.at[0, 1])]
    wide = [qkv.at[pl.ds(0, D), pl.ds(c * D, D)] for c in range(3)]
    copies += [load(w_in.at[c], wide[c], loads.at[0, 2 + c]) for c in range(3)]
    moves.at(13)
    for copy in copies:
        copy.wait()

    def tiles(where, step=None):
        if where == "tile":
            moves.within(step + 14, 14, 17)

    qkv_back_compute(images, cos, gproj, sin, small_ref, wide, gs_own, sin, gs, tiles)
    copy = load(sin, gin_out, loads.at[0, 0])
    gs[...] = gs[...] * weight + gs_mlp[...]
    for number in range(4):
        tiny.stage(number)
        moves.at(18 + number)
    copy.wait()


BACK_PLAN = {
    "d1": (1, 3, 6, 9, 17, 19, 19),
    "u1": (1, 7, 11, 14, 18, 19, 21),
    "d2": (2, 4, 6, 9, 13, 15, 19),
    "u2": (2, 5, 8, 11, 14, 18, 20),
    "o": (0, 4, 7, 13, 16, 18, 21),
    "q0": (6, 7, 11, 15, 18, 19, 20),
    "q1": (9, 10, 14, 16, 18, 19, 20),
    "q2": (13, 14, 17, 18, 19, 20, 21),
}


def finish_kernel(dp, p_axis, gs, act_in, gin_in, rout_in, *refs):
    rd, ru, rq = refs[0:3], refs[3:6], refs[6:9]
    act, gin, rqkv, rout, rup, rdown, sems = refs[9], refs[10], *refs[11:15], refs[-1]
    tinies = refs[15:-2]
    stage = refs[-2]
    ins = [load(act_in, stage.at[0], sems.at[0]), load(gin_in, stage.at[1], sems.at[1])]
    p = lax.axis_index(p_axis)
    run = D // dp
    for out, places in zip(tinies, packed_places(p, dp, [t.shape[0] for t in tinies])):
        for m, (row, lane) in enumerate(places):
            whole = jnp.broadcast_to(gs[pl.ds(row, 1), :], (8, D))
            out[pl.ds(m * run, run)] = pltpu.roll(whole, D - lane, 1)[0, :run]
    copies = []
    for n, dst in enumerate((act, gin)):
        ins[n].wait()
        copies.append(load(stage.at[n], dst, sems.at[n]))
    rout[...] = rout_in[...]
    for c in range(3):
        rdown[c * rd[c].shape[0] : (c + 1) * rd[c].shape[0]] = rd[c][...]
        for b in range(dp):
            rup[:, (b * 3 + c) * 128 : (b * 3 + c + 1) * 128] = ru[c][:, b * 128 : (b + 1) * 128]
        for part in range(3):
            cols = part * D + c * THIRD
            rqkv[:, cols : cols + THIRD] = rq[c][:, part * THIRD : (part + 1) * THIRD]
    for copy in copies:
        copy.wait()


def params(mb=56):
    return pltpu.CompilerParams(vmem_limit_bytes=mb << 20)


def place_rows(p, dp, vec):
    n = vec.shape[0]
    whole = jnp.tile(vec, dp)
    owner = jnp.arange(n * dp, dtype=jnp.int32) // n
    return jnp.where(owner == p, whole, 0.0).reshape(-1, D)


def on_device(
    fast,
    images,
    cotangent,
    resolution,
    assignment,
    counts,
    ln1_gain,
    ln1_shift,
    qkv_weight,
    qkv_bias,
    rope_freqs,
    out_weight,
    out_bias,
    ln2_gain,
    ln2_shift,
    up_weight,
    up_bias,
    down_weight,
    down_bias,
):
    p = lax.axis_index("dp")
    dp = lax.axis_size("dp")
    n = images.shape[0]
    rows = n * SLOT
    x = images.reshape(rows, D)
    cot = cotangent.reshape(rows, D)
    vectors = (ln1_gain, ln1_shift, qkv_bias, rope_freqs, out_bias, ln2_gain, ln2_shift, up_bias, down_bias)
    slots = dp * rows
    sds = jax.ShapeDtypeStruct
    smem = pl.BlockSpec(memory_space=pltpu.SMEM)
    anyw = pl.BlockSpec(memory_space=pl.ANY)
    kept = [
        sds((rows, 3 * D), BF),
        sds((rows, D), BF),
        sds((rows, D), F32),
        sds((rows, D), F32),
        sds((rows, D), BF),
        sds((n * HEADS // 2, 8, SLOT), F32),
    ]
    weights = (qkv_weight, out_weight, up_weight, down_weight)
    dma = pltpu.SemaphoreType.DMA
    vmem = pltpu.VMEM

    def moving(number, mb):
        return pltpu.CompilerParams(vmem_limit_bytes=mb << 20, collective_id=number, has_side_effects=True)

    part = FF // PARTS
    if fast:
        later = [sds((D // dp, part), BF), sds((part // dp, D), BF)]
        fulls = [sds((3, D, D), BF), sds((D, D), BF), sds((PARTS - 1, D, part), BF), sds((PARTS - 1, part, D), BF)]
        outs = pl.pallas_call(
            functools.partial(forward_gather, n),
            out_shape=kept + [sds((R_ALL, D), F32)] + fulls + later,
            in_specs=[smem] + vm(9) + [anyw] * 5,
            out_specs=[anyw] * 4 + vm(3) + [anyw] * 6,
            scratch_shapes=[
                vmem((rows, D), F32),
                vmem((rows, 3 * D), BF),
                vmem((rows, D), BF),
                vmem((rows, D), F32),
                vmem((rows, D), F32),
                vmem((3, D, D), BF),
                vmem((8, R_ALL, 128), F32),
                vmem((3, D // dp, D), BF),
                vmem((D // dp, D), BF),
                vmem((PARTS, D // dp, part), BF),
                vmem((PARTS, part // dp, D), BF),
            ]
            + [vmem(v.shape, F32) for v in weights]
            + [
                dma((16,)),
                dma((8, 16)),
                dma((7,)),
                dma((7,)),
                dma((22,)),
                dma((5,)),
            ],
            compiler_params=moving(0, 56),
            name="forward",
        )(resolution, *vectors, x, *weights)
        qkv, norm1, cos, sin, ctx, lse, small, wqkv, wo, wu, wd, up_later, down_later = outs
    else:
        packed = [place_rows(p, dp, lax.reduce_precision(v, 8, 7)) for v in vectors]
        small = lax.psum(jnp.concatenate(packed + [jnp.zeros((2, D), F32)], axis=0), "dp")
        wqkv, wo, wu, wd = [lax.all_gather(v.astype(BF), "dp", axis=0, tiled=True) for v in weights]
        wqkv = wqkv.reshape(D, 3, 3, THIRD).transpose(2, 0, 1, 3).reshape(3, D, D)
        wu = wu.reshape(D, PARTS, part).transpose(1, 0, 2)
        wd = wd.reshape(PARTS, part, D)
        qkv, norm1, cos, sin, ctx, lse = pl.pallas_call(
            functools.partial(forward_plain, n),
            out_shape=kept,
            in_specs=[smem] + vm(3),
            out_specs=vm(6),
            compiler_params=params(),
            name="forward",
        )(resolution, x, small, wqkv)

    grads = [sds((PARTS, part, D), BF), sds((PARTS, D, part), BF), sds((D, D), BF)]
    rest = [sds((R_ALL, D), F32)]
    firsts = [sds((rows, D), F32), sds((rows, D), F32), sds((rows, D), BF)]
    tables = [vmem((rows, 3 * D), BF), vmem((rows, D), BF), vmem((n * HEADS // 2, 8, SLOT), F32)]
    tables += [vmem((rows, D), F32)] * 2
    gproj_shape = sds((rows, 3 * D), BF)
    if fast:
        sizes = [(part // dp, D), (D // dp, part)]
        act, gm, gctx, gdown, gup, gout, gs_mlp, rdown0, rup0 = pl.pallas_call(
            functools.partial(mlp_moving, n, slots),
            out_shape=firsts
            + [sds((PARTS - 1,) + g.shape[1:], BF) for g in grads[:2]]
            + grads[2:]
            + rest
            + [sds(z, F32) for z in sizes],
            in_specs=[smem] * 3 + vm(1) + [anyw] * 8,
            out_specs=[anyw] * 6 + vm(3),
            scratch_shapes=mlp_scratch(rows)
            + [
                vmem((rows, D), F32),
                vmem((rows, D), BF),
                vmem((D, D), BF),
                vmem((PARTS, D, part), BF),
                vmem((PARTS, part, D), BF),
                vmem((rows, D), F32),
                vmem((rows, D), F32),
                vmem((PARTS, part, D), BF),
                vmem((PARTS, D, part), BF),
            ]
            + sum([Reduce.buffers(*z) for z in sizes], [])
            + [dma((12,)), dma((4,)), dma((2, 16)), dma((2,)), dma((2,)), dma((2, 6))]
            + [dma((3, 2 * n))] * 2,
            compiler_params=moving(3, 63),
            name="mlp",
        )(resolution, assignment, counts, small, x, cot, ctx, wo, wu, wd, up_later, down_later)
        third = (D // dp, D)
        sizes = sizes + sizes + [third] * 4
        gin, gs, rdown1, rup1, rdown2, rup2, rout, rq0, rq1, rq2 = pl.pallas_call(
            functools.partial(backward_reduce, n, slots),
            out_shape=[sds((rows, D), F32)] + rest + [sds(z, F32) for z in sizes],
            in_specs=[smem] * 3 + vm(2) + [anyw] * 12,
            out_specs=[anyw] + vm(9),
            scratch_shapes=tables
            + [vmem((rows, D), BF), vmem((rows, 3 * D), BF), vmem((3, D, D), BF), vmem((8, D), F32)]
            + [vmem((R_ALL, D), F32)]
            + sum([Reduce.buffers(*z) for z in sizes], [])
            + [vmem((12, R_ALL, D), F32), dma((3, 6)), dma((8,)), dma((8,)), dma((8, 6)), dma((3, 4)), dma((3, 4))],
            compiler_params=moving(1, 62),
            name="backward",
        )(resolution, assignment, counts, small, gs_mlp, qkv, gctx, lse, cos, sin, norm1, gdown, gup, gout, x, gm, wqkv)

        matrices = (qkv_weight, out_weight, up_weight, down_weight)
        act, gin, rqkv, rout, rup, rdown, *tinies = pl.pallas_call(
            functools.partial(finish_kernel, dp, "dp"),
            out_shape=[sds((rows, D), F32)] * 2 + [sds(v.shape, F32) for v in matrices + vectors],
            in_specs=vm(1) + [anyw] * 2 + vm(10),
            out_specs=[anyw] * 2 + vm(13),
            scratch_shapes=[vmem((2, rows, D), F32), dma((2,))],
            compiler_params=params(),
            name="finish",
        )(gs, act, gin, rout, rdown0, rdown1, rdown2, rup0, rup1, rup2, rq0, rq1, rq2)
    else:
        act, gm, gctx, gdown, gup, gout, gs_mlp = pl.pallas_call(
            functools.partial(mlp_plain, n, slots),
            out_shape=firsts + grads + rest,
            in_specs=[smem] * 3 + [anyw] + vm(6),
            out_specs=vm(7),
            scratch_shapes=mlp_scratch(rows) + [dma((1,))],
            compiler_params=params(63),
            name="mlp",
        )(resolution, assignment, counts, x, cot, ctx, small, wo, wu, wd)
        gproj, gqkv, gs_att = pl.pallas_call(
            functools.partial(attend_back_plain, n, slots),
            out_shape=[gproj_shape, sds((3, D, D), BF)] + rest,
            in_specs=[smem] * 3 + vm(6),
            out_specs=vm(3),
            scratch_shapes=[vmem((8, D), F32)],
            compiler_params=params(),
            name="attend_back",
        )(resolution, assignment, counts, qkv, gctx, lse, cos, sin, norm1)
        gin, gs_qkv = pl.pallas_call(
            functools.partial(qkv_back_plain, n, slots),
            out_shape=[sds((rows, D), F32)] + rest,
            in_specs=[smem] * 2 + vm(6),
            out_specs=vm(2),
            compiler_params=params(),
            name="project_back",
        )(assignment, counts, x, gproj, gm, small, wqkv, gs_att)

        def reduce(g):
            total = lax.psum_scatter(g, "dp", scatter_dimension=0, tiled=True)
            return lax.psum(total, "group").astype(F32)

        gqkv = gqkv.reshape(3, D, 3, THIRD).transpose(1, 2, 0, 3).reshape(D, 3 * D)
        gup = gup.transpose(1, 0, 2).reshape(D, FF)
        rqkv, rout, rup, rdown = [reduce(g) for g in (gqkv, gout, gup, gdown.reshape(FF, D))]
        gs = lax.psum(gs_mlp + gs_qkv, ("group", "dp"))

        def own(first, count):
            flat = gs[first : first + count].reshape(dp, -1)
            return lax.dynamic_index_in_dim(flat, p, 0, keepdims=False)

        tinies = [own(first, v.shape[0] * dp // D) for first, v in zip(SMALL_ROWS, vectors)]

    g1, s1, qb, fr, ob, g2, s2, ub, db = tinies
    act, gin = act.reshape(images.shape), gin.reshape(images.shape)
    return (act, gin, g1, s1, rqkv, qb, fr, rout, ob, g2, s2, rup, ub, rdown, db)


def solution(mesh):
    batch = P(("group", "dp"), None, None)
    per_image = P(("group", "dp"))
    vec, mat = P("dp"), P("dp", None)
    fast = dict(mesh.shape) == {"group": 4, "dp": 8}
    return jax.shard_map(
        functools.partial(on_device, fast),
        mesh=mesh,
        in_specs=(batch, batch, per_image, per_image, P(), vec, vec, mat, vec, vec, mat, vec, vec, vec, mat, vec, mat, vec),
        out_specs=(batch, batch, vec, vec, mat, vec, vec, mat, vec, vec, vec, mat, vec, mat, vec),
        check_vma=False,
    )
```

```python
import functools
import math

import jax
import jax.numpy as jnp
from jax import lax
from jax.experimental import pallas as pl
from jax.experimental.pallas import tpu as pltpu
from jax.sharding import PartitionSpec as P

HEADS = 12
HD = 64
SIDE_S = 14
SIDE_M = 20
SIDE_L = 24
SLOT = 576
D = 768
FF = 3072
LN_EPS = 1e-06
MASK_FILL = -1e30
BF = jnp.bfloat16
F32 = jnp.float32
NT = (((1,), (1,)), ((), ()))
NN = (((1,), (0,)), ((), ()))
TN = (((0,), (0,)), ((), ()))
R_G1, R_S1, R_QB, R_FR, R_OB, R_G2, R_S2, R_UB, R_DB, R_ALL = 0, 1, 2, 5, 6, 7, 8, 9, 13, 16
THIRD = 256
LOG2E = math.log2(math.e)


def dot(a, b, dims, precision=None):
    return lax.dot_general(a, b, dims, preferred_element_type=F32, precision=precision)


def vm(n):
    return [pl.BlockSpec(memory_space=pltpu.VMEM)] * n


def norm_stats(x):
    mean = jnp.mean(x, axis=-1, keepdims=True)
    cen = x - mean
    var = jnp.mean(cen * cen, axis=-1, keepdims=True)
    inv = lax.rsqrt(var + LN_EPS)
    return cen * inv, inv


def sincos(x):
    n = jnp.floor(x * (2.0 / math.pi) + 0.5)
    r = x - n * 1.5703125
    r = r - n * 4.837512969970703125e-4
    r = r - n * 7.54978995489188216e-8
    q = n.astype(jnp.int32)
    r2 = r * r
    s = r + r * r2 * (-1.6666654611e-1 + r2 * (8.3321608736e-3 + r2 * -1.9515295891e-4))
    c = 1.0 - 0.5 * r2 + r2 * r2 * (
        4.166664568298827e-2 + r2 * (-1.388731625493765e-3 + r2 * 2.443315711809948e-5)
    )
    odd = (q & 1) == 1
    ss = jnp.where(odd, c, s)
    cc = jnp.where(odd, s, c)
    ss = jnp.where((q & 2) == 2, -ss, ss)
    cc = jnp.where(((q + 1) & 2) == 2, -cc, cc)
    return ss, cc


ERFC = (
    0.07314588129520416,
    -0.30809587240219116,
    0.3798876702785492,
    -0.08230462670326233,
    0.245080828666687,
    0.2054724544286728,
    0.24429383873939514,
    0.242519810795784,
)


def gelu_pair(x):
    z = jnp.abs(x)
    t = 1.0 / (1.0 + (0.43 * math.sqrt(0.5)) * z)
    poly = 0.5 * ERFC[0]
    for c in ERFC[1:]:
        poly = poly * t + 0.5 * c
    bell = jnp.exp2((x * x) * (-0.5 * LOG2E))
    half = poly * t * bell
    cdf = jnp.where(x < 0, half, 1.0 - half)
    return x * cdf, cdf + (x * math.sqrt(0.5 / math.pi)) * bell


def swap_halves(x):
    width = x.shape[-1]
    lane = lax.broadcasted_iota(jnp.int32, (1, width), 1)
    ahead = pltpu.roll(x, width - HD // 2, 1)
    behind = pltpu.roll(x, HD // 2, 1)
    return jnp.where(lane % HD < HD // 2, ahead, behind)


def half_sign(width):
    lane = lax.broadcasted_iota(jnp.int32, (1, width), 1)
    return jnp.where(lane % HD < HD // 2, 1.0, -1.0).astype(F32)


def side_of(res_ref, image):
    res = res_ref[image]
    return jnp.where(res == 0, SIDE_S, jnp.where(res == 1, SIDE_M, SIDE_L))


def device_weight(slots, assign_ref, counts_ref):
    groups = counts_ref.shape[0]
    counts = [jnp.full((1, 128), counts_ref[i], jnp.int32).astype(F32) for i in range(groups)]
    mine = jnp.full((1, 128), assign_ref[0], jnp.int32)
    picked = sum(jnp.where(mine == i, counts[i], 0.0) for i in range(groups))
    return (groups * picked / sum(counts) * (1.0 / math.sqrt(slots)))[:, :1]


def patch_columns(side_ref, image):
    side = jnp.full((SLOT, 128), side_of(side_ref, image), jnp.int32).astype(F32)
    slot = lax.broadcasted_iota(jnp.int32, (SLOT, 128), 0).astype(F32)
    row = jnp.floor((slot + 0.5) / side)
    col = slot - row * side
    valid = slot < side * side
    return col, row, valid


def spread(parity):
    src = lax.broadcasted_iota(jnp.int32, (128, 128), 0)
    lane = lax.broadcasted_iota(jnp.int32, (128, 128), 1)
    return (src == parity * HD + (lane // HD) * (HD // 2) + lane % (HD // 2)).astype(BF)


class Place:
    def __init__(self):
        self.p = lax.axis_index("dp")
        self.g = lax.axis_index("group")
        self.z, self.y = self.p // 2, self.p % 2
        self.x, self.core = self.g // 2, self.g % 2

    def over(self):
        return (self.g, self.p ^ 1)

    def sibling(self):
        return (self.g ^ 1, self.p)

    def across(self):
        return (self.g ^ 2, self.p)

    def line(self):
        return [(self.g, self.p ^ (2 * k)) for k in (1, 2, 3)]

    def partners(self):
        return [self.sibling(), self.across(), self.over()] + self.line()


def remote(src, dst, send, recv, device):
    return pltpu.make_async_remote_copy(
        src_ref=src, dst_ref=dst, send_sem=send, recv_sem=recv, device_id=device, device_id_type=pl.DeviceIdType.MESH
    )


def load(src, dst, sem):
    copy = pltpu.make_async_copy(src, dst, sem)
    copy.start()
    return copy


def greet(devices):
    barrier = pltpu.get_barrier_semaphore()
    for device in devices:
        pl.semaphore_signal(barrier, inc=1, device_id=device, device_id_type=pl.DeviceIdType.MESH)
    pl.semaphore_wait(barrier, len(devices))


def timetable(plan):
    return sorted(((step, name, stage) for name, steps in plan.items() for stage, step in enumerate(steps)), key=lambda r: r[0])


class Moves:
    def __init__(self, items, plan):
        self.items, self.rows = items, timetable(plan)

    def at(self, step):
        for when, name, stage in self.rows:
            if when == step:
                self.items[name].stage(stage)

    def within(self, step, first, last):
        for when in sorted({r[0] for r in self.rows if first <= r[0] <= last}):
            pl.when(step == when)(functools.partial(self.at, when))


class Gather:
    STAGES = 5

    def __init__(self, place, own, full, sems, recv, index):
        self.w, self.own, self.full = place, own, full
        self.rows = full.shape[0] // 8
        self.t = self.rows // 3 if self.rows % 48 == 0 else self.rows * 3 // 8
        self.e = self.rows - 2 * self.t
        self.send, self.sib = sems.at[2 * index], sems.at[2 * index + 1]
        self.recv = recv.at[index]

    def part(self, block, piece, ref=None):
        ref = self.full if ref is None else ref
        first = block * self.rows + piece * self.t
        return ref.at[pl.ds(pl.multiple_of(first, 16), self.e if isinstance(piece, int) else self.t)]

    def push(self, ref, device, index, src=None):
        remote(ref if src is None else src, ref, self.send, self.recv.at[index], device).start()

    def got(self, ref, index):
        remote(ref, ref, self.send, self.recv.at[index], self.w.sibling()).wait_recv()

    def hand(self, ref):
        remote(ref, ref, self.send, self.sib, self.w.sibling()).start()

    def stage(self, number):
        w = self.w
        pl.when(w.core == 0)(lambda: self.step(number, w.x, True))
        pl.when(w.core == 1)(lambda: self.step(number, 2, False))

    def step(self, number, piece, split):
        w = self.w
        if number == 0:
            src = self.part(0, piece, self.own)
            for k in (1, 3, 2):
                self.push(self.part(w.p, piece), (w.g, w.p ^ (2 * k)), w.z, src)
            self.push(self.part(w.p, piece), w.over(), 4 + w.z, src)
        elif number in (1, 2):
            for k in (1, 3, 2) if number == 1 else (0, 1, 3, 2):
                z = w.z ^ k
                block = 2 * z + (w.y if number == 1 else 1 - w.y)
                ref = self.part(block, piece)
                self.got(ref, z if number == 1 else 4 + z)
                if number == 1:
                    self.push(ref, w.over(), 4 + z)
                if split:
                    self.push(ref, w.across(), 8 + block)
                self.hand(ref)
        elif number == 3:
            if split:
                for k in (2, 6, 4, 1, 3, 7, 5):
                    block = w.p ^ k
                    ref = self.part(block, 1 - w.x)
                    self.got(ref, 8 + block)
                    self.hand(ref)
        else:
            for count in (14 * self.t, 14 * self.t) if split else (14 * self.e,):
                done = self.full.at[pl.ds(0, count)]
                remote(done, done, self.send, self.sib, w.sibling()).wait_send()
            came = self.full.at[pl.ds(0, 7 * self.e if split else 14 * self.t)]
            remote(came, came, self.send, self.sib, w.sibling()).wait_recv()


class Reduce:
    STAGES = 7

    def __init__(self, place, src, bufs, out, local, send, recv):
        self.w, self.src, self.out = place, src, out
        self.mine, self.cbuf, self.ybuf, self.zbuf, self.xbuf, self.fbuf = bufs
        self.rows = src.shape[0] // 8
        self.t, self.e = self.split(self.rows)
        self.local, self.send, self.recv = local, send, recv

    @staticmethod
    def split(rows):
        t = rows // 4 if rows % 64 == 0 else rows // 3
        return t, rows - 2 * t

    @classmethod
    def buffers(cls, rows, width):
        t, e = cls.split(rows)
        big = max(2 * t, e)
        sizes = (8 * big, 8 * big, 4 * max(t, e), 4 * max(t, e), 8 * t, max(t, e))
        return [pltpu.VMEM((n, width), BF) for n in sizes]

    def copy(self, src, dst, index, device):
        return remote(src, dst, self.send, self.recv.at[index], device)

    def took(self, ref, index):
        self.copy(ref, ref, index, self.w.sibling()).wait_recv()

    def rows_of(self, ref, first, count):
        return ref.at[pl.ds(pl.multiple_of(first, 16), count)]

    def add(self, target, *terms):
        def body(i, _):
            rows = pl.ds(pl.multiple_of(i * 32, 32), 32)
            if len(terms) == 1:
                target[rows] = target[rows] + terms[0][rows]
                return 0
            total = target[rows].astype(F32)
            for term in terms:
                total = total + term[rows].astype(F32)
            target[rows] = total.astype(BF)
            return 0

        lax.fori_loop(0, target.shape[0] // 32, body, 0)

    def each_core(self, first, second):
        pl.when(self.w.core == 0)(first)
        pl.when(self.w.core == 1)(second)

    def exchange(self, theirs, their_rows, ours, our_rows):
        def body(b, _):
            self.copy(
                self.rows_of(self.src, b * self.rows + theirs, their_rows),
                self.rows_of(self.cbuf, b * their_rows, their_rows),
                0,
                self.w.sibling(),
            ).start()
            pltpu.make_async_copy(
                self.rows_of(self.src, b * self.rows + ours, our_rows),
                self.rows_of(self.mine, b * our_rows, our_rows),
                self.local,
            ).start()
            return 0

        lax.fori_loop(0, 8, body, 0)

    def settle(self, count):
        whole = self.mine.at[pl.ds(0, 8 * count)]
        pltpu.make_async_copy(whole, whole, self.local).wait()
        self.took(self.cbuf.at[pl.ds(0, 8 * count)], 0)
        self.add(whole, self.cbuf)

    def zero_at(self, block, piece):
        return self.rows_of(self.mine, block * 2 * self.t + piece * self.t, self.t)

    def one_at(self, block):
        return self.rows_of(self.mine, block * self.e, self.e)

    def send_y(self, count, at):
        w = self.w

        def body(z, _):
            self.copy(at(2 * z + 1 - w.y), self.rows_of(self.ybuf, z * count, count), 2, w.over()).start()
            return 0

        lax.fori_loop(0, 4, body, 0)

    def take_y(self, count, at):
        self.took(self.ybuf.at[pl.ds(0, 4 * count)], 2)

        def body(z, _):
            self.add(at(2 * z + self.w.y), self.rows_of(self.ybuf, z * count, count))
            return 0

        lax.fori_loop(0, 4, body, 0)

    def send_z(self, count, at):
        w = self.w
        for k in (3, 1, 2):
            z = w.z ^ k
            self.copy(at(2 * z + w.y), self.rows_of(self.zbuf, k * count, count), 3, (w.g, 2 * z + w.y)).start()

    def take_z(self, count, at):
        self.took(self.zbuf.at[pl.ds(0, 3 * count)], 3)
        self.add(at(self.w.p), *[self.rows_of(self.zbuf, k * count, count) for k in (1, 2, 3)])

    def give(self, first, count, value):
        ref = self.out.at[pl.ds(pl.multiple_of(first, 8), count)]
        ref[...] = value
        remote(ref, ref, self.send, self.recv.at[5], self.w.sibling()).start()

    def stage(self, number):
        w, t, e = self.w, self.t, self.e
        x_mine = functools.partial(self.zero_at, piece=w.x)
        x_other = functools.partial(self.zero_at, piece=1 - w.x)
        if number == 0:
            self.each_core(lambda: self.exchange(2 * t, e, 0, 2 * t), lambda: self.exchange(0, 2 * t, 2 * t, e))
        elif number == 1:

            def first():
                self.settle(2 * t)

                def body(b, _):
                    self.copy(x_other(b), self.rows_of(self.xbuf, b * t, t), 1, w.across()).start()
                    return 0

                lax.fori_loop(0, 8, body, 0)

            def second():
                self.settle(e)
                self.send_y(e, self.one_at)

            self.each_core(first, second)
        elif number == 2:

            def first():
                self.took(self.xbuf, 1)

                def body(b, _):
                    self.add(x_mine(b), self.rows_of(self.xbuf, b * t, t))
                    return 0

                lax.fori_loop(0, 8, body, 0)
                self.send_y(t, x_mine)

            def second():
                self.take_y(e, self.one_at)
                self.send_z(e, self.one_at)

            self.each_core(first, second)
        elif number == 3:

            def first():
                self.take_y(t, x_mine)
                self.send_z(t, x_mine)

            def second():
                self.take_z(e, self.one_at)
                self.copy(self.one_at(w.p), self.fbuf.at[pl.ds(0, e)], 4, w.across()).start()

            self.each_core(first, second)
        elif number == 4:

            def first():
                self.take_z(t, x_mine)
                self.copy(x_mine(w.p), self.fbuf.at[pl.ds(0, t)], 4, w.across()).start()
                self.give(w.x * t, t, x_mine(w.p)[...].astype(F32))

            def second():
                self.took(self.fbuf.at[pl.ds(0, e)], 4)
                self.give(2 * t, e, self.one_at(w.p)[...].astype(F32) + self.fbuf[pl.ds(0, e)].astype(F32))

            self.each_core(first, second)
        elif number == 5:

            @pl.when(w.core == 0)
            def _():
                self.took(self.fbuf.at[pl.ds(0, t)], 4)
                self.give((1 - w.x) * t, t, self.fbuf[pl.ds(0, t)].astype(F32))

        else:

            def sent(count):
                while count > 0:
                    now = min(count, self.mine.shape[0])
                    part = self.mine.at[pl.ds(0, now)]
                    remote(part, part, self.send, self.recv.at[0], w.sibling()).wait_send()
                    count -= now

            def came(first, count):
                ref = self.out.at[pl.ds(first, count)]
                remote(ref, ref, self.send, self.recv.at[5], w.sibling()).wait_recv()

            def first():
                came(2 * t, e)
                sent(8 * e + 8 * t + 4 * t + 3 * t + t + 4 * t)

            def second():
                came(0, 2 * t)
                sent(16 * t + 4 * e + 3 * e + e + 2 * e)

            self.each_core(first, second)


class SmallSum:
    HOPS = (4, 2, 4)

    def __init__(self, place, value, bufs, send, recv):
        self.w, self.value, self.bufs, self.send, self.recv = place, value, bufs, send, recv

    def copies(self, hop):
        w = self.w
        for k in range(1, self.HOPS[hop]):
            device = ((w.g ^ k, w.p), (w.g, w.p ^ k), (w.g, w.p ^ (2 * k)))[hop]
            ref = self.bufs.at[4 * hop]
            yield remote(ref, self.bufs.at[4 * hop + k], self.send.at[hop, k], self.recv.at[hop, k], device)

    def stage(self, number):
        w = self.w
        if number > 0:
            hop = number - 1
            for copy in self.copies(hop):
                copy.wait()
            mine = (w.g, w.y, w.z)[hop]
            total = self.bufs[4 * hop + mine]
            for k in range(1, self.HOPS[hop]):
                total = total + self.bufs[4 * hop + (mine ^ k)]
        else:
            total = self.value[...]
        if number == 3:
            self.value[...] = total
        else:
            self.bufs[4 * number] = total
            for copy in self.copies(number):
                copy.start()


def mask_column(side_ref, image):
    side = side_of(side_ref, image)
    slot = lax.broadcasted_iota(jnp.int32, (SLOT, 1), 0)
    return jnp.where(slot < side * side, 0.0, MASK_FILL).astype(F32)


def head_pair(images, step):
    i, j = step % images, step // images
    rows = pl.ds(pl.multiple_of(i * SLOT, SLOT), SLOT)
    return i, rows, pl.multiple_of(j * 128, 128), pl.multiple_of((j // 2) * D + (j % 2) * 128, 128)


def attend_step(images, step, side_ref, qkv_ref, ctx_ref, lse_ref):
    i, rows, c, at = head_pair(images, step)
    q = qkv_ref[rows, pl.ds(at, 128)]
    k = qkv_ref[rows, pl.ds(at + THIRD, 128)]
    v = qkv_ref[rows, pl.ds(at + 2 * THIRD, 128)]
    lane = lax.broadcasted_iota(jnp.int32, (1, 128), 1)
    mask = mask_column(side_ref, i)
    outs, logs = [], []
    for h in range(2):
        qm = jnp.where(lane // HD == h, q, jnp.zeros_like(q))
        s = dot(k, qm, NT) * (LOG2E / math.sqrt(HD)) + mask
        top = jnp.max(s, axis=0, keepdims=True)
        e = jnp.exp2(s - top)
        total = jnp.sum(e, axis=0, keepdims=True)
        p = (e * (1.0 / total)).astype(BF)
        outs.append(dot(p, v, TN))
        logs.append(top + jnp.log2(total))
    ctx_ref[rows, pl.ds(c, 128)] = jnp.where(lane < HD, outs[0], outs[1]).astype(BF)
    lse_ref[step] = jnp.concatenate(logs + [jnp.zeros((6, SLOT), F32)], axis=0)


def norm_rows(images, x_ref, small, norm_ref):
    def body(step, _):
        rows = pl.ds(pl.multiple_of(step * 192, 192), 192)
        unit, _ = norm_stats(x_ref[rows])
        norm_ref[rows] = (unit * small[R_G1 : R_G1 + 1] + small[R_S1 : R_S1 + 1]).astype(BF)
        return 0

    lax.fori_loop(0, images * SLOT // 192, body, 0)


def angle_tables(images, side_ref, small, cos_ref, sin_ref, hooks):
    for j in range(D // 128):
        hooks("table", j)
        flat = [small[R_FR : R_FR + 1, n + j // 2 * 128 : n + j // 2 * 128 + 128] for n in (0, D // 2)]
        fc, fr = [dot(jnp.broadcast_to(v, (8, 128)).astype(BF), spread(j % 2), NN)[0:1] for v in flat]

        def body(i, _):
            rows = pl.ds(pl.multiple_of(i * SLOT, SLOT), SLOT)
            col, row, _ = patch_columns(side_ref, i)
            sn, cs = sincos(col * fc + row * fr)
            cos_ref[rows, pl.ds(j * 128, 128)] = cs
            sin_ref[rows, pl.ds(j * 128, 128)] = sn * -half_sign(128)
            return 0

        lax.fori_loop(0, images, body, 0)


def project_block(images, c, r, small, w_ref, norm_ref, qkv_ref, cos_ref, sin_ref):
    i, part = r % images, r // images
    rows = pl.ds(pl.multiple_of(i * SLOT, SLOT), SLOT)
    cols = pl.ds(pl.multiple_of(part * THIRD, THIRD), THIRD)
    lanes = pl.ds(pl.multiple_of(c * D + part * THIRD, THIRD), THIRD)
    inner = pl.ds(pl.multiple_of(c * THIRD, THIRD), THIRD)
    raw = dot(norm_ref[rows], w_ref[c, :, cols], NN) + small[pl.ds(R_QB + part, 1), inner]

    @pl.when(part < 2)
    def _():
        turned = raw * cos_ref[rows, inner] + swap_halves(raw) * sin_ref[rows, inner]
        qkv_ref[rows, lanes] = turned.astype(BF)

    @pl.when(part == 2)
    def _():
        qkv_ref[rows, lanes] = raw.astype(BF)


def forward_compute(images, side_ref, x_ref, small, w_ref, qkv, norm, cos, sin, ctx_ref, lse_ref, hooks):
    hooks("start")
    norm_rows(images, x_ref, small, norm)
    hooks("tables")
    angle_tables(images, side_ref, small, cos, sin, hooks)
    blocks, pairs = 3 * images, 2 * images

    def body(step, _):
        hooks("step", step)
        c, r = step // (blocks + pairs), step % (blocks + pairs)

        @pl.when(r < blocks)
        def _():
            project_block(images, c, r, small, w_ref, norm, qkv, cos, sin)

        @pl.when(r >= blocks)
        def _():
            attend_step(images, c * pairs + r - blocks, side_ref, qkv, ctx_ref, lse_ref)

        return 0

    lax.fori_loop(0, 3 * (blocks + pairs), body, 0)
    hooks("end")


def forward_plain(images, side_ref, x_ref, small_ref, w_ref, *refs):
    qkv, norm, cos, sin, ctx, lse = refs
    forward_compute(images, side_ref, x_ref, small_ref, w_ref, qkv, norm, cos, sin, ctx, lse, lambda *a: None)


def packed_places(p, dp, sizes):
    run = D // dp
    for first, size in zip(SMALL_ROWS, sizes):
        count = size // run
        yield [(first + (p * count + m) // dp, ((p * count + m) % dp) * run) for m in range(count)]


SMALL_ROWS = (R_G1, R_S1, R_QB, R_FR, R_OB, R_G2, R_S2, R_UB, R_DB)


SINGLES = (R_G1, R_S1, R_FR, R_OB, R_G2, R_S2, R_DB)
MORE = ((2, R_QB, 3, 8), (7, R_UB, 4, 11))


def compact(tinies, ref):
    run = tinies[0].shape[0]
    first = {row: i for i, row in enumerate(SMALL_ROWS)}
    for n, row in enumerate(SINGLES):
        ref[n, pl.ds(0, run)] = tinies[first[row]][...].astype(BF).astype(F32)
    for index, _, count, at in MORE:
        for m in range(count):
            ref[at + m, pl.ds(0, run)] = tinies[index][pl.ds(m * run, run)].astype(BF).astype(F32)


def expand(parts, small, run):
    small[...] = jnp.zeros_like(small)
    lane = lax.broadcasted_iota(jnp.int32, (1, 128), 1)
    total = None
    for owner, ref in parts:
        wide = jnp.concatenate([jnp.where(lane < run, ref[...], 0.0), jnp.zeros((R_ALL, D - 128), F32)], axis=1)
        term = pltpu.roll(wide[0:8], owner * run, 1)
        total = term if total is None else total + term
        for _, row, count, at in MORE:
            for m in range(count):
                place = owner * count + m
                moved = pltpu.roll(jnp.broadcast_to(wide[at + m : at + m + 1], (8, D)), (place % 8) * run, 1)
                small[pl.ds(row + place // 8, 1), :] += moved[0:1]
    for n, row in enumerate(SINGLES):
        small[row : row + 1] = total[n : n + 1]


def forward_gather(images, side_ref, *refs):
    tinies, x_in, shards_in = refs[0:9], refs[9], refs[10:14]
    qkv_out, norm_out, cos_out, sin_out, ctx, lse, small, wq_out, wo, wu, wd, up_later, down_later = refs[14:27]
    x_ref, qkv, norm, cos, sin, wq, slots, bq, bo, bu, bd, sq, so, su, sd = refs[27:42]
    sems, recv, psend, precv, local, ins = refs[42:]
    w = Place()
    pairs = [(bq.at[c], wq.at[c]) for c in range(3)] + [(bo, wo)]
    pairs += [(own.at[c], full.at[c]) for c in range(PARTS - 1) for own, full in ((bu, wu), (bd, wd))]
    lanes = [pl.ds(part * THIRD, THIRD) for part in range(3)]
    gathers = [(bq.at[0, :, cols], wq.at[0, :, cols]) for cols in lanes] + pairs[1:]
    gathers = dict(zip(("a0", "a1", "a2", "q1", "q2", "o", "u0", "d0", "u1", "d1"), gathers))
    gathers = {k: Gather(w, *v, sems, recv, i) for i, (k, v) in enumerate(gathers.items())}
    moves = Moves(gathers, FORWARD_PLAN)
    peers = [w.p ^ k for k in range(1, 8)]
    keep = {}

    def store(name, src, dst):
        keep[name] = load(src, dst, local.at[len(keep)])

    def qkv_third(c):
        lanes = pl.ds(c * D, D)
        return pltpu.make_async_copy(qkv.at[:, lanes], qkv_out.at[:, lanes], local.at[16 + c])

    def late(number):
        src, dst = ((cos, cos_out), (sin, sin_out), (wq, wq_out))[number]
        return pltpu.make_async_copy(src, dst, local.at[19 + number])

    def own_rows(full):
        count = full.shape[0] // 8
        return full.at[pl.ds(pl.multiple_of(w.p * count, 16), count)]

    def pack_copy(k):
        return remote(slots.at[0], slots.at[k], psend.at[k - 1], precv.at[k - 1], (w.g, peers[k - 1]))

    def hooks(where, step=None):
        if where == "start":
            reads = [
                load(src, dst, ins.at[i])
                for i, (src, dst) in enumerate(zip(shards_in[:1] + (x_in,) + shards_in[1:], (sq, x_ref, so, su, sd)))
            ]
            compact(tinies, slots.at[0])
            greet([(w.g, q) for q in peers] + [w.sibling(), w.across()])
            for k in range(1, 8):
                pack_copy(k).start()
            reads[0].wait()
            for c in range(3):
                for part in range(3):
                    cols = part * D + c * THIRD
                    bq[c, :, part * THIRD : (part + 1) * THIRD] = sq[:, cols : cols + THIRD].astype(BF)
                if c == 0:
                    moves.at(-1)
            for copy in reads[1:]:
                copy.wait()
            bo[...] = so[...].astype(BF)
            for c in range(PARTS):
                for b in range(8):
                    cols = (b * PARTS + c) * 128
                    bu[c, :, b * 128 : (b + 1) * 128] = su[:, cols : cols + 128].astype(BF)
                bd[c] = sd[c * 128 : (c + 1) * 128].astype(BF)
            for i, (own, full) in enumerate(pairs):
                store(i, own, own_rows(full))
            store("up", bu.at[PARTS - 1], up_later)
            store("down", bd.at[PARTS - 1], down_later)
            for k in range(1, 8):
                pack_copy(k).wait()
            expand([(w.p, slots.at[0])] + [(peers[k - 1], slots.at[k]) for k in range(1, 8)], small, D // 8)
            moves.at(0)
        elif where == "tables":
            store("norm", norm, norm_out)
        elif where == "table":
            moves.at(1 + step / 10)
        elif where == "step":

            @pl.when(step == 0)
            def _():
                for i in range(3):
                    keep[i].wait()
                for number in (0, 1):
                    late(number).start()

            moves.within(step + 2, 2, 31)
            for c in (1, 2):

                @pl.when(step == 10 * c)
                def _(c=c):
                    qkv_third(c - 1).start()
                    if c == 2:
                        late(2).start()

        else:
            qkv_third(2).start()
            moves.at(32)
            for c in range(3):
                qkv_third(c).wait()
                late(c).wait()
            for name, copy in keep.items():
                if name not in (0, 1, 2):
                    copy.wait()

    forward_compute(images, side_ref, x_ref, small, wq, qkv, norm, cos, sin, ctx, lse, hooks)


FORWARD_PLAN = {
    "a0": (-1, 1, 1.2, 1.4, 2),
    "a1": (-1, 1, 1.2, 1.4, 4),
    "a2": (-1, 1, 1.3, 1.5, 6),
    "q1": (0, 1.5, 8, 11, 12),
    "q2": (1, 6, 11, 17, 22),
    "o": (1.5, 7, 13, 26, 32),
    "u0": (3, 11, 19, 26, 32),
    "d0": (7, 16, 20, 28, 32),
    "u1": (13, 21, 26, 30, 32),
    "d1": (8, 18, 24, 29, 32),
}


def bias_at(split, step):
    c, k = step // BLOCKS, step % BLOCKS
    if split:
        return (R_UB + k, c * 128), (R_UB + k, D // 2 + c * 128)
    return (R_UB + step // 3, (step % 3) * 256), (R_UB + step // 3, (step % 3) * 256 + 128)


def mlp_compute(images, split, side_ref, scale, cot_ref, ctx_ref, small, wo_ref, wu, wd, refs, outs, hooks):
    mid, n2, n2t, bl, hid, gpre, ubias, gubias = refs
    act, gm, gctx, gdown, gup, gout, gs = outs
    rows_all = images * SLOT
    tile = SLOT // 2
    hooks("start")
    gain = small[R_G2 : R_G2 + 1]
    gs[...] = jnp.zeros_like(gs)
    for step in range(PARTS * BLOCKS):
        for n, (r, l) in enumerate(bias_at(split, step)):
            ubias[step : step + 1, n * 128 : (n + 1) * 128] = small[r : r + 1, l : l + 128]

    def tile_rows(step):
        side = side_of(side_ref, step // 2)
        slot = lax.broadcasted_iota(jnp.int32, (tile, 1), 0) + (step % 2) * tile
        return pl.ds(pl.multiple_of(step * tile, tile), tile), slot < side * side

    def enter(step, _):
        hooks("enter", step)
        rows, valid = tile_rows(step)
        middle = mid[rows] + (dot(ctx_ref[rows], wo_ref[...], NN) + small[R_OB : R_OB + 1])
        mid[rows] = middle
        act[rows] = middle + small[R_DB : R_DB + 1]
        unit, _ = norm_stats(middle)
        n2[rows] = (unit * gain + small[R_S2 : R_S2 + 1]).astype(BF)
        low = jnp.where(valid, cot_ref[rows], 0.0).astype(BF)
        bl[rows] = low
        gs[R_DB : R_DB + 1] += jnp.sum(low.astype(F32), axis=0, keepdims=True)
        return 0

    lax.fori_loop(0, 2 * images, enter, 0)
    gm[...] = jnp.zeros_like(gm)
    n2t[...] = n2[...].T
    hooks("entered")

    first = pl.ds(0, 256)
    hid[:, first] = jnp.zeros((rows_all, 256), BF)
    gpre[:, first] = jnp.zeros((rows_all, 256), BF)

    def weights(step):
        c = step // BLOCKS
        cols = pl.ds(pl.multiple_of((step % BLOCKS) * 256, 256), 256)
        gdown[c, cols, :] = (dot(hid[:, cols], bl[...], TN) * scale).astype(BF)
        gup[c, :, cols] = (dot(n2t[...], gpre[:, cols], NN) * scale).astype(BF)

    def block(step, _):
        hooks("block", step)
        c, k = step // BLOCKS, step % BLOCKS
        cols = pl.ds(pl.multiple_of(k * 256, 256), 256)
        bias = ubias[pl.ds(step, 1), :]
        wuc = wu[c, :, cols]
        wdc = wd[c, cols, :]
        weights(jnp.maximum(step - 1, 0))
        pieces = [pl.ds(i * tile, tile) for i in range(2 * images)]
        pres = [dot(n2[rows], wuc, NN) + bias for rows in pieces]
        backs = [dot(bl[rows], wdc, NT) for rows in pieces]
        bsum = None
        for rows, pre, back in zip(pieces, pres, backs):
            value, slope = gelu_pair(pre)
            hid[rows, cols] = value.astype(BF)
            g = (back * slope).astype(BF)
            gpre[rows, cols] = g
            part = jnp.sum(g.astype(F32), axis=0, keepdims=True)
            bsum = part if bsum is None else bsum + part
        gubias[pl.ds(step, 1), :] = bsum

        @pl.when(k == BLOCKS - 1)
        def _():
            def tail(n, _):
                rows = pl.ds(pl.multiple_of(n * SLOT, SLOT), SLOT)
                act[rows] += dot(hid[rows], wd[c], NN)
                gm[rows] += dot(gpre[rows], wu[c], NT)
                return 0

            lax.fori_loop(0, images, tail, 0)

        return 0

    lax.fori_loop(0, PARTS * BLOCKS, block, 0)
    weights(PARTS * BLOCKS - 1)
    hooks("blocks")

    def leave(step, _):
        rows, valid = tile_rows(step)
        unit, inv = norm_stats(mid[rows])
        act[rows] = jnp.where(valid, act[rows], 0.0)
        gn = gm[rows]
        gs[R_G2 : R_G2 + 1] += jnp.sum(gn * unit, axis=0, keepdims=True)
        gs[R_S2 : R_S2 + 1] += jnp.sum(gn, axis=0, keepdims=True)
        a = gn * gain
        ma = jnp.mean(a, axis=-1, keepdims=True)
        mu = jnp.mean(a * unit, axis=-1, keepdims=True)
        g = jnp.where(valid, cot_ref[rows], 0.0) + inv * (a - ma - unit * mu)
        gm[rows] = g
        low = g.astype(BF)
        bl[rows] = low
        gs[R_OB : R_OB + 1] += jnp.sum(low.astype(F32), axis=0, keepdims=True)
        gctx[rows] = dot(low, wo_ref[...], NT).astype(BF)
        hooks("left", step)
        return 0

    lax.fori_loop(0, 2 * images, leave, 0)
    for step in range(PARTS * BLOCKS):
        for n, (r, l) in enumerate(bias_at(split, step)):
            gs[r : r + 1, l : l + 128] = gubias[step : step + 1, n * 128 : (n + 1) * 128]
    gout[...] = (dot(ctx_ref[...], bl[...], TN) * scale).astype(BF)
    gs[...] = gs[...] * scale
    hooks("end")


def mlp_scratch(rows):
    vmem = pltpu.VMEM
    return (
        [vmem((rows, D), F32), vmem((rows, D), BF), vmem((D, rows), BF), vmem((rows, D), BF)]
        + [vmem((rows, FF // PARTS), BF)] * 2
        + [vmem((16, 256), F32)] * 2
    )


def mlp_plain(images, slots, side_ref, assign_ref, counts_ref, x_ref, cot_ref, ctx_ref, small, wo_ref, wu, wd, *rest):
    outs, refs, sem = rest[0:7], rest[7:15], rest[15]
    load(x_ref, refs[0], sem.at[0]).wait()
    mlp_compute(
        images, False, side_ref, device_weight(slots, assign_ref, counts_ref), cot_ref, ctx_ref, small, wo_ref, wu, wd, refs, outs, lambda *a: None
    )


def mlp_moving(images, slots, side_ref, assign_ref, counts_ref, small, *rest):
    x_in, cot_in, ctx_in, wo_in, wu_in, wd_in, up_later, down_later = rest[0:8]
    act_out, gm_out, gctx_out, gd_out, gu_out, go_out, gs, rd, ru = rest[8:17]
    refs = rest[17:25]
    mid, n2, n2t = refs[0], refs[1], refs[2]
    cot, ctx, wo, wu, wd, act, gm, gd, gu = rest[25:34]
    bufs, (local, sems, recv, rlocal, rsend, rrecv, tile_in, tile_out) = rest[34:46], rest[46:54]
    w = Place()
    last = PARTS - 1
    items = {
        "u": Gather(w, up_later, wu.at[last], sems, recv, 0),
        "d": Gather(w, down_later, wd.at[last], sems, recv, 1),
        "rd": Reduce(w, gd.at[0], bufs[0:6], rd, rlocal.at[0], rsend.at[0], rrecv.at[0]),
        "ru": Reduce(w, gu.at[0], bufs[6:12], ru, rlocal.at[1], rsend.at[1], rrecv.at[1]),
    }
    moves = Moves(items, MLP_PLAN)
    keep = []

    def move(src, dst):
        keep.append(load(src, dst, local.at[len(keep)]))
        return keep[-1]

    tile = SLOT // 2

    def by_tile(step, pairs, sem):
        rows = pl.ds(pl.multiple_of(step * tile, tile), tile)
        return [pltpu.make_async_copy(src.at[rows], dst.at[rows], sem.at[i, step]) for i, (src, dst) in enumerate(pairs)]

    def arriving(step):
        return by_tile(step, ((ctx_in, ctx), (x_in, mid), (cot_in, cot)), tile_in)

    def leaving(step):
        return by_tile(step, ((act, act_out), (gm, gm_out), (n2, gctx_out)), tile_out)

    def hooks(where, step=None):
        if where == "start":
            move(wo_in, wo)
            for i in range(2 * images):
                for copy in arriving(i):
                    copy.start()
            for c in range(last):
                move(wu_in.at[c], wu.at[c])
                move(wd_in.at[c], wd.at[c])
            for own, full in ((up_later, wu), (down_later, wd)):
                count = full.shape[1] // 8
                move(own, full.at[last, pl.ds(pl.multiple_of(w.p * count, 16), count)])
            greet(w.partners())
            moves.at(0)
            keep[0].wait()
        elif where == "enter":
            for copy in arriving(step):
                copy.wait()
        elif where == "left":
            for copy in leaving(step):
                copy.start()
        elif where == "entered":
            for copy in keep[1:]:
                copy.wait()
            keep.clear()
        elif where == "block":
            moves.within(step + 1, 1, 12)
        elif where == "blocks":
            for c in (1, 2):
                move(gd.at[c], gd_out.at[c - 1])
                move(gu.at[c], gu_out.at[c - 1])
            moves.at(13)
        else:
            move(n2t.at[:, pl.ds(0, D)], go_out)
            moves.at(14)
            for i in range(2 * images):
                for copy in leaving(i):
                    copy.wait()
            for copy in keep:
                copy.wait()

    mlp_compute(
        images,
        True,
        side_ref,
        device_weight(slots, assign_ref, counts_ref),
        cot,
        ctx,
        small,
        wo,
        wu,
        wd,
        refs,
        (act, gm, n2, gd, gu, n2t.at[:, pl.ds(0, D)], gs),
        hooks,
    )


MLP_PLAN = {
    "u": (0, 2, 4, 5, 7),
    "d": (1, 4, 5, 7, 8),
    "rd": (6, 8, 10, 12, 13, 14, 14),
    "ru": (6, 7, 9, 11, 13, 14, 14),
}


PARTS = 3
BLOCKS = 4


def attend_back_step(images, step, side_ref, qkv_ref, gctx_ref, lse_ref, cos_ref, sin_ref, gproj_ref, gs_ref, gf_ref):
    i, rows, c, at = head_pair(images, step)
    q = qkv_ref[rows, pl.ds(at, 128)]
    k = qkv_ref[rows, pl.ds(at + THIRD, 128)]
    v = qkv_ref[rows, pl.ds(at + 2 * THIRD, 128)]
    go = gctx_ref[rows, pl.ds(c, 128)]
    lane = lax.broadcasted_iota(jnp.int32, (1, 128), 1)
    mask = mask_column(side_ref, i)
    lse = lse_ref[step]
    dq, dk, dv = [], [], []
    for h in range(2):
        mine = lane // HD == h
        qm = jnp.where(mine, q, jnp.zeros_like(q))
        gom = jnp.where(mine, go, jnp.zeros_like(go))
        s = dot(k, qm, NT) * (LOG2E / math.sqrt(HD)) + mask
        p = jnp.exp2(s - lse[h : h + 1])
        dp = dot(v, gom, NT)
        dv.append(dot(p.astype(BF), go, NN))
        t = p * dp
        ds = (t - p * jnp.sum(t, axis=0, keepdims=True)).astype(BF)
        dk.append(dot(ds, q, NN))
        dq.append(dot(ds, k, TN))
    first = lane < HD
    cs = cos_ref[rows, pl.ds(c, 128)]
    sn = sin_ref[rows, pl.ds(c, 128)]
    angle = None
    for n, (pair, rot) in enumerate(((dq, q), (dk, k))):
        e = jnp.where(first, pair[0], pair[1]) * (1.0 / math.sqrt(HD))
        other = swap_halves(e)
        back = (e * cs - other * sn).astype(BF)
        gproj_ref[rows, pl.ds(at + n * THIRD, 128)] = back
        gs_ref[pl.ds(R_QB + n, 1), pl.ds(c, 128)] += jnp.sum(back.astype(F32), axis=0, keepdims=True)
        term = rot.astype(F32) * other
        angle = term if angle is None else angle + term
    gv = jnp.where(first, dv[0], dv[1]).astype(BF)
    gproj_ref[rows, pl.ds(at + 2 * THIRD, 128)] = gv
    gs_ref[R_QB + 2 : R_QB + 3, pl.ds(c, 128)] += jnp.sum(gv.astype(F32), axis=0, keepdims=True)
    angle = angle * half_sign(128)
    col, row, _ = patch_columns(side_ref, i)
    gf_ref[0:1, pl.ds(c, 128)] += jnp.sum(angle * col, axis=0, keepdims=True)
    gf_ref[1:2, pl.ds(c, 128)] += jnp.sum(angle * row, axis=0, keepdims=True)


def freq_row(gf_ref, gs_ref):
    for m in range(D // 128):
        which = m // 3
        total = None
        for parity in (0, 1):
            lanes = 2 * (m % 3) + parity
            value = gf_ref[which : which + 1, lanes * 128 : lanes * 128 + 128]
            for _ in range(3):
                term = value.astype(BF)
                value = value - term.astype(F32)
                moved = dot(jnp.broadcast_to(term, (8, 128)), spread(parity), NT)[0:1]
                total = moved if total is None else total + moved
        gs_ref[R_FR : R_FR + 1, m * 128 : m * 128 + 128] = total


def weight_third(c, scale, norm_ref, gproj_ref, gw_ref):
    def block(j, _):
        lanes = pl.ds(pl.multiple_of(j * THIRD, THIRD), THIRD)
        full = pl.ds(pl.multiple_of(c * D + j * THIRD, THIRD), THIRD)
        gw_ref[:, lanes] = (dot(norm_ref[...], gproj_ref[:, full], TN) * scale).astype(BF)
        return 0

    lax.fori_loop(0, 3, block, 0)


def attend_back_compute(images, thirds, side_ref, scale, ins, norm, gproj, gws, gs_ref, gf_ref, hooks):
    hooks("start")
    gs_ref[...] = jnp.zeros_like(gs_ref)
    gf_ref[...] = jnp.zeros_like(gf_ref)

    def body(step, _):
        hooks("step", step)
        attend_back_step(images, step, side_ref, *ins, gproj, gs_ref, gf_ref)
        for c in range(thirds):

            @pl.when(step == 2 * images * (c + 1) - 1)
            def _(c=c):
                weight_third(c, scale, norm, gproj, gws.at[c])

        return 0

    lax.fori_loop(0, images * HEADS // 2, body, 0)
    freq_row(gf_ref, gs_ref)
    hooks("end")


def attend_back_plain(images, slots, side_ref, assign_ref, counts_ref, *refs):
    ins, norm, (gproj, gws, gs, gf) = refs[0:5], refs[5], refs[6:10]
    attend_back_compute(images, 3, side_ref, device_weight(slots, assign_ref, counts_ref), ins, norm, gproj, gws, gs, gf, lambda *a: None)


def qkv_back_compute(images, x_ref, gproj_ref, gm_ref, small_ref, w_ref, gs_in, gin_ref, gs_ref, hooks):
    hooks("start")
    gain = small_ref[R_G1 : R_G1 + 1]
    gs_ref[...] = gs_in[...]
    tile = SLOT // 2

    def body(step, _):
        hooks("tile", step)
        rows = pl.ds(pl.multiple_of(step * tile, tile), tile)
        unit, inv = norm_stats(x_ref[rows])
        gn = None
        for c in range(3):
            term = dot(gproj_ref[rows, c * D : (c + 1) * D], w_ref[c][...], NT)
            gn = term if gn is None else gn + term
        gs_ref[R_G1 : R_G1 + 1] += jnp.sum(gn * unit, axis=0, keepdims=True)
        gs_ref[R_S1 : R_S1 + 1] += jnp.sum(gn, axis=0, keepdims=True)
        a = gn * gain
        ma = jnp.mean(a, axis=-1, keepdims=True)
        mu = jnp.mean(a * unit, axis=-1, keepdims=True)
        gin_ref[rows] = gm_ref[rows] + inv * (a - ma - unit * mu)
        return 0

    lax.fori_loop(0, 2 * images, body, 0)
    hooks("end")


def qkv_back_plain(images, slots, assign_ref, counts_ref, x_ref, gproj_ref, gm_ref, small_ref, w_ref, gs_in, gin, gs):
    def hooks(where, index=None):
        if where == "end":
            gs[...] = gs[...] * device_weight(slots, assign_ref, counts_ref)

    parts = [w_ref.at[c] for c in range(3)]
    qkv_back_compute(images, x_ref, gproj_ref, gm_ref, small_ref, parts, gs_in, gin, gs, hooks)


def backward_reduce(images, slots, side_ref, assign_ref, counts_ref, small_ref, gs_mlp, *refs):
    ins_in, (gd, gu, go), (x_in, gm_in, w_in) = refs[0:6], refs[6:9], refs[9:12]
    gin_out, gs, outs = refs[12], refs[13], refs[14:22]
    ins, gproj, gws, gf, gs_own = refs[22:28], refs[28], refs[29], refs[30], refs[31]
    bufs, tinybufs, (loads, local, send, recv, ssend, srecv) = refs[32:80], refs[80], refs[81:87]
    qkv, cos, sin, norm = ins[0], ins[3], ins[4], ins[5]
    w = Place()
    weight = device_weight(slots, assign_ref, counts_ref)
    srcs = (gd.at[0], gu.at[0], gd.at[1], gu.at[1], go, gws.at[0], gws.at[1], gws.at[2])
    items = {
        name: Reduce(w, srcs[i], bufs[6 * i : 6 * i + 6], outs[i], local.at[i], send.at[i], recv.at[i])
        for i, name in enumerate(BACK_PLAN)
    }
    moves = Moves(items, BACK_PLAN)
    tiny = SmallSum(w, gs, tinybufs, ssend, srecv)

    def third(c):
        copies = []
        for i, width in ((0, D), (1, THIRD), (3, THIRD), (4, THIRD)):
            lanes = pl.ds(c * width, width)
            copies.append(pltpu.make_async_copy(ins_in[i].at[:, lanes], ins[i].at[:, lanes], loads.at[c, i]))
        whole = {0: 2, 1: 5}.get(c)
        if whole is not None:
            copies.append(pltpu.make_async_copy(ins_in[whole], ins[whole], loads.at[c, 5]))
        return copies

    def hooks(where, step=None):
        if where == "start":
            for c in range(3):
                for copy in third(c):
                    copy.start()
            greet(w.partners() + [(w.g ^ 3, w.p)])
            moves.at(0)
            for copy in third(0):
                copy.wait()
        elif where == "step":
            for c, when in ((1, 2 * images - 1), (2, 4 * images)):

                @pl.when(step == when)
                def _(c=c):
                    for copy in third(c):
                        copy.wait()

            moves.within(step + 1, 1, 12)

    attend_back_compute(images, 3, side_ref, weight, ins[0:5], norm, gproj, gws, gs_own, gf, hooks)
    copies = [load(x_in, cos, loads.at[0, 0]), load(gm_in, sin, loads.at[0, 1])]
    wide = [qkv.at[pl.ds(0, D), pl.ds(c * D, D)] for c in range(3)]
    copies += [load(w_in.at[c], wide[c], loads.at[0, 2 + c]) for c in range(3)]
    moves.at(13)
    for copy in copies:
        copy.wait()

    def tiles(where, step=None):
        if where == "tile":
            moves.within(step + 14, 14, 17)

    qkv_back_compute(images, cos, gproj, sin, small_ref, wide, gs_own, sin, gs, tiles)
    copy = load(sin, gin_out, loads.at[0, 0])
    gs[...] = gs[...] * weight + gs_mlp[...]
    for number in range(4):
        tiny.stage(number)
        moves.at(18 + number)
    copy.wait()


BACK_PLAN = {
    "d1": (1, 3, 6, 9, 17, 19, 19),
    "u1": (1, 7, 11, 14, 18, 19, 21),
    "d2": (2, 4, 6, 9, 13, 15, 19),
    "u2": (2, 5, 8, 11, 14, 18, 20),
    "o": (0, 4, 7, 13, 16, 18, 21),
    "q0": (6, 7, 11, 15, 18, 19, 20),
    "q1": (9, 10, 14, 16, 18, 19, 20),
    "q2": (13, 14, 17, 18, 19, 20, 21),
}


def finish_kernel(dp, p_axis, gs, act_in, gin_in, rout_in, *refs):
    rd, ru, rq = refs[0:3], refs[3:6], refs[6:9]
    act, gin, rqkv, rout, rup, rdown, sems = refs[9], refs[10], *refs[11:15], refs[-1]
    tinies = refs[15:-2]
    stage = refs[-2]
    ins = [load(act_in, stage.at[0], sems.at[0]), load(gin_in, stage.at[1], sems.at[1])]
    p = lax.axis_index(p_axis)
    run = D // dp
    for out, places in zip(tinies, packed_places(p, dp, [t.shape[0] for t in tinies])):
        for m, (row, lane) in enumerate(places):
            whole = jnp.broadcast_to(gs[pl.ds(row, 1), :], (8, D))
            out[pl.ds(m * run, run)] = pltpu.roll(whole, D - lane, 1)[0, :run]
    copies = []
    for n, dst in enumerate((act, gin)):
        ins[n].wait()
        copies.append(load(stage.at[n], dst, sems.at[n]))
    rout[...] = rout_in[...]
    for c in range(3):
        rdown[c * rd[c].shape[0] : (c + 1) * rd[c].shape[0]] = rd[c][...]
        for b in range(dp):
            rup[:, (b * 3 + c) * 128 : (b * 3 + c + 1) * 128] = ru[c][:, b * 128 : (b + 1) * 128]
        for part in range(3):
            cols = part * D + c * THIRD
            rqkv[:, cols : cols + THIRD] = rq[c][:, part * THIRD : (part + 1) * THIRD]
    for copy in copies:
        copy.wait()


def params(mb=56):
    return pltpu.CompilerParams(vmem_limit_bytes=mb << 20)


def place_rows(p, dp, vec):
    n = vec.shape[0]
    whole = jnp.tile(vec, dp)
    owner = jnp.arange(n * dp, dtype=jnp.int32) // n
    return jnp.where(owner == p, whole, 0.0).reshape(-1, D)


def on_device(
    fast,
    images,
    cotangent,
    resolution,
    assignment,
    counts,
    ln1_gain,
    ln1_shift,
    qkv_weight,
    qkv_bias,
    rope_freqs,
    out_weight,
    out_bias,
    ln2_gain,
    ln2_shift,
    up_weight,
    up_bias,
    down_weight,
    down_bias,
):
    p = lax.axis_index("dp")
    dp = lax.axis_size("dp")
    n = images.shape[0]
    rows = n * SLOT
    x = images.reshape(rows, D)
    cot = cotangent.reshape(rows, D)
    vectors = (ln1_gain, ln1_shift, qkv_bias, rope_freqs, out_bias, ln2_gain, ln2_shift, up_bias, down_bias)
    slots = dp * rows
    sds = jax.ShapeDtypeStruct
    smem = pl.BlockSpec(memory_space=pltpu.SMEM)
    anyw = pl.BlockSpec(memory_space=pl.ANY)
    kept = [
        sds((rows, 3 * D), BF),
        sds((rows, D), BF),
        sds((rows, D), F32),
        sds((rows, D), F32),
        sds((rows, D), BF),
        sds((n * HEADS // 2, 8, SLOT), F32),
    ]
    weights = (qkv_weight, out_weight, up_weight, down_weight)
    dma = pltpu.SemaphoreType.DMA
    vmem = pltpu.VMEM

    def moving(number, mb):
        return pltpu.CompilerParams(vmem_limit_bytes=mb << 20, collective_id=number, has_side_effects=True)

    part = FF // PARTS
    if fast:
        later = [sds((D // dp, part), BF), sds((part // dp, D), BF)]
        fulls = [sds((3, D, D), BF), sds((D, D), BF), sds((PARTS - 1, D, part), BF), sds((PARTS - 1, part, D), BF)]
        outs = pl.pallas_call(
            functools.partial(forward_gather, n),
            out_shape=kept + [sds((R_ALL, D), F32)] + fulls + later,
            in_specs=[smem] + vm(9) + [anyw] * 5,
            out_specs=[anyw] * 4 + vm(3) + [anyw] * 6,
            scratch_shapes=[
                vmem((rows, D), F32),
                vmem((rows, 3 * D), BF),
                vmem((rows, D), BF),
                vmem((rows, D), F32),
                vmem((rows, D), F32),
                vmem((3, D, D), BF),
                vmem((8, R_ALL, 128), F32),
                vmem((3, D // dp, D), BF),
                vmem((D // dp, D), BF),
                vmem((PARTS, D // dp, part), BF),
                vmem((PARTS, part // dp, D), BF),
            ]
            + [vmem(v.shape, F32) for v in weights]
            + [
                dma((20,)),
                dma((10, 16)),
                dma((7,)),
                dma((7,)),
                dma((22,)),
                dma((5,)),
            ],
            compiler_params=moving(0, 56),
            name="forward",
        )(resolution, *vectors, x, *weights)
        qkv, norm1, cos, sin, ctx, lse, small, wqkv, wo, wu, wd, up_later, down_later = outs
    else:
        packed = [place_rows(p, dp, lax.reduce_precision(v, 8, 7)) for v in vectors]
        small = lax.psum(jnp.concatenate(packed + [jnp.zeros((2, D), F32)], axis=0), "dp")
        wqkv, wo, wu, wd = [lax.all_gather(v.astype(BF), "dp", axis=0, tiled=True) for v in weights]
        wqkv = wqkv.reshape(D, 3, 3, THIRD).transpose(2, 0, 1, 3).reshape(3, D, D)
        wu = wu.reshape(D, PARTS, part).transpose(1, 0, 2)
        wd = wd.reshape(PARTS, part, D)
        qkv, norm1, cos, sin, ctx, lse = pl.pallas_call(
            functools.partial(forward_plain, n),
            out_shape=kept,
            in_specs=[smem] + vm(3),
            out_specs=vm(6),
            compiler_params=params(),
            name="forward",
        )(resolution, x, small, wqkv)

    grads = [sds((PARTS, part, D), BF), sds((PARTS, D, part), BF), sds((D, D), BF)]
    rest = [sds((R_ALL, D), F32)]
    firsts = [sds((rows, D), F32), sds((rows, D), F32), sds((rows, D), BF)]
    tables = [vmem((rows, 3 * D), BF), vmem((rows, D), BF), vmem((n * HEADS // 2, 8, SLOT), F32)]
    tables += [vmem((rows, D), F32)] * 2
    gproj_shape = sds((rows, 3 * D), BF)
    if fast:
        sizes = [(part // dp, D), (D // dp, part)]
        act, gm, gctx, gdown, gup, gout, gs_mlp, rdown0, rup0 = pl.pallas_call(
            functools.partial(mlp_moving, n, slots),
            out_shape=firsts
            + [sds((PARTS - 1,) + g.shape[1:], BF) for g in grads[:2]]
            + grads[2:]
            + rest
            + [sds(z, F32) for z in sizes],
            in_specs=[smem] * 3 + vm(1) + [anyw] * 8,
            out_specs=[anyw] * 6 + vm(3),
            scratch_shapes=mlp_scratch(rows)
            + [
                vmem((rows, D), F32),
                vmem((rows, D), BF),
                vmem((D, D), BF),
                vmem((PARTS, D, part), BF),
                vmem((PARTS, part, D), BF),
                vmem((rows, D), F32),
                vmem((rows, D), F32),
                vmem((PARTS, part, D), BF),
                vmem((PARTS, D, part), BF),
            ]
            + sum([Reduce.buffers(*z) for z in sizes], [])
            + [dma((12,)), dma((4,)), dma((2, 16)), dma((2,)), dma((2,)), dma((2, 6))]
            + [dma((3, 2 * n))] * 2,
            compiler_params=moving(3, 63),
            name="mlp",
        )(resolution, assignment, counts, small, x, cot, ctx, wo, wu, wd, up_later, down_later)
        third = (D // dp, D)
        sizes = sizes + sizes + [third] * 4
        gin, gs, rdown1, rup1, rdown2, rup2, rout, rq0, rq1, rq2 = pl.pallas_call(
            functools.partial(backward_reduce, n, slots),
            out_shape=[sds((rows, D), F32)] + rest + [sds(z, F32) for z in sizes],
            in_specs=[smem] * 3 + vm(2) + [anyw] * 12,
            out_specs=[anyw] + vm(9),
            scratch_shapes=tables
            + [vmem((rows, D), BF), vmem((rows, 3 * D), BF), vmem((3, D, D), BF), vmem((8, D), F32)]
            + [vmem((R_ALL, D), F32)]
            + sum([Reduce.buffers(*z) for z in sizes], [])
            + [vmem((12, R_ALL, D), F32), dma((3, 6)), dma((8,)), dma((8,)), dma((8, 6)), dma((3, 4)), dma((3, 4))],
            compiler_params=moving(1, 62),
            name="backward",
        )(resolution, assignment, counts, small, gs_mlp, qkv, gctx, lse, cos, sin, norm1, gdown, gup, gout, x, gm, wqkv)

        matrices = (qkv_weight, out_weight, up_weight, down_weight)
        act, gin, rqkv, rout, rup, rdown, *tinies = pl.pallas_call(
            functools.partial(finish_kernel, dp, "dp"),
            out_shape=[sds((rows, D), F32)] * 2 + [sds(v.shape, F32) for v in matrices + vectors],
            in_specs=vm(1) + [anyw] * 2 + vm(10),
            out_specs=[anyw] * 2 + vm(13),
            scratch_shapes=[vmem((2, rows, D), F32), dma((2,))],
            compiler_params=params(),
            name="finish",
        )(gs, act, gin, rout, rdown0, rdown1, rdown2, rup0, rup1, rup2, rq0, rq1, rq2)
    else:
        act, gm, gctx, gdown, gup, gout, gs_mlp = pl.pallas_call(
            functools.partial(mlp_plain, n, slots),
            out_shape=firsts + grads + rest,
            in_specs=[smem] * 3 + [anyw] + vm(6),
            out_specs=vm(7),
            scratch_shapes=mlp_scratch(rows) + [dma((1,))],
            compiler_params=params(63),
            name="mlp",
        )(resolution, assignment, counts, x, cot, ctx, small, wo, wu, wd)
        gproj, gqkv, gs_att = pl.pallas_call(
            functools.partial(attend_back_plain, n, slots),
            out_shape=[gproj_shape, sds((3, D, D), BF)] + rest,
            in_specs=[smem] * 3 + vm(6),
            out_specs=vm(3),
            scratch_shapes=[vmem((8, D), F32)],
            compiler_params=params(),
            name="attend_back",
        )(resolution, assignment, counts, qkv, gctx, lse, cos, sin, norm1)
        gin, gs_qkv = pl.pallas_call(
            functools.partial(qkv_back_plain, n, slots),
            out_shape=[sds((rows, D), F32)] + rest,
            in_specs=[smem] * 2 + vm(6),
            out_specs=vm(2),
            compiler_params=params(),
            name="project_back",
        )(assignment, counts, x, gproj, gm, small, wqkv, gs_att)

        def reduce(g):
            total = lax.psum_scatter(g, "dp", scatter_dimension=0, tiled=True)
            return lax.psum(total, "group").astype(F32)

        gqkv = gqkv.reshape(3, D, 3, THIRD).transpose(1, 2, 0, 3).reshape(D, 3 * D)
        gup = gup.transpose(1, 0, 2).reshape(D, FF)
        rqkv, rout, rup, rdown = [reduce(g) for g in (gqkv, gout, gup, gdown.reshape(FF, D))]
        gs = lax.psum(gs_mlp + gs_qkv, ("group", "dp"))

        def own(first, count):
            flat = gs[first : first + count].reshape(dp, -1)
            return lax.dynamic_index_in_dim(flat, p, 0, keepdims=False)

        tinies = [own(first, v.shape[0] * dp // D) for first, v in zip(SMALL_ROWS, vectors)]

    g1, s1, qb, fr, ob, g2, s2, ub, db = tinies
    act, gin = act.reshape(images.shape), gin.reshape(images.shape)
    return (act, gin, g1, s1, rqkv, qb, fr, rout, ob, g2, s2, rup, ub, rdown, db)


def solution(mesh):
    batch = P(("group", "dp"), None, None)
    per_image = P(("group", "dp"))
    vec, mat = P("dp"), P("dp", None)
    fast = dict(mesh.shape) == {"group": 4, "dp": 8}
    return jax.shard_map(
        functools.partial(on_device, fast),
        mesh=mesh,
        in_specs=(batch, batch, per_image, per_image, P(), vec, vec, mat, vec, vec, mat, vec, vec, vec, mat, vec, mat, vec),
        out_specs=(batch, batch, vec, vec, mat, vec, vec, mat, vec, vec, vec, mat, vec, mat, vec),
        check_vma=False,
    )
```

```python
import functools
import math

import jax
import jax.numpy as jnp
from jax import lax
from jax.experimental import pallas as pl
from jax.experimental.pallas import tpu as pltpu
from jax.sharding import PartitionSpec as P

HEADS = 12
HD = 64
SIDE_S = 14
SIDE_M = 20
SIDE_L = 24
SLOT = 576
D = 768
FF = 3072
LN_EPS = 1e-06
MASK_FILL = -1e30
BF = jnp.bfloat16
F32 = jnp.float32
NT = (((1,), (1,)), ((), ()))
NN = (((1,), (0,)), ((), ()))
TN = (((0,), (0,)), ((), ()))
R_G1, R_S1, R_QB, R_FR, R_OB, R_G2, R_S2, R_UB, R_DB, R_ALL = 0, 1, 2, 5, 6, 7, 8, 9, 13, 16
THIRD = 256
LOG2E = math.log2(math.e)


def dot(a, b, dims, precision=None):
    return lax.dot_general(a, b, dims, preferred_element_type=F32, precision=precision)


def vm(n):
    return [pl.BlockSpec(memory_space=pltpu.VMEM)] * n


def norm_stats(x):
    mean = jnp.mean(x, axis=-1, keepdims=True)
    cen = x - mean
    var = jnp.mean(cen * cen, axis=-1, keepdims=True)
    inv = lax.rsqrt(var + LN_EPS)
    return cen * inv, inv


def sincos(x):
    n = jnp.floor(x * (2.0 / math.pi) + 0.5)
    r = x - n * 1.5703125
    r = r - n * 4.837512969970703125e-4
    r = r - n * 7.54978995489188216e-8
    q = n.astype(jnp.int32)
    r2 = r * r
    s = r + r * r2 * (-1.6666654611e-1 + r2 * (8.3321608736e-3 + r2 * -1.9515295891e-4))
    c = 1.0 - 0.5 * r2 + r2 * r2 * (
        4.166664568298827e-2 + r2 * (-1.388731625493765e-3 + r2 * 2.443315711809948e-5)
    )
    odd = (q & 1) == 1
    ss = jnp.where(odd, c, s)
    cc = jnp.where(odd, s, c)
    ss = jnp.where((q & 2) == 2, -ss, ss)
    cc = jnp.where(((q + 1) & 2) == 2, -cc, cc)
    return ss, cc


ERFC = (
    0.07314588129520416,
    -0.30809587240219116,
    0.3798876702785492,
    -0.08230462670326233,
    0.245080828666687,
    0.2054724544286728,
    0.24429383873939514,
    0.242519810795784,
)


def gelu_pair(x):
    z = jnp.abs(x)
    t = 1.0 / (1.0 + (0.43 * math.sqrt(0.5)) * z)
    poly = 0.5 * ERFC[0]
    for c in ERFC[1:]:
        poly = poly * t + 0.5 * c
    bell = jnp.exp2((x * x) * (-0.5 * LOG2E))
    half = poly * t * bell
    cdf = jnp.where(x < 0, half, 1.0 - half)
    return x * cdf, cdf + (x * math.sqrt(0.5 / math.pi)) * bell


def swap_halves(x):
    width = x.shape[-1]
    lane = lax.broadcasted_iota(jnp.int32, (1, width), 1)
    ahead = pltpu.roll(x, width - HD // 2, 1)
    behind = pltpu.roll(x, HD // 2, 1)
    return jnp.where(lane % HD < HD // 2, ahead, behind)


def half_sign(width):
    lane = lax.broadcasted_iota(jnp.int32, (1, width), 1)
    return jnp.where(lane % HD < HD // 2, 1.0, -1.0).astype(F32)


def side_of(res_ref, image):
    res = res_ref[image]
    return jnp.where(res == 0, SIDE_S, jnp.where(res == 1, SIDE_M, SIDE_L))


def device_weight(slots, assign_ref, counts_ref):
    groups = counts_ref.shape[0]
    counts = [jnp.full((1, 128), counts_ref[i], jnp.int32).astype(F32) for i in range(groups)]
    mine = jnp.full((1, 128), assign_ref[0], jnp.int32)
    picked = sum(jnp.where(mine == i, counts[i], 0.0) for i in range(groups))
    return (groups * picked / sum(counts) * (1.0 / math.sqrt(slots)))[:, :1]


def patch_columns(side_ref, image):
    side = jnp.full((SLOT, 128), side_of(side_ref, image), jnp.int32).astype(F32)
    slot = lax.broadcasted_iota(jnp.int32, (SLOT, 128), 0).astype(F32)
    row = jnp.floor((slot + 0.5) / side)
    col = slot - row * side
    valid = slot < side * side
    return col, row, valid


def spread(parity):
    src = lax.broadcasted_iota(jnp.int32, (128, 128), 0)
    lane = lax.broadcasted_iota(jnp.int32, (128, 128), 1)
    return (src == parity * HD + (lane // HD) * (HD // 2) + lane % (HD // 2)).astype(BF)


class Place:
    def __init__(self):
        self.p = lax.axis_index("dp")
        self.g = lax.axis_index("group")
        self.z, self.y = self.p // 2, self.p % 2
        self.x, self.core = self.g // 2, self.g % 2

    def over(self):
        return (self.g, self.p ^ 1)

    def sibling(self):
        return (self.g ^ 1, self.p)

    def across(self):
        return (self.g ^ 2, self.p)

    def line(self):
        return [(self.g, self.p ^ (2 * k)) for k in (1, 2, 3)]

    def partners(self):
        return [self.sibling(), self.across(), self.over()] + self.line()


def remote(src, dst, send, recv, device):
    return pltpu.make_async_remote_copy(
        src_ref=src, dst_ref=dst, send_sem=send, recv_sem=recv, device_id=device, device_id_type=pl.DeviceIdType.MESH
    )


def load(src, dst, sem):
    copy = pltpu.make_async_copy(src, dst, sem)
    copy.start()
    return copy


def greet(devices):
    barrier = pltpu.get_barrier_semaphore()
    for device in devices:
        pl.semaphore_signal(barrier, inc=1, device_id=device, device_id_type=pl.DeviceIdType.MESH)
    pl.semaphore_wait(barrier, len(devices))


def timetable(plan):
    return sorted(((step, name, stage) for name, steps in plan.items() for stage, step in enumerate(steps)), key=lambda r: r[0])


class Moves:
    def __init__(self, items, plan):
        self.items, self.rows = items, timetable(plan)

    def at(self, step):
        for when, name, stage in self.rows:
            if when == step:
                self.items[name].stage(stage)

    def within(self, step, first, last):
        for when in sorted({r[0] for r in self.rows if first <= r[0] <= last}):
            pl.when(step == when)(functools.partial(self.at, when))


class Gather:
    STAGES = 5

    def __init__(self, place, own, full, sems, recv, index):
        self.w, self.own, self.full = place, own, full
        self.rows = full.shape[0] // 8
        self.t = self.rows // 3 if self.rows % 48 == 0 else self.rows * 3 // 8
        self.e = self.rows - 2 * self.t
        self.send, self.sib = sems.at[2 * index], sems.at[2 * index + 1]
        self.recv = recv.at[index]

    def part(self, block, piece, ref=None):
        ref = self.full if ref is None else ref
        first = block * self.rows + piece * self.t
        return ref.at[pl.ds(pl.multiple_of(first, 16), self.e if isinstance(piece, int) else self.t)]

    def push(self, ref, device, index, src=None):
        remote(ref if src is None else src, ref, self.send, self.recv.at[index], device).start()

    def got(self, ref, index):
        remote(ref, ref, self.send, self.recv.at[index], self.w.sibling()).wait_recv()

    def hand(self, ref):
        remote(ref, ref, self.send, self.sib, self.w.sibling()).start()

    def stage(self, number):
        w = self.w
        pl.when(w.core == 0)(lambda: self.step(number, w.x, True))
        pl.when(w.core == 1)(lambda: self.step(number, 2, False))

    def step(self, number, piece, split):
        w = self.w
        if number == 0:
            src = self.part(0, piece, self.own)
            for k in (1, 3, 2):
                self.push(self.part(w.p, piece), (w.g, w.p ^ (2 * k)), w.z, src)
            self.push(self.part(w.p, piece), w.over(), 4 + w.z, src)
        elif number in (1, 2):
            for k in (1, 3, 2) if number == 1 else (0, 1, 3, 2):
                z = w.z ^ k
                block = 2 * z + (w.y if number == 1 else 1 - w.y)
                ref = self.part(block, piece)
                self.got(ref, z if number == 1 else 4 + z)
                if number == 1:
                    self.push(ref, w.over(), 4 + z)
                if split:
                    self.push(ref, w.across(), 8 + block)
                self.hand(ref)
        elif number == 3:
            if split:
                for k in (2, 6, 4, 1, 3, 7, 5):
                    block = w.p ^ k
                    ref = self.part(block, 1 - w.x)
                    self.got(ref, 8 + block)
                    self.hand(ref)
        else:
            for count in (14 * self.t, 14 * self.t) if split else (14 * self.e,):
                done = self.full.at[pl.ds(0, count)]
                remote(done, done, self.send, self.sib, w.sibling()).wait_send()
            came = self.full.at[pl.ds(0, 7 * self.e if split else 14 * self.t)]
            remote(came, came, self.send, self.sib, w.sibling()).wait_recv()


class Reduce:
    STAGES = 7

    def __init__(self, place, src, bufs, out, local, send, recv):
        self.w, self.src, self.out = place, src, out
        self.mine, self.cbuf, self.ybuf, self.zbuf, self.xbuf, self.fbuf = bufs
        self.rows = src.shape[0] // 8
        self.t, self.e = self.split(self.rows)
        self.local, self.send, self.recv = local, send, recv

    @staticmethod
    def split(rows):
        t = rows // 4 if rows % 64 == 0 else rows // 3
        return t, rows - 2 * t

    @classmethod
    def buffers(cls, rows, width):
        t, e = cls.split(rows)
        big = max(2 * t, e)
        sizes = (8 * big, 8 * big, 4 * max(t, e), 4 * max(t, e), 8 * t, max(t, e))
        return [pltpu.VMEM((n, width), BF) for n in sizes]

    def copy(self, src, dst, index, device):
        return remote(src, dst, self.send, self.recv.at[index], device)

    def took(self, ref, index):
        self.copy(ref, ref, index, self.w.sibling()).wait_recv()

    def rows_of(self, ref, first, count):
        return ref.at[pl.ds(pl.multiple_of(first, 16), count)]

    def add(self, target, *terms):
        def body(i, _):
            rows = pl.ds(pl.multiple_of(i * 32, 32), 32)
            if len(terms) == 1:
                target[rows] = target[rows] + terms[0][rows]
                return 0
            total = target[rows].astype(F32)
            for term in terms:
                total = total + term[rows].astype(F32)
            target[rows] = total.astype(BF)
            return 0

        lax.fori_loop(0, target.shape[0] // 32, body, 0)

    def each_core(self, first, second):
        pl.when(self.w.core == 0)(first)
        pl.when(self.w.core == 1)(second)

    def exchange(self, theirs, their_rows, ours, our_rows):
        def body(b, _):
            self.copy(
                self.rows_of(self.src, b * self.rows + theirs, their_rows),
                self.rows_of(self.cbuf, b * their_rows, their_rows),
                0,
                self.w.sibling(),
            ).start()
            pltpu.make_async_copy(
                self.rows_of(self.src, b * self.rows + ours, our_rows),
                self.rows_of(self.mine, b * our_rows, our_rows),
                self.local,
            ).start()
            return 0

        lax.fori_loop(0, 8, body, 0)

    def settle(self, count):
        whole = self.mine.at[pl.ds(0, 8 * count)]
        pltpu.make_async_copy(whole, whole, self.local).wait()
        self.took(self.cbuf.at[pl.ds(0, 8 * count)], 0)
        self.add(whole, self.cbuf)

    def zero_at(self, block, piece):
        return self.rows_of(self.mine, block * 2 * self.t + piece * self.t, self.t)

    def one_at(self, block):
        return self.rows_of(self.mine, block * self.e, self.e)

    def send_y(self, count, at):
        w = self.w

        def body(z, _):
            self.copy(at(2 * z + 1 - w.y), self.rows_of(self.ybuf, z * count, count), 2, w.over()).start()
            return 0

        lax.fori_loop(0, 4, body, 0)

    def take_y(self, count, at):
        self.took(self.ybuf.at[pl.ds(0, 4 * count)], 2)

        def body(z, _):
            self.add(at(2 * z + self.w.y), self.rows_of(self.ybuf, z * count, count))
            return 0

        lax.fori_loop(0, 4, body, 0)

    def send_z(self, count, at):
        w = self.w
        for k in (3, 1, 2):
            z = w.z ^ k
            self.copy(at(2 * z + w.y), self.rows_of(self.zbuf, k * count, count), 3, (w.g, 2 * z + w.y)).start()

    def take_z(self, count, at):
        self.took(self.zbuf.at[pl.ds(0, 3 * count)], 3)
        self.add(at(self.w.p), *[self.rows_of(self.zbuf, k * count, count) for k in (1, 2, 3)])

    def give(self, first, count, value):
        ref = self.out.at[pl.ds(pl.multiple_of(first, 8), count)]
        ref[...] = value
        remote(ref, ref, self.send, self.recv.at[5], self.w.sibling()).start()

    def stage(self, number):
        w, t, e = self.w, self.t, self.e
        x_mine = functools.partial(self.zero_at, piece=w.x)
        x_other = functools.partial(self.zero_at, piece=1 - w.x)
        if number == 0:
            self.each_core(lambda: self.exchange(2 * t, e, 0, 2 * t), lambda: self.exchange(0, 2 * t, 2 * t, e))
        elif number == 1:

            def first():
                self.settle(2 * t)

                def body(b, _):
                    self.copy(x_other(b), self.rows_of(self.xbuf, b * t, t), 1, w.across()).start()
                    return 0

                lax.fori_loop(0, 8, body, 0)

            def second():
                self.settle(e)
                self.send_y(e, self.one_at)

            self.each_core(first, second)
        elif number == 2:

            def first():
                self.took(self.xbuf, 1)

                def body(b, _):
                    self.add(x_mine(b), self.rows_of(self.xbuf, b * t, t))
                    return 0

                lax.fori_loop(0, 8, body, 0)
                self.send_y(t, x_mine)

            def second():
                self.take_y(e, self.one_at)
                self.send_z(e, self.one_at)

            self.each_core(first, second)
        elif number == 3:

            def first():
                self.take_y(t, x_mine)
                self.send_z(t, x_mine)

            def second():
                self.take_z(e, self.one_at)
                self.copy(self.one_at(w.p), self.fbuf.at[pl.ds(0, e)], 4, w.across()).start()

            self.each_core(first, second)
        elif number == 4:

            def first():
                self.take_z(t, x_mine)
                self.copy(x_mine(w.p), self.fbuf.at[pl.ds(0, t)], 4, w.across()).start()
                self.give(w.x * t, t, x_mine(w.p)[...].astype(F32))

            def second():
                self.took(self.fbuf.at[pl.ds(0, e)], 4)
                self.give(2 * t, e, self.one_at(w.p)[...].astype(F32) + self.fbuf[pl.ds(0, e)].astype(F32))

            self.each_core(first, second)
        elif number == 5:

            @pl.when(w.core == 0)
            def _():
                self.took(self.fbuf.at[pl.ds(0, t)], 4)
                self.give((1 - w.x) * t, t, self.fbuf[pl.ds(0, t)].astype(F32))

        else:

            def sent(count):
                while count > 0:
                    now = min(count, self.mine.shape[0])
                    part = self.mine.at[pl.ds(0, now)]
                    remote(part, part, self.send, self.recv.at[0], w.sibling()).wait_send()
                    count -= now

            def came(first, count):
                ref = self.out.at[pl.ds(first, count)]
                remote(ref, ref, self.send, self.recv.at[5], w.sibling()).wait_recv()

            def first():
                came(2 * t, e)
                sent(8 * e + 8 * t + 4 * t + 3 * t + t + 4 * t)

            def second():
                came(0, 2 * t)
                sent(16 * t + 4 * e + 3 * e + e + 2 * e)

            self.each_core(first, second)


class SmallSum:
    HOPS = (4, 2, 4)

    def __init__(self, place, value, bufs, send, recv):
        self.w, self.value, self.bufs, self.send, self.recv = place, value, bufs, send, recv

    def copies(self, hop):
        w = self.w
        for k in range(1, self.HOPS[hop]):
            device = ((w.g ^ k, w.p), (w.g, w.p ^ k), (w.g, w.p ^ (2 * k)))[hop]
            ref = self.bufs.at[4 * hop]
            yield remote(ref, self.bufs.at[4 * hop + k], self.send.at[hop, k], self.recv.at[hop, k], device)

    def stage(self, number):
        w = self.w
        if number > 0:
            hop = number - 1
            for copy in self.copies(hop):
                copy.wait()
            mine = (w.g, w.y, w.z)[hop]
            total = self.bufs[4 * hop + mine]
            for k in range(1, self.HOPS[hop]):
                total = total + self.bufs[4 * hop + (mine ^ k)]
        else:
            total = self.value[...]
        if number == 3:
            self.value[...] = total
        else:
            self.bufs[4 * number] = total
            for copy in self.copies(number):
                copy.start()


def mask_column(side_ref, image):
    side = side_of(side_ref, image)
    slot = lax.broadcasted_iota(jnp.int32, (SLOT, 1), 0)
    return jnp.where(slot < side * side, 0.0, MASK_FILL).astype(F32)


def head_pair(images, step):
    i, j = step % images, step // images
    rows = pl.ds(pl.multiple_of(i * SLOT, SLOT), SLOT)
    return i, rows, pl.multiple_of(j * 128, 128), pl.multiple_of((j // 2) * D + (j % 2) * 128, 128)


def attend_step(images, step, side_ref, qkv_ref, ctx_ref, lse_ref):
    i, rows, c, at = head_pair(images, step)
    q = qkv_ref[rows, pl.ds(at, 128)]
    k = qkv_ref[rows, pl.ds(at + THIRD, 128)]
    v = qkv_ref[rows, pl.ds(at + 2 * THIRD, 128)]
    lane = lax.broadcasted_iota(jnp.int32, (1, 128), 1)
    mask = mask_column(side_ref, i)
    outs, logs = [], []
    for h in range(2):
        qm = jnp.where(lane // HD == h, q, jnp.zeros_like(q))
        s = dot(k, qm, NT) * (LOG2E / math.sqrt(HD)) + mask
        top = jnp.max(s, axis=0, keepdims=True)
        e = jnp.exp2(s - top)
        total = jnp.sum(e, axis=0, keepdims=True)
        p = (e * (1.0 / total)).astype(BF)
        outs.append(dot(p, v, TN))
        logs.append(top + jnp.log2(total))
    ctx_ref[rows, pl.ds(c, 128)] = jnp.where(lane < HD, outs[0], outs[1]).astype(BF)
    lse_ref[step] = jnp.concatenate(logs + [jnp.zeros((6, SLOT), F32)], axis=0)


def norm_rows(images, x_ref, small, norm_ref):
    def body(step, _):
        rows = pl.ds(pl.multiple_of(step * 192, 192), 192)
        unit, _ = norm_stats(x_ref[rows])
        norm_ref[rows] = (unit * small[R_G1 : R_G1 + 1] + small[R_S1 : R_S1 + 1]).astype(BF)
        return 0

    lax.fori_loop(0, images * SLOT // 192, body, 0)


def angle_tables(images, side_ref, small, cos_ref, sin_ref, hooks):
    for j in range(D // 128):
        hooks("table", j)
        flat = [small[R_FR : R_FR + 1, n + j // 2 * 128 : n + j // 2 * 128 + 128] for n in (0, D // 2)]
        fc, fr = [dot(jnp.broadcast_to(v, (8, 128)).astype(BF), spread(j % 2), NN)[0:1] for v in flat]

        def body(i, _):
            rows = pl.ds(pl.multiple_of(i * SLOT, SLOT), SLOT)
            col, row, _ = patch_columns(side_ref, i)
            sn, cs = sincos(col * fc + row * fr)
            cos_ref[rows, pl.ds(j * 128, 128)] = cs
            sin_ref[rows, pl.ds(j * 128, 128)] = sn * -half_sign(128)
            return 0

        lax.fori_loop(0, images, body, 0)


def project_block(images, c, r, small, w_ref, norm_ref, qkv_ref, cos_ref, sin_ref):
    i, part = r % images, r // images
    rows = pl.ds(pl.multiple_of(i * SLOT, SLOT), SLOT)
    cols = pl.ds(pl.multiple_of(part * THIRD, THIRD), THIRD)
    lanes = pl.ds(pl.multiple_of(c * D + part * THIRD, THIRD), THIRD)
    inner = pl.ds(pl.multiple_of(c * THIRD, THIRD), THIRD)
    raw = dot(norm_ref[rows], w_ref[c, :, cols], NN) + small[pl.ds(R_QB + part, 1), inner]

    @pl.when(part < 2)
    def _():
        turned = raw * cos_ref[rows, inner] + swap_halves(raw) * sin_ref[rows, inner]
        qkv_ref[rows, lanes] = turned.astype(BF)

    @pl.when(part == 2)
    def _():
        qkv_ref[rows, lanes] = raw.astype(BF)


def forward_compute(images, side_ref, x_ref, small, w_ref, qkv, norm, cos, sin, ctx_ref, lse_ref, hooks):
    hooks("start")
    norm_rows(images, x_ref, small, norm)
    hooks("tables")
    angle_tables(images, side_ref, small, cos, sin, hooks)
    blocks, pairs = 3 * images, 2 * images

    def body(step, _):
        hooks("step", step)
        c, r = step // (blocks + pairs), step % (blocks + pairs)

        @pl.when(r < blocks)
        def _():
            project_block(images, c, r, small, w_ref, norm, qkv, cos, sin)

        @pl.when(r >= blocks)
        def _():
            attend_step(images, c * pairs + r - blocks, side_ref, qkv, ctx_ref, lse_ref)

        return 0

    lax.fori_loop(0, 3 * (blocks + pairs), body, 0)
    hooks("end")


def forward_plain(images, side_ref, x_ref, small_ref, w_ref, *refs):
    qkv, norm, cos, sin, ctx, lse = refs
    forward_compute(images, side_ref, x_ref, small_ref, w_ref, qkv, norm, cos, sin, ctx, lse, lambda *a: None)


def packed_places(p, dp, sizes):
    run = D // dp
    for first, size in zip(SMALL_ROWS, sizes):
        count = size // run
        yield [(first + (p * count + m) // dp, ((p * count + m) % dp) * run) for m in range(count)]


SMALL_ROWS = (R_G1, R_S1, R_QB, R_FR, R_OB, R_G2, R_S2, R_UB, R_DB)


SINGLES = (R_G1, R_S1, R_FR, R_OB, R_G2, R_S2, R_DB)
MORE = ((2, R_QB, 3, 8), (7, R_UB, 4, 11))


def compact(tinies, ref):
    run = tinies[0].shape[0]
    first = {row: i for i, row in enumerate(SMALL_ROWS)}
    for n, row in enumerate(SINGLES):
        ref[n, pl.ds(0, run)] = tinies[first[row]][...].astype(BF).astype(F32)
    for index, _, count, at in MORE:
        for m in range(count):
            ref[at + m, pl.ds(0, run)] = tinies[index][pl.ds(m * run, run)].astype(BF).astype(F32)


def expand(parts, small, run):
    small[...] = jnp.zeros_like(small)
    lane = lax.broadcasted_iota(jnp.int32, (1, 128), 1)
    total = None
    for owner, ref in parts:
        wide = jnp.concatenate([jnp.where(lane < run, ref[...], 0.0), jnp.zeros((R_ALL, D - 128), F32)], axis=1)
        term = pltpu.roll(wide[0:8], owner * run, 1)
        total = term if total is None else total + term
        for _, row, count, at in MORE:
            for m in range(count):
                place = owner * count + m
                moved = pltpu.roll(jnp.broadcast_to(wide[at + m : at + m + 1], (8, D)), (place % 8) * run, 1)
                small[pl.ds(row + place // 8, 1), :] += moved[0:1]
    for n, row in enumerate(SINGLES):
        small[row : row + 1] = total[n : n + 1]


def forward_gather(images, side_ref, *refs):
    tinies, x_in, shards_in = refs[0:9], refs[9], refs[10:14]
    qkv_out, norm_out, cos_out, sin_out, ctx, lse, small, wq_out, wo, wu, wd, up_later, down_later = refs[14:27]
    x_ref, qkv, norm, cos, sin, wq, slots, bq, bo, bu, bd, sq, so, su, sd = refs[27:42]
    sems, recv, psend, precv, local, ins = refs[42:]
    w = Place()
    pairs = [(bq.at[c], wq.at[c]) for c in range(3)] + [(bo, wo)]
    pairs += [(own.at[c], full.at[c]) for c in range(PARTS - 1) for own, full in ((bu, wu), (bd, wd))]
    lanes = [pl.ds(part * THIRD, THIRD) for part in range(3)]
    gathers = [(bq.at[0, :, cols], wq.at[0, :, cols]) for cols in lanes] + pairs[1:]
    gathers = dict(zip(("a0", "a1", "a2", "q1", "q2", "o", "u0", "d0", "u1", "d1"), gathers))
    gathers = {k: Gather(w, *v, sems, recv, i) for i, (k, v) in enumerate(gathers.items())}
    moves = Moves(gathers, FORWARD_PLAN)
    peers = [w.p ^ k for k in range(1, 8)]
    keep = {}

    def store(name, src, dst):
        keep[name] = load(src, dst, local.at[len(keep)])

    def qkv_third(c):
        lanes = pl.ds(c * D, D)
        return pltpu.make_async_copy(qkv.at[:, lanes], qkv_out.at[:, lanes], local.at[16 + c])

    def late(number):
        src, dst = ((cos, cos_out), (sin, sin_out), (wq, wq_out))[number]
        return pltpu.make_async_copy(src, dst, local.at[19 + number])

    def own_rows(full):
        count = full.shape[0] // 8
        return full.at[pl.ds(pl.multiple_of(w.p * count, 16), count)]

    def pack_copy(k):
        return remote(slots.at[0], slots.at[k], psend.at[k - 1], precv.at[k - 1], (w.g, peers[k - 1]))

    def hooks(where, step=None):
        if where == "start":
            reads = [
                load(src, dst, ins.at[i])
                for i, (src, dst) in enumerate(zip(shards_in[:1] + (x_in,) + shards_in[1:], (sq, x_ref, so, su, sd)))
            ]
            compact(tinies, slots.at[0])
            greet([(w.g, q) for q in peers] + [w.sibling(), w.across()])
            for k in range(1, 8):
                pack_copy(k).start()
            reads[0].wait()
            for c in range(3):
                for part in range(3):
                    cols = part * D + c * THIRD
                    bq[c, :, part * THIRD : (part + 1) * THIRD] = sq[:, cols : cols + THIRD].astype(BF)
                if c == 0:
                    moves.at(-1)
            for copy in reads[1:]:
                copy.wait()
            bo[...] = so[...].astype(BF)
            for c in range(PARTS):
                for b in range(8):
                    cols = (b * PARTS + c) * 128
                    bu[c, :, b * 128 : (b + 1) * 128] = su[:, cols : cols + 128].astype(BF)
                bd[c] = sd[c * 128 : (c + 1) * 128].astype(BF)
            for i, (own, full) in enumerate(pairs):
                store(i, own, own_rows(full))
            store("up", bu.at[PARTS - 1], up_later)
            store("down", bd.at[PARTS - 1], down_later)
            for k in range(1, 8):
                pack_copy(k).wait()
            expand([(w.p, slots.at[0])] + [(peers[k - 1], slots.at[k]) for k in range(1, 8)], small, D // 8)
            moves.at(0)
        elif where == "tables":
            store("norm", norm, norm_out)
        elif where == "table":
            moves.at(1 + step / 10)
        elif where == "step":

            @pl.when(step == 0)
            def _():
                for i in range(3):
                    keep[i].wait()
                for number in (0, 1):
                    late(number).start()

            moves.within(step + 2, 2, 31)
            for c in (1, 2):

                @pl.when(step == 10 * c)
                def _(c=c):
                    qkv_third(c - 1).start()
                    if c == 2:
                        late(2).start()

        else:
            qkv_third(2).start()
            moves.at(32)
            for c in range(3):
                qkv_third(c).wait()
                late(c).wait()
            for name, copy in keep.items():
                if name not in (0, 1, 2):
                    copy.wait()

    forward_compute(images, side_ref, x_ref, small, wq, qkv, norm, cos, sin, ctx, lse, hooks)


FORWARD_PLAN = {
    "a0": (-1, 1, 1.2, 1.4, 2),
    "a1": (-1, 1, 1.2, 1.4, 4),
    "a2": (-1, 1, 1.3, 1.5, 6),
    "q1": (0, 1.5, 8, 11, 12),
    "q2": (1, 7, 12, 18, 22),
    "o": (1.5, 7, 13, 26, 32),
    "u0": (3, 12, 20, 27, 32),
    "d0": (7, 17, 22, 29, 32),
    "u1": (13, 23, 28, 31, 32),
    "d1": (9, 20, 26, 30, 32),
}


def bias_at(split, step):
    c, k = step // BLOCKS, step % BLOCKS
    if split:
        return (R_UB + k, c * 128), (R_UB + k, D // 2 + c * 128)
    return (R_UB + step // 3, (step % 3) * 256), (R_UB + step // 3, (step % 3) * 256 + 128)


def mlp_compute(images, split, side_ref, scale, cot_ref, ctx_ref, small, wo_ref, wu, wd, refs, outs, hooks):
    mid, n2, n2t, bl, hid, gpre, ubias, gubias = refs
    act, gm, gctx, gdown, gup, gout, gs = outs
    rows_all = images * SLOT
    tile = SLOT // 2
    hooks("start")
    gain = small[R_G2 : R_G2 + 1]
    gs[...] = jnp.zeros_like(gs)
    for step in range(PARTS * BLOCKS):
        for n, (r, l) in enumerate(bias_at(split, step)):
            ubias[step : step + 1, n * 128 : (n + 1) * 128] = small[r : r + 1, l : l + 128]

    def tile_rows(step):
        side = side_of(side_ref, step // 2)
        slot = lax.broadcasted_iota(jnp.int32, (tile, 1), 0) + (step % 2) * tile
        return pl.ds(pl.multiple_of(step * tile, tile), tile), slot < side * side

    def enter(step, _):
        hooks("enter", step)
        rows, valid = tile_rows(step)
        middle = mid[rows] + (dot(ctx_ref[rows], wo_ref[...], NN) + small[R_OB : R_OB + 1])
        mid[rows] = middle
        act[rows] = middle + small[R_DB : R_DB + 1]
        unit, _ = norm_stats(middle)
        n2[rows] = (unit * gain + small[R_S2 : R_S2 + 1]).astype(BF)
        low = jnp.where(valid, cot_ref[rows], 0.0).astype(BF)
        bl[rows] = low
        gs[R_DB : R_DB + 1] += jnp.sum(low.astype(F32), axis=0, keepdims=True)
        return 0

    lax.fori_loop(0, 2 * images, enter, 0)
    gm[...] = jnp.zeros_like(gm)
    n2t[...] = n2[...].T
    hooks("entered")

    first = pl.ds(0, 256)
    hid[:, first] = jnp.zeros((rows_all, 256), BF)
    gpre[:, first] = jnp.zeros((rows_all, 256), BF)

    def weights(step):
        c = step // BLOCKS
        cols = pl.ds(pl.multiple_of((step % BLOCKS) * 256, 256), 256)
        gdown[c, cols, :] = (dot(hid[:, cols], bl[...], TN) * scale).astype(BF)
        gup[c, :, cols] = (dot(n2t[...], gpre[:, cols], NN) * scale).astype(BF)

    def block(step, _):
        hooks("block", step)
        c, k = step // BLOCKS, step % BLOCKS
        cols = pl.ds(pl.multiple_of(k * 256, 256), 256)
        bias = ubias[pl.ds(step, 1), :]
        wuc = wu[c, :, cols]
        wdc = wd[c, cols, :]
        weights(jnp.maximum(step - 1, 0))
        pieces = [pl.ds(i * tile, tile) for i in range(2 * images)]
        pres = [dot(n2[rows], wuc, NN) + bias for rows in pieces]
        backs = [dot(bl[rows], wdc, NT) for rows in pieces]
        bsum = None
        for rows, pre, back in zip(pieces, pres, backs):
            value, slope = gelu_pair(pre)
            hid[rows, cols] = value.astype(BF)
            g = (back * slope).astype(BF)
            gpre[rows, cols] = g
            part = jnp.sum(g.astype(F32), axis=0, keepdims=True)
            bsum = part if bsum is None else bsum + part
        gubias[pl.ds(step, 1), :] = bsum

        @pl.when(k == BLOCKS - 1)
        def _():
            def tail(n, _):
                rows = pl.ds(pl.multiple_of(n * SLOT, SLOT), SLOT)
                act[rows] += dot(hid[rows], wd[c], NN)
                gm[rows] += dot(gpre[rows], wu[c], NT)
                return 0

            lax.fori_loop(0, images, tail, 0)

        return 0

    lax.fori_loop(0, PARTS * BLOCKS, block, 0)
    weights(PARTS * BLOCKS - 1)
    hooks("blocks")

    def leave(step, _):
        rows, valid = tile_rows(step)
        unit, inv = norm_stats(mid[rows])
        act[rows] = jnp.where(valid, act[rows], 0.0)
        gn = gm[rows]
        gs[R_G2 : R_G2 + 1] += jnp.sum(gn * unit, axis=0, keepdims=True)
        gs[R_S2 : R_S2 + 1] += jnp.sum(gn, axis=0, keepdims=True)
        a = gn * gain
        ma = jnp.mean(a, axis=-1, keepdims=True)
        mu = jnp.mean(a * unit, axis=-1, keepdims=True)
        g = jnp.where(valid, cot_ref[rows], 0.0) + inv * (a - ma - unit * mu)
        gm[rows] = g
        low = g.astype(BF)
        bl[rows] = low
        gs[R_OB : R_OB + 1] += jnp.sum(low.astype(F32), axis=0, keepdims=True)
        gctx[rows] = dot(low, wo_ref[...], NT).astype(BF)
        hooks("left", step)
        return 0

    lax.fori_loop(0, 2 * images, leave, 0)
    for step in range(PARTS * BLOCKS):
        for n, (r, l) in enumerate(bias_at(split, step)):
            gs[r : r + 1, l : l + 128] = gubias[step : step + 1, n * 128 : (n + 1) * 128]
    gout[...] = (dot(ctx_ref[...], bl[...], TN) * scale).astype(BF)
    gs[...] = gs[...] * scale
    hooks("end")


def mlp_scratch(rows):
    vmem = pltpu.VMEM
    return (
        [vmem((rows, D), F32), vmem((rows, D), BF), vmem((D, rows), BF), vmem((rows, D), BF)]
        + [vmem((rows, FF // PARTS), BF)] * 2
        + [vmem((16, 256), F32)] * 2
    )


def mlp_plain(images, slots, side_ref, assign_ref, counts_ref, x_ref, cot_ref, ctx_ref, small, wo_ref, wu, wd, *rest):
    outs, refs, sem = rest[0:7], rest[7:15], rest[15]
    load(x_ref, refs[0], sem.at[0]).wait()
    mlp_compute(
        images, False, side_ref, device_weight(slots, assign_ref, counts_ref), cot_ref, ctx_ref, small, wo_ref, wu, wd, refs, outs, lambda *a: None
    )


def mlp_moving(images, slots, side_ref, assign_ref, counts_ref, small, *rest):
    x_in, cot_in, ctx_in, wo_in, wu_in, wd_in, up_later, down_later = rest[0:8]
    act_out, gm_out, gctx_out, gd_out, gu_out, go_out, gs, rd, ru = rest[8:17]
    refs = rest[17:25]
    mid, n2, n2t = refs[0], refs[1], refs[2]
    cot, ctx, wo, wu, wd, act, gm, gd, gu = rest[25:34]
    bufs, (local, sems, recv, rlocal, rsend, rrecv, tile_in, tile_out) = rest[34:46], rest[46:54]
    w = Place()
    last = PARTS - 1
    items = {
        "u": Gather(w, up_later, wu.at[last], sems, recv, 0),
        "d": Gather(w, down_later, wd.at[last], sems, recv, 1),
        "rd": Reduce(w, gd.at[0], bufs[0:6], rd, rlocal.at[0], rsend.at[0], rrecv.at[0]),
        "ru": Reduce(w, gu.at[0], bufs[6:12], ru, rlocal.at[1], rsend.at[1], rrecv.at[1]),
    }
    moves = Moves(items, MLP_PLAN)
    keep = []

    def move(src, dst):
        keep.append(load(src, dst, local.at[len(keep)]))
        return keep[-1]

    tile = SLOT // 2

    def by_tile(step, pairs, sem):
        rows = pl.ds(pl.multiple_of(step * tile, tile), tile)
        return [pltpu.make_async_copy(src.at[rows], dst.at[rows], sem.at[i, step]) for i, (src, dst) in enumerate(pairs)]

    def arriving(step):
        return by_tile(step, ((ctx_in, ctx), (x_in, mid), (cot_in, cot)), tile_in)

    def leaving(step):
        return by_tile(step, ((act, act_out), (gm, gm_out), (n2, gctx_out)), tile_out)

    def hooks(where, step=None):
        if where == "start":
            move(wo_in, wo)
            for i in range(2 * images):
                for copy in arriving(i):
                    copy.start()
            for c in range(last):
                move(wu_in.at[c], wu.at[c])
                move(wd_in.at[c], wd.at[c])
            for own, full in ((up_later, wu), (down_later, wd)):
                count = full.shape[1] // 8
                move(own, full.at[last, pl.ds(pl.multiple_of(w.p * count, 16), count)])
            greet(w.partners())
            moves.at(0)
            keep[0].wait()
        elif where == "enter":
            for copy in arriving(step):
                copy.wait()
        elif where == "left":
            for copy in leaving(step):
                copy.start()
        elif where == "entered":
            for copy in keep[1:]:
                copy.wait()
            keep.clear()
        elif where == "block":
            moves.within(step + 1, 1, 12)
        elif where == "blocks":
            for c in (1, 2):
                move(gd.at[c], gd_out.at[c - 1])
                move(gu.at[c], gu_out.at[c - 1])
            moves.at(13)
        else:
            move(n2t.at[:, pl.ds(0, D)], go_out)
            moves.at(14)
            for i in range(2 * images):
                for copy in leaving(i):
                    copy.wait()
            for copy in keep:
                copy.wait()

    mlp_compute(
        images,
        True,
        side_ref,
        device_weight(slots, assign_ref, counts_ref),
        cot,
        ctx,
        small,
        wo,
        wu,
        wd,
        refs,
        (act, gm, n2, gd, gu, n2t.at[:, pl.ds(0, D)], gs),
        hooks,
    )


MLP_PLAN = {
    "u": (0, 2, 4, 5, 7),
    "d": (1, 4, 5, 7, 8),
    "rd": (6, 8, 10, 12, 13, 14, 14),
    "ru": (6, 7, 9, 11, 13, 14, 14),
}


PARTS = 3
BLOCKS = 4


def attend_back_step(images, step, side_ref, qkv_ref, gctx_ref, lse_ref, cos_ref, sin_ref, gproj_ref, gs_ref, gf_ref):
    i, rows, c, at = head_pair(images, step)
    q = qkv_ref[rows, pl.ds(at, 128)]
    k = qkv_ref[rows, pl.ds(at + THIRD, 128)]
    v = qkv_ref[rows, pl.ds(at + 2 * THIRD, 128)]
    go = gctx_ref[rows, pl.ds(c, 128)]
    lane = lax.broadcasted_iota(jnp.int32, (1, 128), 1)
    mask = mask_column(side_ref, i)
    lse = lse_ref[step]
    dq, dk, dv = [], [], []
    for h in range(2):
        mine = lane // HD == h
        qm = jnp.where(mine, q, jnp.zeros_like(q))
        gom = jnp.where(mine, go, jnp.zeros_like(go))
        s = dot(k, qm, NT) * (LOG2E / math.sqrt(HD)) + mask
        p = jnp.exp2(s - lse[h : h + 1])
        dp = dot(v, gom, NT)
        dv.append(dot(p.astype(BF), go, NN))
        t = p * dp
        ds = (t - p * jnp.sum(t, axis=0, keepdims=True)).astype(BF)
        dk.append(dot(ds, q, NN))
        dq.append(dot(ds, k, TN))
    first = lane < HD
    cs = cos_ref[rows, pl.ds(c, 128)]
    sn = sin_ref[rows, pl.ds(c, 128)]
    angle = None
    for n, (pair, rot) in enumerate(((dq, q), (dk, k))):
        e = jnp.where(first, pair[0], pair[1]) * (1.0 / math.sqrt(HD))
        other = swap_halves(e)
        back = (e * cs - other * sn).astype(BF)
        gproj_ref[rows, pl.ds(at + n * THIRD, 128)] = back
        gs_ref[pl.ds(R_QB + n, 1), pl.ds(c, 128)] += jnp.sum(back.astype(F32), axis=0, keepdims=True)
        term = rot.astype(F32) * other
        angle = term if angle is None else angle + term
    gv = jnp.where(first, dv[0], dv[1]).astype(BF)
    gproj_ref[rows, pl.ds(at + 2 * THIRD, 128)] = gv
    gs_ref[R_QB + 2 : R_QB + 3, pl.ds(c, 128)] += jnp.sum(gv.astype(F32), axis=0, keepdims=True)
    angle = angle * half_sign(128)
    col, row, _ = patch_columns(side_ref, i)
    gf_ref[0:1, pl.ds(c, 128)] += jnp.sum(angle * col, axis=0, keepdims=True)
    gf_ref[1:2, pl.ds(c, 128)] += jnp.sum(angle * row, axis=0, keepdims=True)


def freq_row(gf_ref, gs_ref):
    for m in range(D // 128):
        which = m // 3
        total = None
        for parity in (0, 1):
            lanes = 2 * (m % 3) + parity
            value = gf_ref[which : which + 1, lanes * 128 : lanes * 128 + 128]
            for _ in range(3):
                term = value.astype(BF)
                value = value - term.astype(F32)
                moved = dot(jnp.broadcast_to(term, (8, 128)), spread(parity), NT)[0:1]
                total = moved if total is None else total + moved
        gs_ref[R_FR : R_FR + 1, m * 128 : m * 128 + 128] = total


def weight_third(c, scale, norm_ref, gproj_ref, gw_ref):
    def block(j, _):
        lanes = pl.ds(pl.multiple_of(j * THIRD, THIRD), THIRD)
        full = pl.ds(pl.multiple_of(c * D + j * THIRD, THIRD), THIRD)
        gw_ref[:, lanes] = (dot(norm_ref[...], gproj_ref[:, full], TN) * scale).astype(BF)
        return 0

    lax.fori_loop(0, 3, block, 0)


def attend_back_compute(images, thirds, side_ref, scale, ins, norm, gproj, gws, gs_ref, gf_ref, hooks):
    hooks("start")
    gs_ref[...] = jnp.zeros_like(gs_ref)
    gf_ref[...] = jnp.zeros_like(gf_ref)

    def body(step, _):
        hooks("step", step)
        attend_back_step(images, step, side_ref, *ins, gproj, gs_ref, gf_ref)
        for c in range(thirds):

            @pl.when(step == 2 * images * (c + 1) - 1)
            def _(c=c):
                weight_third(c, scale, norm, gproj, gws.at[c])

        return 0

    lax.fori_loop(0, images * HEADS // 2, body, 0)
    freq_row(gf_ref, gs_ref)
    hooks("end")


def attend_back_plain(images, slots, side_ref, assign_ref, counts_ref, *refs):
    ins, norm, (gproj, gws, gs, gf) = refs[0:5], refs[5], refs[6:10]
    attend_back_compute(images, 3, side_ref, device_weight(slots, assign_ref, counts_ref), ins, norm, gproj, gws, gs, gf, lambda *a: None)


def qkv_back_compute(images, x_ref, gproj_ref, gm_ref, small_ref, w_ref, gs_in, gin_ref, gs_ref, hooks):
    hooks("start")
    gain = small_ref[R_G1 : R_G1 + 1]
    gs_ref[...] = gs_in[...]
    tile = SLOT // 2

    def body(step, _):
        hooks("tile", step)
        rows = pl.ds(pl.multiple_of(step * tile, tile), tile)
        unit, inv = norm_stats(x_ref[rows])
        gn = None
        for c in range(3):
            term = dot(gproj_ref[rows, c * D : (c + 1) * D], w_ref[c][...], NT)
            gn = term if gn is None else gn + term
        gs_ref[R_G1 : R_G1 + 1] += jnp.sum(gn * unit, axis=0, keepdims=True)
        gs_ref[R_S1 : R_S1 + 1] += jnp.sum(gn, axis=0, keepdims=True)
        a = gn * gain
        ma = jnp.mean(a, axis=-1, keepdims=True)
        mu = jnp.mean(a * unit, axis=-1, keepdims=True)
        gin_ref[rows] = gm_ref[rows] + inv * (a - ma - unit * mu)
        return 0

    lax.fori_loop(0, 2 * images, body, 0)
    hooks("end")


def qkv_back_plain(images, slots, assign_ref, counts_ref, x_ref, gproj_ref, gm_ref, small_ref, w_ref, gs_in, gin, gs):
    def hooks(where, index=None):
        if where == "end":
            gs[...] = gs[...] * device_weight(slots, assign_ref, counts_ref)

    parts = [w_ref.at[c] for c in range(3)]
    qkv_back_compute(images, x_ref, gproj_ref, gm_ref, small_ref, parts, gs_in, gin, gs, hooks)


def backward_reduce(images, slots, side_ref, assign_ref, counts_ref, small_ref, gs_mlp, *refs):
    ins_in, (gd, gu, go), (x_in, gm_in, w_in) = refs[0:6], refs[6:9], refs[9:12]
    gin_out, gs, outs = refs[12], refs[13], refs[14:22]
    ins, gproj, gws, gf, gs_own = refs[22:28], refs[28], refs[29], refs[30], refs[31]
    bufs, tinybufs, (loads, local, send, recv, ssend, srecv) = refs[32:80], refs[80], refs[81:87]
    qkv, cos, sin, norm = ins[0], ins[3], ins[4], ins[5]
    w = Place()
    weight = device_weight(slots, assign_ref, counts_ref)
    srcs = (gd.at[0], gu.at[0], gd.at[1], gu.at[1], go, gws.at[0], gws.at[1], gws.at[2])
    items = {
        name: Reduce(w, srcs[i], bufs[6 * i : 6 * i + 6], outs[i], local.at[i], send.at[i], recv.at[i])
        for i, name in enumerate(BACK_PLAN)
    }
    moves = Moves(items, BACK_PLAN)
    tiny = SmallSum(w, gs, tinybufs, ssend, srecv)

    def third(c):
        copies = []
        for i, width in ((0, D), (1, THIRD), (3, THIRD), (4, THIRD)):
            lanes = pl.ds(c * width, width)
            copies.append(pltpu.make_async_copy(ins_in[i].at[:, lanes], ins[i].at[:, lanes], loads.at[c, i]))
        whole = {0: 2, 1: 5}.get(c)
        if whole is not None:
            copies.append(pltpu.make_async_copy(ins_in[whole], ins[whole], loads.at[c, 5]))
        return copies

    def hooks(where, step=None):
        if where == "start":
            for c in range(3):
                for copy in third(c):
                    copy.start()
            greet(w.partners() + [(w.g ^ 3, w.p)])
            moves.at(0)
            for copy in third(0):
                copy.wait()
        elif where == "step":
            for c, when in ((1, 2 * images - 1), (2, 4 * images)):

                @pl.when(step == when)
                def _(c=c):
                    for copy in third(c):
                        copy.wait()

            moves.within(step + 1, 1, 12)

    attend_back_compute(images, 3, side_ref, weight, ins[0:5], norm, gproj, gws, gs_own, gf, hooks)
    copies = [load(x_in, cos, loads.at[0, 0]), load(gm_in, sin, loads.at[0, 1])]
    wide = [qkv.at[pl.ds(0, D), pl.ds(c * D, D)] for c in range(3)]
    copies += [load(w_in.at[c], wide[c], loads.at[0, 2 + c]) for c in range(3)]
    moves.at(13)
    for copy in copies:
        copy.wait()

    def tiles(where, step=None):
        if where == "tile":
            moves.within(step + 14, 14, 17)

    qkv_back_compute(images, cos, gproj, sin, small_ref, wide, gs_own, sin, gs, tiles)
    copy = load(sin, gin_out, loads.at[0, 0])
    gs[...] = gs[...] * weight + gs_mlp[...]
    for number in range(4):
        tiny.stage(number)
        moves.at(18 + number)
    copy.wait()


BACK_PLAN = {
    "d1": (1, 3, 6, 9, 17, 19, 19),
    "u1": (1, 7, 11, 14, 18, 19, 21),
    "d2": (2, 4, 6, 9, 13, 15, 19),
    "u2": (2, 5, 8, 11, 14, 18, 20),
    "o": (0, 4, 7, 13, 16, 18, 21),
    "q0": (6, 7, 11, 15, 18, 19, 20),
    "q1": (9, 10, 14, 16, 18, 19, 20),
    "q2": (13, 14, 17, 18, 19, 20, 21),
}


def finish_kernel(dp, p_axis, gs, act_in, gin_in, rout_in, *refs):
    rd, ru, rq = refs[0:3], refs[3:6], refs[6:9]
    act, gin, rqkv, rout, rup, rdown, sems = refs[9], refs[10], *refs[11:15], refs[-1]
    tinies = refs[15:-2]
    stage = refs[-2]
    ins = [load(act_in, stage.at[0], sems.at[0]), load(gin_in, stage.at[1], sems.at[1])]
    p = lax.axis_index(p_axis)
    run = D // dp
    for out, places in zip(tinies, packed_places(p, dp, [t.shape[0] for t in tinies])):
        for m, (row, lane) in enumerate(places):
            whole = jnp.broadcast_to(gs[pl.ds(row, 1), :], (8, D))
            out[pl.ds(m * run, run)] = pltpu.roll(whole, D - lane, 1)[0, :run]
    copies = []
    for n, dst in enumerate((act, gin)):
        ins[n].wait()
        copies.append(load(stage.at[n], dst, sems.at[n]))
    rout[...] = rout_in[...]
    for c in range(3):
        rdown[c * rd[c].shape[0] : (c + 1) * rd[c].shape[0]] = rd[c][...]
        for b in range(dp):
            rup[:, (b * 3 + c) * 128 : (b * 3 + c + 1) * 128] = ru[c][:, b * 128 : (b + 1) * 128]
        for part in range(3):
            cols = part * D + c * THIRD
            rqkv[:, cols : cols + THIRD] = rq[c][:, part * THIRD : (part + 1) * THIRD]
    for copy in copies:
        copy.wait()


def params(mb=56):
    return pltpu.CompilerParams(vmem_limit_bytes=mb << 20)


def place_rows(p, dp, vec):
    n = vec.shape[0]
    whole = jnp.tile(vec, dp)
    owner = jnp.arange(n * dp, dtype=jnp.int32) // n
    return jnp.where(owner == p, whole, 0.0).reshape(-1, D)


def on_device(
    fast,
    images,
    cotangent,
    resolution,
    assignment,
    counts,
    ln1_gain,
    ln1_shift,
    qkv_weight,
    qkv_bias,
    rope_freqs,
    out_weight,
    out_bias,
    ln2_gain,
    ln2_shift,
    up_weight,
    up_bias,
    down_weight,
    down_bias,
):
    p = lax.axis_index("dp")
    dp = lax.axis_size("dp")
    n = images.shape[0]
    rows = n * SLOT
    x = images.reshape(rows, D)
    cot = cotangent.reshape(rows, D)
    vectors = (ln1_gain, ln1_shift, qkv_bias, rope_freqs, out_bias, ln2_gain, ln2_shift, up_bias, down_bias)
    slots = dp * rows
    sds = jax.ShapeDtypeStruct
    smem = pl.BlockSpec(memory_space=pltpu.SMEM)
    anyw = pl.BlockSpec(memory_space=pl.ANY)
    kept = [
        sds((rows, 3 * D), BF),
        sds((rows, D), BF),
        sds((rows, D), F32),
        sds((rows, D), F32),
        sds((rows, D), BF),
        sds((n * HEADS // 2, 8, SLOT), F32),
    ]
    weights = (qkv_weight, out_weight, up_weight, down_weight)
    dma = pltpu.SemaphoreType.DMA
    vmem = pltpu.VMEM

    def moving(number, mb):
        return pltpu.CompilerParams(vmem_limit_bytes=mb << 20, collective_id=number, has_side_effects=True)

    part = FF // PARTS
    if fast:
        later = [sds((D // dp, part), BF), sds((part // dp, D), BF)]
        fulls = [sds((3, D, D), BF), sds((D, D), BF), sds((PARTS - 1, D, part), BF), sds((PARTS - 1, part, D), BF)]
        outs = pl.pallas_call(
            functools.partial(forward_gather, n),
            out_shape=kept + [sds((R_ALL, D), F32)] + fulls + later,
            in_specs=[smem] + vm(9) + [anyw] * 5,
            out_specs=[anyw] * 4 + vm(3) + [anyw] * 6,
            scratch_shapes=[
                vmem((rows, D), F32),
                vmem((rows, 3 * D), BF),
                vmem((rows, D), BF),
                vmem((rows, D), F32),
                vmem((rows, D), F32),
                vmem((3, D, D), BF),
                vmem((8, R_ALL, 128), F32),
                vmem((3, D // dp, D), BF),
                vmem((D // dp, D), BF),
                vmem((PARTS, D // dp, part), BF),
                vmem((PARTS, part // dp, D), BF),
            ]
            + [vmem(v.shape, F32) for v in weights]
            + [
                dma((20,)),
                dma((10, 16)),
                dma((7,)),
                dma((7,)),
                dma((22,)),
                dma((5,)),
            ],
            compiler_params=moving(0, 56),
            name="forward",
        )(resolution, *vectors, x, *weights)
        qkv, norm1, cos, sin, ctx, lse, small, wqkv, wo, wu, wd, up_later, down_later = outs
    else:
        packed = [place_rows(p, dp, lax.reduce_precision(v, 8, 7)) for v in vectors]
        small = lax.psum(jnp.concatenate(packed + [jnp.zeros((2, D), F32)], axis=0), "dp")
        wqkv, wo, wu, wd = [lax.all_gather(v.astype(BF), "dp", axis=0, tiled=True) for v in weights]
        wqkv = wqkv.reshape(D, 3, 3, THIRD).transpose(2, 0, 1, 3).reshape(3, D, D)
        wu = wu.reshape(D, PARTS, part).transpose(1, 0, 2)
        wd = wd.reshape(PARTS, part, D)
        qkv, norm1, cos, sin, ctx, lse = pl.pallas_call(
            functools.partial(forward_plain, n),
            out_shape=kept,
            in_specs=[smem] + vm(3),
            out_specs=vm(6),
            compiler_params=params(),
            name="forward",
        )(resolution, x, small, wqkv)

    grads = [sds((PARTS, part, D), BF), sds((PARTS, D, part), BF), sds((D, D), BF)]
    rest = [sds((R_ALL, D), F32)]
    firsts = [sds((rows, D), F32), sds((rows, D), F32), sds((rows, D), BF)]
    tables = [vmem((rows, 3 * D), BF), vmem((rows, D), BF), vmem((n * HEADS // 2, 8, SLOT), F32)]
    tables += [vmem((rows, D), F32)] * 2
    gproj_shape = sds((rows, 3 * D), BF)
    if fast:
        sizes = [(part // dp, D), (D // dp, part)]
        act, gm, gctx, gdown, gup, gout, gs_mlp, rdown0, rup0 = pl.pallas_call(
            functools.partial(mlp_moving, n, slots),
            out_shape=firsts
            + [sds((PARTS - 1,) + g.shape[1:], BF) for g in grads[:2]]
            + grads[2:]
            + rest
            + [sds(z, F32) for z in sizes],
            in_specs=[smem] * 3 + vm(1) + [anyw] * 8,
            out_specs=[anyw] * 6 + vm(3),
            scratch_shapes=mlp_scratch(rows)
            + [
                vmem((rows, D), F32),
                vmem((rows, D), BF),
                vmem((D, D), BF),
                vmem((PARTS, D, part), BF),
                vmem((PARTS, part, D), BF),
                vmem((rows, D), F32),
                vmem((rows, D), F32),
                vmem((PARTS, part, D), BF),
                vmem((PARTS, D, part), BF),
            ]
            + sum([Reduce.buffers(*z) for z in sizes], [])
            + [dma((12,)), dma((4,)), dma((2, 16)), dma((2,)), dma((2,)), dma((2, 6))]
            + [dma((3, 2 * n))] * 2,
            compiler_params=moving(3, 63),
            name="mlp",
        )(resolution, assignment, counts, small, x, cot, ctx, wo, wu, wd, up_later, down_later)
        third = (D // dp, D)
        sizes = sizes + sizes + [third] * 4
        gin, gs, rdown1, rup1, rdown2, rup2, rout, rq0, rq1, rq2 = pl.pallas_call(
            functools.partial(backward_reduce, n, slots),
            out_shape=[sds((rows, D), F32)] + rest + [sds(z, F32) for z in sizes],
            in_specs=[smem] * 3 + vm(2) + [anyw] * 12,
            out_specs=[anyw] + vm(9),
            scratch_shapes=tables
            + [vmem((rows, D), BF), vmem((rows, 3 * D), BF), vmem((3, D, D), BF), vmem((8, D), F32)]
            + [vmem((R_ALL, D), F32)]
            + sum([Reduce.buffers(*z) for z in sizes], [])
            + [vmem((12, R_ALL, D), F32), dma((3, 6)), dma((8,)), dma((8,)), dma((8, 6)), dma((3, 4)), dma((3, 4))],
            compiler_params=moving(1, 62),
            name="backward",
        )(resolution, assignment, counts, small, gs_mlp, qkv, gctx, lse, cos, sin, norm1, gdown, gup, gout, x, gm, wqkv)

        matrices = (qkv_weight, out_weight, up_weight, down_weight)
        act, gin, rqkv, rout, rup, rdown, *tinies = pl.pallas_call(
            functools.partial(finish_kernel, dp, "dp"),
            out_shape=[sds((rows, D), F32)] * 2 + [sds(v.shape, F32) for v in matrices + vectors],
            in_specs=vm(1) + [anyw] * 2 + vm(10),
            out_specs=[anyw] * 2 + vm(13),
            scratch_shapes=[vmem((2, rows, D), F32), dma((2,))],
            compiler_params=params(),
            name="finish",
        )(gs, act, gin, rout, rdown0, rdown1, rdown2, rup0, rup1, rup2, rq0, rq1, rq2)
    else:
        act, gm, gctx, gdown, gup, gout, gs_mlp = pl.pallas_call(
            functools.partial(mlp_plain, n, slots),
            out_shape=firsts + grads + rest,
            in_specs=[smem] * 3 + [anyw] + vm(6),
            out_specs=vm(7),
            scratch_shapes=mlp_scratch(rows) + [dma((1,))],
            compiler_params=params(63),
            name="mlp",
        )(resolution, assignment, counts, x, cot, ctx, small, wo, wu, wd)
        gproj, gqkv, gs_att = pl.pallas_call(
            functools.partial(attend_back_plain, n, slots),
            out_shape=[gproj_shape, sds((3, D, D), BF)] + rest,
            in_specs=[smem] * 3 + vm(6),
            out_specs=vm(3),
            scratch_shapes=[vmem((8, D), F32)],
            compiler_params=params(),
            name="attend_back",
        )(resolution, assignment, counts, qkv, gctx, lse, cos, sin, norm1)
        gin, gs_qkv = pl.pallas_call(
            functools.partial(qkv_back_plain, n, slots),
            out_shape=[sds((rows, D), F32)] + rest,
            in_specs=[smem] * 2 + vm(6),
            out_specs=vm(2),
            compiler_params=params(),
            name="project_back",
        )(assignment, counts, x, gproj, gm, small, wqkv, gs_att)

        def reduce(g):
            total = lax.psum_scatter(g, "dp", scatter_dimension=0, tiled=True)
            return lax.psum(total, "group").astype(F32)

        gqkv = gqkv.reshape(3, D, 3, THIRD).transpose(1, 2, 0, 3).reshape(D, 3 * D)
        gup = gup.transpose(1, 0, 2).reshape(D, FF)
        rqkv, rout, rup, rdown = [reduce(g) for g in (gqkv, gout, gup, gdown.reshape(FF, D))]
        gs = lax.psum(gs_mlp + gs_qkv, ("group", "dp"))

        def own(first, count):
            flat = gs[first : first + count].reshape(dp, -1)
            return lax.dynamic_index_in_dim(flat, p, 0, keepdims=False)

        tinies = [own(first, v.shape[0] * dp // D) for first, v in zip(SMALL_ROWS, vectors)]

    g1, s1, qb, fr, ob, g2, s2, ub, db = tinies
    act, gin = act.reshape(images.shape), gin.reshape(images.shape)
    return (act, gin, g1, s1, rqkv, qb, fr, rout, ob, g2, s2, rup, ub, rdown, db)


def solution(mesh):
    batch = P(("group", "dp"), None, None)
    per_image = P(("group", "dp"))
    vec, mat = P("dp"), P("dp", None)
    fast = dict(mesh.shape) == {"group": 4, "dp": 8}
    return jax.shard_map(
        functools.partial(on_device, fast),
        mesh=mesh,
        in_specs=(batch, batch, per_image, per_image, P(), vec, vec, mat, vec, vec, mat, vec, vec, vec, mat, vec, mat, vec),
        out_specs=(batch, batch, vec, vec, mat, vec, vec, mat, vec, vec, vec, mat, vec, mat, vec),
        check_vma=False,
    )
```
